32 devices in a mesh: dp: 8 (over y, x, core), tensor: 4 (over z).
Axes of the slice: x: 2, y: 2, z: 4, core: 2. Of those that a mesh axis runs over, the one named last changes fastest.
Arguments:
- tokens: bfloat16 [8, 1024, 2048], P('dp', 'tensor'), may hold values from -6 to 6
- segments: int32 [8, 1024], P('dp'), may hold values from 0 to 7, never falling along the last dimension, each value on 1 to 512 neighbouring positions
- valid: int32 [8, 1024], P('dp'), may hold values 0 or 1
- routes: int32 [8, 1024, 8], P('dp'), may hold values from 0 to 15, all different within a row; in each aligned block of 1024 rows (0 to 1023, 1024 to 2047, ..., all dimensions but the last counted through in order) at most 544 rows name the same one
- cotangent: bfloat16 [8, 1024, 2048], P('dp', 'tensor'), may hold values from -6 to 6
- query_weight: bfloat16 [2048, 2048], P('dp', 'tensor'), may hold values from -0.125 to 0.125
- key_weight: bfloat16 [2048, 2048], P('dp', 'tensor'), may hold values from -0.125 to 0.125
- value_weight: bfloat16 [2048, 2048], P('dp', 'tensor'), may hold values from -0.125 to 0.125
- output_weight: bfloat16 [2048, 2048], P('dp', 'tensor'), may hold values from -0.75 to 0.75
- attn_norm_gain: bfloat16 [2048], replicated, may hold values from 0.25 to 1.75
- expert_norm_gain: bfloat16 [2048], replicated, may hold values from 0.25 to 1.75
- query_norm_gain: bfloat16 [2048], replicated, may hold values from 0.25 to 1.75
- key_norm_gain: bfloat16 [2048], replicated, may hold values from 0.25 to 1.75
- router_weight: bfloat16 [2048, 16], replicated, may hold values from -0.0625 to 0.0625
- gate_weight: bfloat16 [16, 2048, 1024], P(None, 'dp', 'tensor'), may hold values from -0.125 to 0.125
- up_weight: bfloat16 [16, 2048, 1024], P(None, 'dp', 'tensor'), may hold values from -0.125 to 0.125
- down_weight: bfloat16 [16, 2048, 1024], P(None, 'dp', 'tensor'), may hold values from -1.5 to 1.5
Outputs:
- layer_out: bfloat16 [8, 1024, 2048], P('dp', 'tensor')
- grad_tokens: float32 [8, 1024, 2048], P('dp', 'tensor')
- grad_query: float32 [2048, 2048], P('dp', 'tensor')
- grad_key: float32 [2048, 2048], P('dp', 'tensor')
- grad_value: float32 [2048, 2048], P('dp', 'tensor')
- grad_output: float32 [2048, 2048], P('dp', 'tensor')
- grad_gate: float32 [16, 2048, 1024], P(None, 'dp', 'tensor')
- grad_up: float32 [16, 2048, 1024], P(None, 'dp', 'tensor')
- grad_down: float32 [16, 2048, 1024], P(None, 'dp', 'tensor')
- grad_router: float32 [2048, 16], replicated
- grad_attn_norm: float32 [2048], replicated
- grad_expert_norm: float32 [2048], replicated
- grad_query_norm: float32 [2048], replicated
- grad_key_norm: float32 [2048], replicated
The draws below stay inside these ranges and needn't reach their ends.
Inputs may be any that keep to these rules, and one draw needn't show every extreme that they name: `routes`: each row names 8 different experts; within one sequence no expert is named by more than 544 rows, and in every draw some expert of some sequence is named by exactly 544 rows. `segments`: document numbers never fall along a sequence; each document has 1 to 512 tokens and one has exactly 512.
All inputs are finite; a program needn't handle non-finite values. No bound on the sum of `valid` on one device may be relied on, other than what follows from the above.
Results may differ from the reference program's by a relative error of at most 0.015.
Values may be sent and summed in bfloat16 or wider, within the bound.
No kernel may reach another device: no remote copies, remote signals or barrier semaphores. Data moves between devices by JAX's collectives and lax.ppermute only.
A program may use at most 640 MiB of HBM per device.

```python
import math
from functools import partial
import jax
import jax.numpy as jnp
import numpy as np
from jax import lax

D = 2048
HEADS = 16
HEAD = 128
FF = 1024
TOP = 8
EXPERTS = 16
LEN = 1024
SEQS = 8
CAP = 544
DOCS = 8
DOC_MOST = 512


def with_ends(values, rng, low, high):
    longest = values.shape.index(max(values.shape))
    spots = []
    for shift in (0, 1):
        where = [jax.random.randint(jax.random.fold_in(rng, axis), (), 0, length) for axis, length in enumerate(values.shape)]
        where[longest] = (where[longest] + shift) % values.shape[longest]
        spots.append(tuple(where))
    return values.at[spots[0]].set(low).at[spots[1]].set(high)


def level_of(own_key, extent, split, low, high):
    level = 1.0
    for dim, parts in split:
        heights = jax.random.uniform(jax.random.fold_in(jax.random.fold_in(own_key, 6), dim), (parts,), jnp.float32, low / len(split), high / len(split))
        level = level * jnp.repeat(jnp.exp(heights), extent[dim] // parts).reshape((-1,) + (1,) * (len(extent) - 1 - dim))
    return level


def length_profile(count, total, bound, lean):
    weights = [(1 << 20) // math.isqrt(rank ** lean) + 1 for rank in range(2, count + 1)]
    surplus, given = total - bound - (count - 1), [1] * (count - 1)
    while surplus > 0:
        free = [i for i in range(count - 1) if given[i] < bound]
        whole, remaining = sum([weights[i] for i in free]), surplus
        for i in free:
            addition = min(bound - given[i], max(1, remaining * weights[i] // whole), surplus)
            given[i] = given[i] + addition
            surplus = surplus - addition
    return np.array([bound] + given)


def ragged(key, count, total, limit, lean):
    if count == 2:
        one = jax.random.randint(key, (), max(1, total - limit), min(limit, total - 1) + 1)
        return jnp.stack([one, total - one])
    sizes = jnp.asarray(length_profile(count, total, limit, lean), jnp.int32)
    pairs = (count - 1) // 2
    donor, sink = sizes[1:1 + 2 * pairs:2], sizes[2:2 + 2 * pairs:2]
    room = jnp.minimum(donor - 1, limit - sink)
    shifted = jax.random.randint(jax.random.fold_in(key, 1), (pairs,), 0, 1 << 20) % (room + 1)
    sizes = sizes.at[1:1 + 2 * pairs:2].set(donor - shifted).at[2:2 + 2 * pairs:2].set(sink + shifted)
    return sizes[jax.random.permutation(jax.random.fold_in(key, 2), count)]


def routed_block(key, own, number, rows, amount, top, bound, lean):
    ranking = jax.random.permutation(key, amount)
    packed, common = load_shares(amount, rows * top, bound, lean, True), load_shares(amount, rows * top, bound, lean, False)
    places = jnp.arange(amount)

    def named(tallies, rotation):
        used = int((tallies > 0).sum())
        fixed = max(1, used // 4)
        moved = fixed + (places - fixed + rotation * (used - fixed)) % max(1, amount - fixed)
        return jnp.zeros((amount,), jnp.int32).at[ranking[jnp.where(places < fixed, places, moved)]].set(jnp.asarray(tallies, jnp.int32))

    tallies = jnp.where(number % 4 == 0, named(packed, number // 4), named(common, number - number // 4 - 1))
    mixed = jax.random.permutation(jax.random.fold_in(own, 3), amount)
    donor, sink = mixed[0:amount // 2 * 2:2], mixed[1:amount // 2 * 2:2]
    margin = jnp.minimum(tallies[donor] - 1, bound - tallies[sink]) // 2
    margin = jnp.where((donor == ranking[0]) | (sink == ranking[0]) | (tallies[sink] == 0), 0, jnp.maximum(margin, 0))
    moved = jax.random.randint(jax.random.fold_in(own, 4), (amount // 2,), 0, 1 << 20) % (margin + 1)
    tallies = tallies.at[donor].add(-moved).at[sink].add(moved)
    items = jnp.searchsorted(jnp.cumsum(tallies), jnp.arange(rows * top), side="right").astype(jnp.int32)
    listing = items.reshape(top, rows).T
    listing = listing[jax.random.permutation(jax.random.fold_in(own, 1), rows)]
    rotation = jax.random.randint(jax.random.fold_in(own, 2), (rows, 1), 0, top)
    return jnp.take_along_axis(listing, (jnp.arange(top)[None, :] + rotation) % top, axis=1)


def load_shares(number_of, total, bound, lean, full):
    weights = [(1 << 20) // math.isqrt(grade ** lean) + 1 for grade in range(1, number_of + 1)]
    largest = bound if full else min(bound, max(-(-total // number_of), total * weights[0] // sum(weights)))
    least = 1 if total - largest >= number_of - 1 else 0
    holding, spare = [largest] + [least] * (number_of - 1), total - largest - least * (number_of - 1)
    while spare > 0:
        free = [i for i in range(1, number_of) if holding[i] < largest] or [i for i in range(1, number_of) if holding[i] < bound]
        whole, left = sum([weights[i] for i in free]), spare
        for i in free:
            more = min(bound - holding[i], max(1, left * weights[i] // whole), spare)
            holding[i] = holding[i] + more
            spare = spare - more
    return np.array(holding)


def gaussian(rng, shape, scale, bound, split=(), kind=jnp.bfloat16):
    drawn = scale * jax.random.normal(rng, shape, jnp.float32)
    if split:
        drawn = drawn * level_of(rng, shape, split, -0.22, 0.18)
    return jnp.clip(drawn, -bound, bound).astype(kind)


def setup_inputs(seed: int = 0) -> dict:
    key_list = jax.random.split(jax.random.key(seed), 18)
    tokens = gaussian(key_list[0], (SEQS, LEN, D), 1.0, 6.0, ((0, 8), (1, 4)))
    segments = jax.vmap(lambda own: jnp.searchsorted(jnp.cumsum(ragged(own, DOCS, LEN, DOC_MOST, 2)), jnp.arange(LEN), side="right"))(jax.random.split(key_list[1], SEQS)).reshape((SEQS, LEN)).astype(jnp.int32)
    valid = with_ends((jax.random.randint(key_list[2], (SEQS, LEN), 0, 8) < 7).astype(jnp.int32), jax.random.fold_in(key_list[2], 1), 0, 1)
    routes_keys = jax.random.split(jax.random.fold_in(key_list[3], 1), SEQS * LEN // LEN)
    routes_turns = jax.random.permutation(jax.random.fold_in(key_list[3], 3), SEQS * LEN // LEN)
    routes = jax.vmap(lambda own, number: routed_block(jax.random.fold_in(key_list[3], 2), own, number, LEN, EXPERTS, TOP, CAP, 1))(routes_keys, routes_turns).reshape((SEQS, LEN, TOP))
    cotangent = gaussian(key_list[4], (SEQS, LEN, D), 1.0, 6.0, ((0, 8), (1, 4)))
    query_weight = gaussian(key_list[5], (D, D), D ** -0.5, 0.125, ((0, 8), (1, 4)))
    key_weight = gaussian(key_list[6], (D, D), D ** -0.5, 0.125, ((0, 8), (1, 4)))
    value_weight = gaussian(key_list[7], (D, D), D ** -0.5, 0.125, ((0, 8), (1, 4)))
    output_weight = gaussian(key_list[8], (D, D), (D // 32) ** -0.5, 0.75, ((0, 8), (1, 4)))
    attn_norm_gain = jnp.clip(1.0 + 0.15 * jax.random.normal(key_list[9], (D,), jnp.float32), 0.25, 1.75).astype(jnp.bfloat16)
    expert_norm_gain = jnp.clip(1.0 + 0.15 * jax.random.normal(key_list[10], (D,), jnp.float32), 0.25, 1.75).astype(jnp.bfloat16)
    query_norm_gain = jnp.clip(1.0 + 0.15 * jax.random.normal(key_list[11], (D,), jnp.float32), 0.25, 1.75).astype(jnp.bfloat16)
    key_norm_gain = jnp.clip(1.0 + 0.15 * jax.random.normal(key_list[12], (D,), jnp.float32), 0.25, 1.75).astype(jnp.bfloat16)
    router_weight = gaussian(key_list[13], (D, EXPERTS), (4 * D) ** -0.5, 0.0625)
    gate_weight = gaussian(key_list[14], (EXPERTS, D, FF), D ** -0.5, 0.125, ((1, 8), (2, 4)))
    up_weight = gaussian(key_list[15], (EXPERTS, D, FF), D ** -0.5, 0.125, ((1, 8), (2, 4)))
    down_weight = gaussian(key_list[16], (EXPERTS, D, FF), (FF // 64) ** -0.5, 1.5, ((1, 8), (2, 4)))
    return {"tokens": tokens, "segments": segments, "valid": valid, "routes": routes, "cotangent": cotangent, "query_weight": query_weight, "key_weight": key_weight, "value_weight": value_weight, "output_weight": output_weight, "attn_norm_gain": attn_norm_gain, "expert_norm_gain": expert_norm_gain, "query_norm_gain": query_norm_gain, "key_norm_gain": key_norm_gain, "router_weight": router_weight, "gate_weight": gate_weight, "up_weight": up_weight, "down_weight": down_weight}


EPS = 1e-05
THETA = 10000.0
MASKED = -1e+30
PRECISE = lax.Precision.HIGHEST

@jax.custom_vjp
def low(v):
    return lax.optimization_barrier(v.astype(jnp.bfloat16)).astype(jnp.float32)

@jax.custom_vjp
def low_back(v):
    return v

def low_keep(v):
    return (low(v), None)

def low_pass(kept, grad):
    return (grad,)

def back_keep(v):
    return (v, None)

def back_low(kept, grad):
    return (low(grad),)
low.defvjp(low_keep, low_pass)
low_back.defvjp(back_keep, back_low)

def matmul(left, right):
    return jnp.dot(left, right, precision=PRECISE, preferred_element_type=jnp.float32)

def rms_gain(values, gain):
    return values * lax.rsqrt(lax.optimization_barrier(jnp.mean(values * values, axis=-1, keepdims=True)) + EPS) * gain

def rotary_tables(length, width):
    half = width // 2
    freq = THETA ** (-(jnp.arange(half, dtype=jnp.float32) * 2.0) / width)
    angle = jnp.arange(length, dtype=jnp.float32)[:, None] * freq[None, :]
    return (jnp.cos(angle)[:, None, :], jnp.sin(angle)[:, None, :])

def rotate(values, cosine, sine_table):
    half = values.shape[-1] // 2
    first = values[..., :half]
    second = values[..., half:]
    return jnp.concatenate([first * cosine - second * sine_table, second * cosine + first * sine_table], axis=-1)

def allowed_mask(segment, usable):
    length = segment.shape[0]
    position = jnp.arange(length, dtype=jnp.int32)
    same = segment[:, None] == segment[None, :]
    causal = position[None, :] <= position[:, None]
    live = (usable[None, :] == 1) | (position[None, :] == position[:, None])
    return same & causal & live

def dispatch(route):
    length = route.shape[0]
    flat = route.reshape(-1).astype(jnp.int32)
    onehot = (flat[:, None] == jnp.arange(EXPERTS, dtype=jnp.int32)[None, :]).astype(jnp.int32)
    before = jnp.cumsum(onehot, axis=0) - onehot
    rank = lax.optimization_barrier(jnp.sum(before * onehot, axis=1)).astype(jnp.int32)
    slot = (flat * CAP + rank).astype(jnp.int32)
    owner = (jnp.arange(length * TOP, dtype=jnp.int32) // TOP).astype(jnp.int32)
    slot_token = jnp.zeros((EXPERTS * CAP,), jnp.int32).at[slot].set(owner)
    slot_used = jnp.zeros((EXPERTS * CAP,), jnp.int32).at[slot].set(1)
    return (slot_token.reshape(EXPERTS, CAP), slot_used.reshape(EXPERTS, CAP))

def forward_one(segment, usable, slot_token, slot_used, params, inputs):
    wquery, wkey, wvalue, woutput, gain_attn, gain_expert, gain_query, gain_key, router, wgate, wup, wdown = params
    length = inputs.shape[0]
    cosine, sine_table = rotary_tables(length, HEAD)
    normed1 = low(rms_gain(inputs, gain_attn))
    query_raw = low_back(matmul(normed1, wquery))
    key_raw = low_back(matmul(normed1, wkey))
    values = low(low_back(matmul(normed1, wvalue))).reshape(length, HEADS, HEAD)
    queries = low(rotate(rms_gain(query_raw, gain_query).reshape(length, HEADS, HEAD), cosine, sine_table))
    keys = low(rotate(rms_gain(key_raw, gain_key).reshape(length, HEADS, HEAD), cosine, sine_table))
    scores = low_back(jnp.einsum('qhd,khd->hqk', queries, keys, precision=PRECISE) * HEAD ** (-0.5))
    scores = jnp.where(allowed_mask(segment, usable)[None], scores, MASKED)
    weights = low(jax.nn.softmax(scores, axis=-1))
    mixed_heads = low(low_back(jnp.einsum('hqk,khd->qhd', weights, values, precision=PRECISE)))
    mixed_heads = mixed_heads.reshape(length, HEADS * HEAD)
    attended = low_back(jnp.dot(mixed_heads, woutput.T, precision=PRECISE, preferred_element_type=jnp.float32))
    resid = inputs + attended
    normed2 = low(rms_gain(resid, gain_expert))
    route_probs = jax.nn.softmax(matmul(normed2, router), axis=-1)
    expert_ids = jnp.arange(EXPERTS, dtype=jnp.int32)[:, None]
    gate_slot = route_probs[slot_token, expert_ids] * slot_used.astype(jnp.float32)
    rows_in = normed2[slot_token]
    gate_pre = low_back(jnp.einsum('ecd,edf->ecf', rows_in, wgate, precision=PRECISE))
    up_pre = low_back(jnp.einsum('ecd,edf->ecf', rows_in, wup, precision=PRECISE))
    hidden_act = low(jax.nn.silu(gate_pre) * up_pre)
    expert_out = low_back(jnp.einsum('ecf,edf->ecd', hidden_act, wdown, precision=PRECISE))
    weighted = (expert_out * gate_slot[:, :, None]).reshape(-1, resid.shape[1])
    combined = jnp.zeros_like(resid).at[slot_token.reshape(-1)].add(weighted)
    return resid + low_back(combined)

def reference(tokens, segments, valid, routes, cotangent, query_weight, key_weight, value_weight, output_weight, attn_norm_gain, expert_norm_gain, query_norm_gain, key_norm_gain, router_weight, gate_weight, up_weight, down_weight):
    params = tuple((item.astype(jnp.float32) for item in (query_weight, key_weight, value_weight, output_weight, attn_norm_gain, expert_norm_gain, query_norm_gain, key_norm_gain, router_weight, gate_weight, up_weight, down_weight)))

    def one_sequence(carried, pieces):
        inputs, segment, usable, route, upstream = pieces
        slot_token, slot_used = dispatch(route)
        forward = partial(forward_one, segment, usable, slot_token, slot_used)
        result, pullback = jax.vjp(forward, params, inputs.astype(jnp.float32))
        start_grad = upstream.astype(jnp.float32) * usable.astype(jnp.float32)[:, None]
        grad_params, grad_inputs = pullback(start_grad)
        carried = jax.tree.map(jnp.add, carried, grad_params)
        return (carried, (result.astype(jnp.bfloat16), grad_inputs))
    zeros = jax.tree.map(jnp.zeros_like, params)
    grads, (outputs, grad_inputs) = lax.scan(one_sequence, zeros, (tokens, segments, valid, routes, cotangent))
    return (outputs, grad_inputs, grads[0], grads[1], grads[2], grads[3], grads[9], grads[10], grads[11], grads[8], grads[4], grads[5], grads[6], grads[7])
```

```python
import jax
import jax.numpy as jnp
from jax import lax
from jax.experimental import pallas as pl
from jax.experimental.pallas import tpu as pltpu
from jax.sharding import PartitionSpec as P

HEAD = 128
EXPERTS = 16


EPS = 1e-05
THETA = 10000.0
MASKED = -1e30
PRECISE = lax.Precision.HIGHEST


def rows_norm(values, gain):
    scale = lax.rsqrt(jnp.mean(values * values, axis=-1, keepdims=True) + EPS)
    normed = values * scale
    return (normed * gain, normed, scale)


def norm_back(grad_out, gain, normed, scale):
    grad_normed = grad_out * gain
    inner_mean = jnp.mean(grad_normed * normed, axis=-1, keepdims=True)
    return (scale * (grad_normed - normed * inner_mean), jnp.sum(grad_out * normed, axis=0))


def rotary_tables(length, width):
    half = width // 2
    freq = THETA ** (-(jnp.arange(half, dtype=jnp.float32) * 2.0) / width)
    angle = jnp.arange(length, dtype=jnp.float32)[:, None] * freq[None, :]
    return (jnp.cos(angle)[:, None, :], jnp.sin(angle)[:, None, :])


def rotate(values, cosine, sine_table):
    half = values.shape[-1] // 2
    first = values[..., :half]
    second = values[..., half:]
    return jnp.concatenate(
        [first * cosine - second * sine_table, second * cosine + first * sine_table], axis=-1
    )


def rotate_back(grads, cosine, sine_table):
    half = grads.shape[-1] // 2
    first = grads[..., :half]
    second = grads[..., half:]
    return jnp.concatenate(
        [first * cosine + second * sine_table, second * cosine - first * sine_table], axis=-1
    )


def allowed_rows(segment, usable, first_row, block_rows):
    query_pos = first_row + jnp.arange(block_rows, dtype=jnp.int32)
    key_pos = jnp.arange(segment.shape[0], dtype=jnp.int32)
    segment_rows = lax.dynamic_slice_in_dim(segment, first_row, block_rows)
    same = segment_rows[:, None] == segment[None, :]
    causal = key_pos[None, :] <= query_pos[:, None]
    live = (usable[None, :] == 1) | (key_pos[None, :] == query_pos[:, None])
    return same & causal & live


NN = (((1,), (0,)), ((), ()))
NT = (((1,), (1,)), ((), ()))


def dot32(left, right, dims=NN):
    return lax.dot_general(left, right, dims, preferred_element_type=jnp.float32)


def ring_gather(own, axis):
    n = lax.axis_size(axis)
    right = [(i, (i + 1) % n) for i in range(n)]
    chunks = [own]
    for _ in range(n - 1):
        chunks.append(lax.ppermute(chunks[-1], axis, right))
    return chunks


def in_order(chunks, axis):
    n = lax.axis_size(axis)
    here = lax.axis_index(axis)
    rows = chunks[0].shape[0]
    full = jnp.zeros((n * rows,) + chunks[0].shape[1:], chunks[0].dtype)
    for step, chunk in enumerate(chunks):
        full = lax.dynamic_update_slice_in_dim(full, chunk, ((here - step) % n) * rows, 0)
    return full


def ring_scatter(part_of, axis):
    n = lax.axis_size(axis)
    here = lax.axis_index(axis)
    right = [(i, (i + 1) % n) for i in range(n)]
    total = part_of((here - 1) % n)
    for step in range(1, n):
        moved = lax.ppermute(total.astype(jnp.bfloat16), axis, right)
        total = moved.astype(jnp.float32) + part_of((here - 1 - step) % n)
    return total


def all_sum(value, axes):
    for axis in axes:
        n = lax.axis_size(axis)
        if n & (n - 1):
            value = lax.psum(value, axis)
            continue
        bit = 1
        while bit < n:
            value = value + lax.ppermute(value, axis, [(i, i ^ bit) for i in range(n)])
            bit *= 2
    return value


def moe_first(rows_in, upstream, weight, gate_all, up_all, down_all):
    tokens, width = rows_in.shape
    experts, _, hidden = gate_all.shape
    block = min(512, tokens)
    bf16 = jnp.bfloat16

    def kernel(x_ref, f_ref, w_ref, g_ref, u_ref, d_ref, dx_ref, gp_ref, wh_ref, dg_ref, du_ref):
        e = pl.program_id(0)

        @pl.when(e == 0)
        def _():
            dx_ref[...] = jnp.zeros_like(dx_ref)
            gp_ref[...] = jnp.zeros_like(gp_ref)

        lane = lax.broadcasted_iota(jnp.int32, (block, experts), 1)
        for r in range(tokens // block):
            rs = pl.ds(r * block, block)
            x = x_ref[rs, :]
            w = jnp.sum(jnp.where(lane == e, w_ref[rs, :], 0.0), axis=1, keepdims=True)
            gate_pre = dot32(x, g_ref[0])
            up_pre = dot32(x, u_ref[0])
            projected = dot32(f_ref[rs, :], d_ref[0])
            sig = 1.0 / (1.0 + jnp.exp(-gate_pre))
            act = gate_pre * sig
            hidden_f = act * up_pre
            wh_ref[0, rs, :] = (w * hidden_f).astype(bf16)
            inner = jnp.sum(hidden_f * projected, axis=1, keepdims=True)
            gp_ref[rs, :] = jnp.where(lane == e, inner, gp_ref[rs, :])
            grad_hidden = w * projected
            dg = (grad_hidden * up_pre * (sig + act * (1.0 - sig))).astype(bf16)
            du = (grad_hidden * act).astype(bf16)
            dg_ref[0, rs, :] = dg
            du_ref[0, rs, :] = du
            dx_ref[rs, :] += dot32(dg, g_ref[0], NT) + dot32(du, u_ref[0], NT)

    once = pl.Buffered(1)

    def whole(shape):
        return pl.BlockSpec(shape, lambda e: (0, 0), pipeline_mode=once)

    w_spec = pl.BlockSpec((1, width, hidden), lambda e: (e, 0, 0))
    h_spec = pl.BlockSpec((1, tokens, hidden), lambda e: (e, 0, 0))
    kept = jax.ShapeDtypeStruct((experts, tokens, hidden), bf16)
    return pl.pallas_call(
        kernel,
        grid=(experts,),
        in_specs=[whole((tokens, width)), whole((tokens, width)), whole((tokens, experts)), w_spec, w_spec, w_spec],
        out_specs=[
            pl.BlockSpec((tokens, width), lambda e: (0, 0)),
            pl.BlockSpec((tokens, experts), lambda e: (0, 0)),
            h_spec,
            h_spec,
            h_spec,
        ],
        out_shape=[
            jax.ShapeDtypeStruct((tokens, width), jnp.float32),
            jax.ShapeDtypeStruct((tokens, experts), jnp.float32),
            kept,
            kept,
            kept,
        ],
        compiler_params=pltpu.CompilerParams(vmem_limit_bytes=58 << 20),
        cost_estimate=pl.CostEstimate(
            flops=10 * tokens * width * hidden * experts,
            transcendentals=tokens * hidden * experts,
            bytes_accessed=6 * experts * hidden * (width + tokens) + 12 * tokens * width,
        ),
        name="moe_first",
    )(rows_in, upstream, weight, gate_all, up_all, down_all)


def moe_second(x_t, f_t, wh, dg, du, down_all):
    width, tokens = x_t.shape
    experts, _, hidden = down_all.shape
    bf16 = jnp.bfloat16

    def kernel(x_ref, f_ref, wh_ref, dg_ref, du_ref, d_ref, out_ref, gd_ref, gg_ref, gu_ref, acc):
        e = pl.program_id(0)

        @pl.when(e == 0)
        def _():
            acc[...] = jnp.zeros_like(acc)

        gd_ref[0] = dot32(f_ref[...], wh_ref[0]).astype(bf16)
        gg_ref[0] = dot32(x_ref[...], dg_ref[0]).astype(bf16)
        gu_ref[0] = dot32(x_ref[...], du_ref[0]).astype(bf16)
        acc[...] += dot32(wh_ref[0], d_ref[0], NT)

        @pl.when(e == experts - 1)
        def _():
            out_ref[...] = acc[...].astype(bf16)

    once = pl.Buffered(1)
    x_spec = pl.BlockSpec((width, tokens), lambda e: (0, 0), pipeline_mode=once)
    w_spec = pl.BlockSpec((1, width, hidden), lambda e: (e, 0, 0))
    h_spec = pl.BlockSpec((1, tokens, hidden), lambda e: (e, 0, 0))
    grad = jax.ShapeDtypeStruct((experts, width, hidden), bf16)
    return pl.pallas_call(
        kernel,
        grid=(experts,),
        in_specs=[x_spec, x_spec, h_spec, h_spec, h_spec, w_spec],
        out_specs=[pl.BlockSpec((tokens, width), lambda e: (0, 0)), w_spec, w_spec, w_spec],
        out_shape=[jax.ShapeDtypeStruct((tokens, width), bf16), grad, grad, grad],
        scratch_shapes=[pltpu.VMEM((tokens, width), jnp.float32)],
        compiler_params=pltpu.CompilerParams(vmem_limit_bytes=58 << 20),
        cost_estimate=pl.CostEstimate(
            flops=8 * tokens * width * hidden * experts,
            transcendentals=0,
            bytes_accessed=2 * experts * hidden * (4 * width + 3 * tokens) + 10 * tokens * width,
        ),
        name="moe_second",
    )(x_t, f_t, wh, dg, du, down_all)


def on_device(
    tokens,
    segments,
    valid,
    routes,
    cotangent,
    query_weight,
    key_weight,
    value_weight,
    output_weight,
    attn_norm_gain,
    expert_norm_gain,
    query_norm_gain,
    key_norm_gain,
    router_weight,
    gate_weight,
    up_weight,
    down_weight,
):
    f32 = jnp.float32
    bf16 = jnp.bfloat16
    local_x = tokens[0].astype(f32)
    rows_here = local_x.shape[0]
    model_width = local_x.shape[1]
    seg_all = segments[0]
    valid_all = valid[0]
    route_all = routes[0]
    length = seg_all.shape[0]
    row_offset = lax.axis_index("tensor") * rows_here
    scale = HEAD ** (-0.5)
    own_final = (
        cotangent[0].astype(f32)
        * lax.dynamic_slice_in_dim(valid_all, row_offset, rows_here).astype(f32)[:, None]
    )
    attn_all = lax.all_gather(
        jnp.stack([query_weight, key_weight, value_weight, output_weight]), "dp", axis=1, tiled=True
    )
    query_w, key_w, value_w, output_w = (attn_all[i] for i in range(4))
    gate_all = lax.all_gather(gate_weight, "dp", axis=1, tiled=True)
    up_all = lax.all_gather(up_weight, "dp", axis=1, tiled=True)
    down_all = lax.all_gather(down_weight, "dp", axis=1, tiled=True)
    local_cols = query_w.shape[1]
    heads_here = local_cols // HEAD
    head_offset = lax.axis_index("tensor") * local_cols
    gain_attn = attn_norm_gain.astype(f32)
    gain_expert = expert_norm_gain.astype(f32)
    gain_query = lax.dynamic_slice_in_dim(query_norm_gain.astype(f32), head_offset, local_cols)
    gain_key = lax.dynamic_slice_in_dim(key_norm_gain.astype(f32), head_offset, local_cols)
    normed1, unit1, scale1 = rows_norm(local_x, gain_attn)
    normed1_low = normed1.astype(bf16)
    normed1_full = in_order(ring_gather(normed1_low, "tensor"), "tensor")
    final_full = in_order(ring_gather(own_final.astype(bf16), "tensor"), "tensor")
    query_raw = jnp.dot(normed1_full, query_w, preferred_element_type=f32)
    key_raw = jnp.dot(normed1_full, key_w, preferred_element_type=f32)
    value_heads = (
        jnp.dot(normed1_full, value_w, preferred_element_type=f32)
        .astype(bf16)
        .reshape(length, heads_here, HEAD)
    )
    squares = lax.psum(
        (jnp.sum(query_raw * query_raw, axis=1), jnp.sum(key_raw * key_raw, axis=1)), "tensor"
    )
    query_scale = lax.rsqrt(squares[0] / model_width + EPS)[:, None]
    key_scale = lax.rsqrt(squares[1] / model_width + EPS)[:, None]
    query_unit = query_raw * query_scale
    key_unit = key_raw * key_scale
    cosine, sine_table = rotary_tables(length, HEAD)
    query_rot = rotate(
        (query_unit * gain_query).reshape(length, heads_here, HEAD), cosine, sine_table
    ).astype(bf16)
    key_rot = rotate(
        (key_unit * gain_key).reshape(length, heads_here, HEAD), cosine, sine_table
    ).astype(bf16)
    block_rows = min(512, length)
    starts = jnp.arange(length // block_rows, dtype=jnp.int32) * block_rows

    def attend(first_row):
        query_rows = lax.dynamic_slice_in_dim(query_rot, first_row, block_rows, 0)
        allowed = allowed_rows(seg_all, valid_all, first_row, block_rows)
        scores = jnp.einsum("qhd,khd->hqk", query_rows, key_rot, preferred_element_type=f32) * scale
        scores = jnp.where(allowed[None], scores, MASKED)
        row_max = jnp.max(scores, axis=-1, keepdims=True)
        row_exp = jnp.exp(scores - row_max)
        row_sum = jnp.sum(row_exp, axis=-1, keepdims=True)
        weights_low = (row_exp / row_sum).astype(bf16)
        mixed_rows = jnp.einsum(
            "hqk,khd->qhd", weights_low, value_heads, preferred_element_type=f32
        ).astype(bf16)
        return (mixed_rows, (row_max + jnp.log(row_sum))[..., 0])

    mixed_blocks, lse_blocks = lax.map(attend, starts)
    mixed_heads = mixed_blocks.reshape(length, local_cols)
    def rows_of(array, chunk):
        return lax.dynamic_slice_in_dim(array, chunk * rows_here, rows_here, 0)

    attn_local = ring_scatter(
        lambda c: dot32(rows_of(mixed_heads, c), output_w, NT), "tensor"
    )
    resid = local_x + attn_local
    normed2, unit2, scale2 = rows_norm(resid, gain_expert)
    normed2_low = normed2.astype(bf16)
    normed2_full = in_order(ring_gather(normed2_low, "tensor"), "tensor")
    router_f = router_weight.astype(f32)
    logits = jnp.dot(normed2_full, router_weight, preferred_element_type=f32)
    route_probs = jax.nn.softmax(logits, axis=-1)
    routed = jnp.any(
        route_all[:, :, None] == jnp.arange(EXPERTS, dtype=jnp.int32)[None, None, :], axis=1
    )
    gate_weights = jnp.where(routed, route_probs, 0.0)
    normed2_part, gate_grad_part, weighted_hidden, grad_gpre, grad_upre = moe_first(
        normed2_full, final_full, gate_weights, gate_all, up_all, down_all
    )
    prob_grad = lax.psum_scatter(
        jnp.where(routed, gate_grad_part, 0.0), "tensor", scatter_dimension=0, tiled=True
    )
    normed2_grad = ring_scatter(lambda c: rows_of(normed2_part, c), "tensor")
    moe_partial, grad_down_all, grad_gate_all, grad_up_all = moe_second(
        normed2_full.T, final_full.T, weighted_hidden, grad_gpre, grad_upre, down_all
    )
    reduced_experts = tuple(
        lax.psum_scatter(grad, "dp", scatter_dimension=1, tiled=True).astype(f32)
        for grad in (grad_gate_all, grad_up_all, grad_down_all)
    )
    grad_final = own_final
    probs_here = lax.dynamic_slice_in_dim(route_probs, row_offset, rows_here, 0)
    grad_logits = probs_here * (prob_grad - jnp.sum(probs_here * prob_grad, axis=1, keepdims=True))
    normed2_grad = normed2_grad + jnp.dot(
        grad_logits, router_f.T, precision=PRECISE, preferred_element_type=f32
    )
    grad_router_part = lax.dot_general(
        normed2_low.astype(f32),
        grad_logits,
        (((0,), (0,)), ((), ())),
        precision=PRECISE,
        preferred_element_type=f32,
    )
    resid_norm_grad, grad_expert_part = norm_back(normed2_grad, gain_expert, unit2, scale2)
    grad_resid = grad_final + resid_norm_grad
    resid_full = in_order(ring_gather(grad_resid.astype(bf16), "tensor"), "tensor")
    moe_local = ring_scatter(lambda c: rows_of(moe_partial, c).astype(f32), "tensor")
    layer_local = (resid + moe_local).astype(bf16)
    grad_output_part = lax.dot_general(
        resid_full, mixed_heads, (((0,), (0,)), ((), ())), preferred_element_type=f32
    )
    grad_mixed = (
        jnp.dot(resid_full, output_w, preferred_element_type=f32)
        .astype(bf16)
        .reshape(length, heads_here, HEAD)
    )

    def attend_back(carried, pieces):
        key_grad, value_grad = carried
        first_row, lse_rows = pieces
        query_rows = lax.dynamic_slice_in_dim(query_rot, first_row, block_rows, 0)
        mixed_grad_rows = lax.dynamic_slice_in_dim(grad_mixed, first_row, block_rows, 0)
        allowed = allowed_rows(seg_all, valid_all, first_row, block_rows)
        scores = jnp.einsum("qhd,khd->hqk", query_rows, key_rot, preferred_element_type=f32) * scale
        scores = jnp.where(allowed[None], scores, MASKED)
        weights_full = jnp.exp(scores - lse_rows[:, :, None])
        weights_low = weights_full.astype(bf16)
        value_grad = value_grad + jnp.einsum(
            "hqk,qhd->khd", weights_low, mixed_grad_rows, preferred_element_type=f32
        )
        weight_grad = jnp.einsum(
            "qhd,khd->hqk", mixed_grad_rows, value_heads, preferred_element_type=f32
        )
        row_dot = jnp.sum(weights_full * weight_grad, axis=-1, keepdims=True)
        score_grad = (weights_full * (weight_grad - row_dot)).astype(bf16)
        query_grad = (
            jnp.einsum("hqk,khd->qhd", score_grad, key_rot, preferred_element_type=f32) * scale
        )
        key_grad = (
            key_grad
            + jnp.einsum("hqk,qhd->khd", score_grad, query_rows, preferred_element_type=f32) * scale
        )
        return ((key_grad, value_grad), query_grad)

    zero_heads = jnp.zeros((length, heads_here, HEAD), f32)
    (key_rot_grad, value_grad), query_blocks = lax.scan(
        attend_back, (zero_heads, zero_heads), (starts, lse_blocks)
    )
    query_rot_grad = query_blocks.reshape(length, heads_here, HEAD)
    query_unit_grad = rotate_back(query_rot_grad, cosine, sine_table).reshape(length, local_cols)
    key_unit_grad = rotate_back(key_rot_grad, cosine, sine_table).reshape(length, local_cols)
    query_gained = query_unit_grad * gain_query
    key_gained = key_unit_grad * gain_key
    inner_sums = lax.psum(
        (jnp.sum(query_unit * query_gained, axis=1), jnp.sum(key_unit * key_gained, axis=1)),
        "tensor",
    )
    query_raw_low = (
        query_scale * (query_gained - query_unit * (inner_sums[0] / model_width)[:, None])
    ).astype(bf16)
    key_raw_low = (
        key_scale * (key_gained - key_unit * (inner_sums[1] / model_width)[:, None])
    ).astype(bf16)
    value_low = value_grad.reshape(length, local_cols).astype(bf16)
    grad_qgain_here = jnp.sum(query_unit_grad * query_unit, axis=0)
    grad_kgain_here = jnp.sum(key_unit_grad * key_unit, axis=0)
    grad_query_part = lax.dot_general(
        normed1_full, query_raw_low, (((0,), (0,)), ((), ())), preferred_element_type=f32
    )
    grad_key_part = lax.dot_general(
        normed1_full, key_raw_low, (((0,), (0,)), ((), ())), preferred_element_type=f32
    )
    grad_value_part = lax.dot_general(
        normed1_full, value_low, (((0,), (0,)), ((), ())), preferred_element_type=f32
    )
    normed1_grad = ring_scatter(
        lambda c: dot32(rows_of(query_raw_low, c), query_w, NT)
        + dot32(rows_of(key_raw_low, c), key_w, NT)
        + dot32(rows_of(value_low, c), value_w, NT),
        "tensor",
    )
    input_norm_grad, grad_attn_part = norm_back(normed1_grad, gain_attn, unit1, scale1)
    grad_input = grad_resid + input_norm_grad
    reduced_qkv = lax.psum_scatter(
        jnp.stack([grad_query_part, grad_key_part, grad_value_part]).astype(bf16),
        "dp",
        scatter_dimension=1,
        tiled=True,
    ).astype(f32)
    reduced_output = lax.psum_scatter(
        grad_output_part.astype(bf16), "dp", scatter_dimension=0, tiled=True
    ).astype(f32)
    early = all_sum(
        jnp.concatenate([grad_router_part.T, grad_expert_part[None]]), ("tensor", "dp")
    )
    zeros_width = jnp.zeros((model_width,), f32)
    qgain_full = lax.dynamic_update_slice(zeros_width, grad_qgain_here, (head_offset,))
    kgain_full = lax.dynamic_update_slice(zeros_width, grad_kgain_here, (head_offset,))
    late = all_sum(jnp.stack([qgain_full, kgain_full, grad_attn_part]), ("tensor", "dp"))
    return (
        layer_local[None],
        grad_input[None],
        reduced_qkv[0],
        reduced_qkv[1],
        reduced_qkv[2],
        reduced_output,
        reduced_experts[0],
        reduced_experts[1],
        reduced_experts[2],
        early[:EXPERTS].T,
        late[2],
        early[EXPERTS],
        late[0],
        late[1],
    )


def solution(mesh):
    in_specs = (
        P("dp", "tensor", None),
        P("dp", None),
        P("dp", None),
        P("dp", None, None),
        P("dp", "tensor", None),
        P("dp", "tensor"),
        P("dp", "tensor"),
        P("dp", "tensor"),
        P("dp", "tensor"),
        P(),
        P(),
        P(),
        P(),
        P(),
        P(None, "dp", "tensor"),
        P(None, "dp", "tensor"),
        P(None, "dp", "tensor"),
    )
    out_specs = (
        P("dp", "tensor", None),
        P("dp", "tensor", None),
        P("dp", "tensor"),
        P("dp", "tensor"),
        P("dp", "tensor"),
        P("dp", "tensor"),
        P(None, "dp", "tensor"),
        P(None, "dp", "tensor"),
        P(None, "dp", "tensor"),
        P(),
        P(),
        P(),
        P(),
        P(),
    )
    return jax.shard_map(
        on_device, mesh=mesh, in_specs=in_specs, out_specs=out_specs, check_vma=False
    )
```

```python
import jax
import jax.numpy as jnp
from jax import lax
from jax.experimental import pallas as pl
from jax.experimental.pallas import tpu as pltpu
from jax.sharding import PartitionSpec as P

HEAD = 128
EXPERTS = 16


EPS = 1e-05
THETA = 10000.0
MASKED = -1e30
PRECISE = lax.Precision.HIGHEST


def rows_norm(values, gain):
    scale = lax.rsqrt(jnp.mean(values * values, axis=-1, keepdims=True) + EPS)
    normed = values * scale
    return (normed * gain, normed, scale)


def norm_back(grad_out, gain, normed, scale):
    grad_normed = grad_out * gain
    inner_mean = jnp.mean(grad_normed * normed, axis=-1, keepdims=True)
    return (scale * (grad_normed - normed * inner_mean), jnp.sum(grad_out * normed, axis=0))


def rotary_tables(length, width):
    half = width // 2
    freq = THETA ** (-(jnp.arange(half, dtype=jnp.float32) * 2.0) / width)
    angle = jnp.arange(length, dtype=jnp.float32)[:, None] * freq[None, :]
    return (jnp.cos(angle)[:, None, :], jnp.sin(angle)[:, None, :])


NN = (((1,), (0,)), ((), ()))
NT = (((1,), (1,)), ((), ()))


def dot32(left, right, dims=NN):
    return lax.dot_general(left, right, dims, preferred_element_type=jnp.float32)


def in_order(chunks, axis):
    n = lax.axis_size(axis)
    here = lax.axis_index(axis)
    rows = chunks[0].shape[0]
    full = jnp.zeros((n * rows,) + chunks[0].shape[1:], chunks[0].dtype)
    for step, chunk in enumerate(chunks):
        full = lax.dynamic_update_slice_in_dim(full, chunk, ((here - step) % n) * rows, 0)
    return full


def held_until(value, *others):
    return lax.optimization_barrier((value,) + others)[0]


def bits_of(n):
    return [1 << k for k in range(n.bit_length() - 1)]


def swap(value, axis, bit):
    n = lax.axis_size(axis)
    return lax.ppermute(value, axis, [(i, i ^ bit) for i in range(n)])


def cube_orders(axis):
    far = bits_of(lax.axis_size(axis))[1:]
    return [far, far[::-1]]


class CubeScatter:
    def __init__(self, stay, axis):
        self.axis = axis
        self.orders = [order[1:] for order in cube_orders(axis)]
        far = bits_of(lax.axis_size(axis))[1:]
        self.left = [[b for b in far[::-1] if b in order] for order in self.orders]
        self.pieces = [
            s.reshape(s.shape[:1] + (2,) * len(order) + s.shape[2:])
            for s, order in zip(stay, self.orders)
        ]

    def start(self):
        flying, stay = [], []
        for part, piece in enumerate(self.pieces):
            bit = self.orders[part].pop(0)
            place = 1 + self.left[part].index(bit)
            self.left[part].remove(bit)
            sent = lax.index_in_dim(piece, 1, place, keepdims=False).astype(jnp.bfloat16)
            flying.append(swap(sent, self.axis, bit))
            stay.append(lax.index_in_dim(piece, 0, place, keepdims=False))
        self.pieces = stay
        return flying

    def finish(self, arrived):
        self.pieces = [
            stay.astype(jnp.float32) + came.reshape(stay.shape).astype(jnp.float32)
            for stay, came in zip(self.pieces, arrived)
        ]

    def result(self):
        return jnp.concatenate(self.pieces)


def ring_hop(total, axis):
    n = lax.axis_size(axis)
    return lax.ppermute(total, axis, [(i, (i + 1) % n) for i in range(n)])


def all_sum(value, axes):
    flat = value.reshape(-1)
    for axis in axes:
        n = lax.axis_size(axis)
        if n & (n - 1):
            flat = lax.psum(flat, axis)
            continue
        for bit in bits_of(n):
            flat = flat + swap(flat, axis, bit)
    return flat.reshape(value.shape)


def together(*values):
    return lax.optimization_barrier(values)


def xor_blocks(value, axis):
    n = lax.axis_size(axis)
    here = lax.axis_index(axis)
    blocks = jnp.split(value, n, axis=1)
    for bit in bits_of(n):
        turned = (here // bit) % 2 == 1
        blocks = [jnp.where(turned, blocks[j ^ bit], blocks[j]) for j in range(n)]
    return jnp.concatenate(blocks, axis=1)


def same_core(axis):
    n = lax.axis_size(axis)
    return [list(range(0, n, 2)), list(range(1, n, 2))]


DOC_MOST = 512
TILE = 256


def key_span(tile):
    first = max(0, tile - (DOC_MOST + TILE - 2) // TILE)
    return first * TILE, (tile + 1 - first) * TILE


def rotary_full(length, width):
    cosine, sine = rotary_tables(length, width)
    cosine, sine = cosine[:, 0], sine[:, 0]
    return jnp.concatenate([cosine, cosine], axis=1), jnp.concatenate([-sine, sine], axis=1)


def row_sums(values):
    sums = jnp.sum(values, axis=1, keepdims=True)
    return jnp.broadcast_to(sums, (values.shape[0], 128)).T[:8]


def projections(chunks, weights, places, n, filled):
    count = len(chunks)
    rows, width = chunks[0].shape
    columns = weights.shape[2]
    f32, bf16 = jnp.float32, jnp.bfloat16
    before = [] if filled is None else list(filled)

    def kernel(place_ref, *refs):
        w_ref = refs[count]
        q_ref, k_ref, v_ref, s_ref = refs[-4:]
        for s in range(count):

            @pl.when(pl.program_id(0) == s)
            def _(s=s):
                x = refs[s][...]
                for i, out in enumerate((q_ref, k_ref)):
                    raw = dot32(x, w_ref[i])
                    out[...] = raw
                    s_ref[i] = row_sums(raw * raw)
                v_ref[...] = dot32(x, w_ref[2]).astype(bf16)

    out = pl.BlockSpec((rows, columns), lambda s, place: (place[s], 0))
    return pl.pallas_call(
        kernel,
        grid_spec=pltpu.PrefetchScalarGridSpec(
            num_scalar_prefetch=1,
            grid=(count,),
            in_specs=[
                pl.BlockSpec((rows, width), lambda s, place: (0, 0), pipeline_mode=pl.Buffered(1))
            ]
            * count
            + [
                pl.BlockSpec(
                    (3, width, columns), lambda s, place: (0, 0, 0), pipeline_mode=pl.Buffered(1)
                )
            ]
            + [pl.BlockSpec(memory_space=pl.ANY)] * len(before),
            out_specs=[out, out, out, pl.BlockSpec((2, 8, rows), lambda s, place: (0, 0, place[s]))],
        ),
        out_shape=[
            jax.ShapeDtypeStruct((n * rows, columns), f32),
            jax.ShapeDtypeStruct((n * rows, columns), f32),
            jax.ShapeDtypeStruct((n * rows, columns), bf16),
            jax.ShapeDtypeStruct((2, 8, n * rows), f32),
        ],
        input_output_aliases={2 + count + i: i for i in range(len(before))},
        compiler_params=pltpu.CompilerParams(vmem_limit_bytes=58 << 20),
        cost_estimate=pl.CostEstimate(
            flops=6 * count * rows * width * columns,
            transcendentals=0,
            bytes_accessed=6 * width * columns + count * rows * (2 * width + 10 * columns),
        ),
        name="projections",
    )(jnp.stack(places).astype(jnp.int32), *chunks, weights, *before)


def projection_back(raws, gaineds, value_low, scales, inner, weights, order):
    count = len(order)
    length, columns = value_low.shape
    rows = length // count
    width = weights.shape[1]
    f32, bf16 = jnp.float32, jnp.bfloat16

    def kernel(place_ref, qr, kr, qg, kg, v_ref, s_ref, i_ref, w_ref, ql, kl, out_ref):
        total = dot32(v_ref[...], w_ref[2], NT)
        for j, (raw, gained, low) in enumerate(((qr, qg, ql), (kr, kg, kl))):
            scale = s_ref[:, j : j + 1]
            value = scale * (gained[...] - raw[...] * scale * i_ref[:, j : j + 1])
            low[...] = value.astype(bf16)
            total += dot32(value.astype(bf16), w_ref[j], NT)
        out_ref[0] = total.astype(bf16)

    part = pl.BlockSpec((rows, columns), lambda s, place: (place[s], 0))
    pair = pl.BlockSpec((rows, 2), lambda s, place: (place[s], 0))
    low_shape = jax.ShapeDtypeStruct((length, columns), bf16)
    return pl.pallas_call(
        kernel,
        grid_spec=pltpu.PrefetchScalarGridSpec(
            num_scalar_prefetch=1,
            grid=(count,),
            in_specs=[part] * 5
            + [
                pair,
                pair,
                pl.BlockSpec(
                    (3, width, columns), lambda s, place: (0, 0, 0), pipeline_mode=pl.Buffered(1)
                ),
            ],
            out_specs=[part, part, pl.BlockSpec((1, rows, width), lambda s, place: (s, 0, 0))],
        ),
        out_shape=[low_shape, low_shape, jax.ShapeDtypeStruct((count, rows, width), bf16)],
        compiler_params=pltpu.CompilerParams(vmem_limit_bytes=58 << 20),
        cost_estimate=pl.CostEstimate(
            flops=6 * length * width * columns,
            transcendentals=0,
            bytes_accessed=6 * width * columns + length * (22 * columns + 2 * width),
        ),
        name="projection_back",
    )(jnp.stack(order).astype(jnp.int32), *raws, *gaineds, value_low, scales, inner, weights)


def pair_sum(first, second):
    block = pl.BlockSpec((1,) + first.shape[1:], lambda i: (i, 0, 0, 0))

    def kernel(a_ref, b_ref, out_ref):
        add_pair((a_ref, b_ref), (out_ref,))

    return pl.pallas_call(
        kernel,
        grid=(first.shape[0],),
        in_specs=[block, block],
        out_specs=block,
        out_shape=jax.ShapeDtypeStruct(first.shape, first.dtype),
        compiler_params=pltpu.CompilerParams(vmem_limit_bytes=58 << 20),
        cost_estimate=pl.CostEstimate(flops=first.size, transcendentals=0, bytes_accessed=6 * first.size),
        name="pair_sum",
    )(first, second)


def projection_grads(firsts, places, seconds, lows, axis):
    n = lax.axis_size(axis)
    count = len(firsts)
    chunk, width = firsts[0].shape
    rows, columns = lows[0].shape
    arrays = len(lows)
    block = width // n
    half = pl.BlockSpec((1, n // 2, block, columns), lambda i, place: (i, 0, 0, 0))
    shape = jax.ShapeDtypeStruct((arrays, n // 2, block, columns), jnp.bfloat16)

    def kernel(place_ref, *refs):
        low_refs = refs[2 * count : 2 * count + arrays]
        keep_ref, send_ref, turned = refs[-3:]
        i = pl.program_id(0)
        for begin, group in ((0, refs[:count]), (arrays - 1, refs[count : 2 * count])):

            @pl.when(i == begin)
            def _(group=group):
                for s in range(count):
                    at = pl.multiple_of(place_ref[s] * chunk, chunk)
                    turned[:, pl.ds(at, chunk)] = group[s][...].T

        for j in range(arrays):

            @pl.when(i == j)
            def _(j=j):
                for q in range(n // 2):
                    for out, side in ((keep_ref, place_ref[count]), (send_ref, 1 - place_ref[count])):
                        at = pl.multiple_of((2 * q + side) * block, block)
                        product = dot32(turned[pl.ds(at, block), :], low_refs[j][...])
                        out[0, q] = product.astype(jnp.bfloat16)

    def whole(shape):
        return pl.BlockSpec(shape, lambda i, place: (0, 0), pipeline_mode=pl.Buffered(1))

    return pl.pallas_call(
        kernel,
        grid_spec=pltpu.PrefetchScalarGridSpec(
            num_scalar_prefetch=1,
            grid=(arrays,),
            in_specs=[whole((chunk, width))] * (2 * count) + [whole((rows, columns))] * arrays,
            out_specs=[half, half],
            scratch_shapes=[pltpu.VMEM((width, rows), jnp.bfloat16)],
        ),
        out_shape=[shape, shape],
        compiler_params=pltpu.CompilerParams(vmem_limit_bytes=58 << 20),
        cost_estimate=pl.CostEstimate(
            flops=2 * arrays * rows * width * columns,
            transcendentals=0,
            bytes_accessed=4 * rows * width + 2 * arrays * columns * (width + rows),
        ),
        name="projection_grads",
    )(jnp.stack([*places, lax.axis_index(axis) % 2]).astype(jnp.int32), *firsts, *seconds, *lows)


def attention_forward(query_raw, key_raw, values, scales, gains, tables, marks):
    length, columns = query_raw.shape
    heads = columns // HEAD
    tiles = length // TILE
    f32, bf16 = jnp.float32, jnp.bfloat16
    widest = max(key_span(t)[1] for t in range(tiles))

    def kernel(q_ref, k_ref, v_ref, s_ref, g_ref, cos_ref, sin_ref, col_ref, row_ref, qo, ko, mo, bias):
        @pl.when(pl.program_id(0) == 0)
        def _():
            for t in range(tiles):
                start, width = key_span(t)
                rows = pl.ds(t * TILE, TILE)
                keys = pl.ds(start, width)
                same = col_ref[rows, 0:1] == row_ref[0:1, keys]
                query_at = t * TILE + lax.broadcasted_iota(jnp.int32, (TILE, width), 0)
                key_at = start + lax.broadcasted_iota(jnp.int32, (TILE, width), 1)
                live = (row_ref[1:2, keys] == 1) | (key_at == query_at)
                ok = same & (key_at <= query_at) & live
                bias[rows, 0:width] = jnp.where(ok, 0.0, MASKED)

        cosine, sine = cos_ref[...], sin_ref[...]
        for place, (raw, out) in enumerate(((q_ref, qo), (k_ref, ko))):
            unit = raw[...] * s_ref[:, place : place + 1] * g_ref[place : place + 1, :]
            out[...] = (unit * cosine + pltpu.roll(unit, HEAD // 2, 1) * sine).astype(bf16)
        for t in range(tiles):
            start, width = key_span(t)
            rows = pl.ds(t * TILE, TILE)
            keys = pl.ds(start, width)
            scores = dot32(qo[rows, :], ko[keys, :], NT) * HEAD ** (-0.5) + bias[rows, 0:width]
            raised = jnp.exp(scores - jnp.max(scores, axis=1, keepdims=True))
            probs = (raised * (1.0 / jnp.sum(raised, axis=1, keepdims=True))).astype(bf16)
            mo[rows, :] = dot32(probs, v_ref[keys, :]).astype(bf16)

    head = pl.BlockSpec((length, HEAD), lambda h: (0, h))

    def whole(shape):
        return pl.BlockSpec(shape, lambda h: (0, 0))

    low = jax.ShapeDtypeStruct((length, columns), bf16)
    return pl.pallas_call(
        kernel,
        grid=(heads,),
        in_specs=[
            head,
            head,
            head,
            whole((length, 2)),
            pl.BlockSpec((2, HEAD), lambda h: (0, h)),
            whole((length, HEAD)),
            whole((length, HEAD)),
            whole((length, 2)),
            whole((2, length)),
        ],
        out_specs=[head, head, head],
        out_shape=[low, low, low],
        scratch_shapes=[pltpu.VMEM((length, widest), f32)],
        compiler_params=pltpu.CompilerParams(vmem_limit_bytes=58 << 20),
        cost_estimate=pl.CostEstimate(
            flops=4 * length * widest * columns,
            transcendentals=heads * length * widest,
            bytes_accessed=16 * length * columns,
        ),
        name="attention_forward",
    )(query_raw, key_raw, values, scales, gains, *tables, marks.T, marks)


def attention_backward(
    query_rot, key_rot, values, grad_mixed, query_raw, key_raw, scales, gains, tables, marks, addends, axis
):
    length, columns = query_raw.shape
    heads = columns // HEAD
    tiles = length // TILE
    f32, bf16 = jnp.float32, jnp.bfloat16
    widest = max(key_span(t)[1] for t in range(tiles))
    tn = (((0,), (0,)), ((), ()))
    experts, blocks = addends[0].shape[:2]
    each = experts // heads
    part = pl.BlockSpec((each,) + addends[0].shape[1:], lambda h: (h, 0, 0, 0))
    fewer = (blocks // 2,) + addends[0].shape[2:]
    split_specs = [
        pl.BlockSpec((each,) + fewer, lambda h: (jnp.minimum(h, heads // 2 - 1), 0, 0, 0)),
        pl.BlockSpec((each,) + fewer, lambda h: (jnp.maximum(h - heads // 2, 0), 0, 0, 0)),
    ]
    firsts = [order[0] // 2 for order in cube_orders(axis)]

    def kernel(
        q_ref, k_ref, v_ref, m_ref, qr_ref, kr_ref, s_ref, g_ref, cos_ref, sin_ref, col_ref, row_ref, a_ref, b_ref,
        dq_out, dk_out, dv_out, inner_out, gain_out, stay_0, stay_1, send_0, send_1, bias, dq, dk, dv,
    ):
        h = pl.program_id(0)
        for p, (stay, send) in enumerate(((stay_0, send_0), (stay_1, send_1))):

            @pl.when((h >= heads // 2) == bool(p))
            def _(p=p, stay=stay, send=send):
                at = [0, 0]
                for m in range(blocks):
                    out = 1 if m & firsts[p] else 0
                    total = a_ref[:, m].astype(f32) + b_ref[:, m].astype(f32)
                    (stay, send)[out][:, at[out]] = total.astype(bf16)
                    at[out] += 1

        @pl.when(h == 0)
        def _():
            inner_out[...] = jnp.zeros_like(inner_out)
            for t in range(tiles):
                start, width = key_span(t)
                rows = pl.ds(t * TILE, TILE)
                keys = pl.ds(start, width)
                same = col_ref[keys, 0:1] == row_ref[0:1, rows]
                key_at = start + lax.broadcasted_iota(jnp.int32, (width, TILE), 0)
                query_at = t * TILE + lax.broadcasted_iota(jnp.int32, (width, TILE), 1)
                live = (col_ref[keys, 1:2] == 1) | (key_at == query_at)
                ok = same & (key_at <= query_at) & live
                bias[0:width, rows] = jnp.where(ok, 0.0, MASKED)

        dk[...] = jnp.zeros_like(dk)
        dv[...] = jnp.zeros_like(dv)
        for t in range(tiles):
            start, width = key_span(t)
            rows = pl.ds(t * TILE, TILE)
            keys = pl.ds(start, width)
            scores = dot32(k_ref[keys, :], q_ref[rows, :], NT) * HEAD ** (-0.5) + bias[0:width, rows]
            raised = jnp.exp(scores - jnp.max(scores, axis=0, keepdims=True))
            probs = raised * (1.0 / jnp.sum(raised, axis=0, keepdims=True))
            dv[keys, :] += dot32(probs.astype(bf16), m_ref[rows, :])
            grad_probs = dot32(v_ref[keys, :], m_ref[rows, :], NT)
            row_dot = jnp.sum(probs * grad_probs, axis=0, keepdims=True)
            grad_scores = (probs * (grad_probs - row_dot)).astype(bf16)
            dk[keys, :] += dot32(grad_scores, q_ref[rows, :])
            dq[rows, :] = dot32(grad_scores, k_ref[keys, :], tn)
        dv_out[...] = dv[...].astype(bf16)
        cosine, sine = cos_ref[...], sin_ref[...]
        for place, (grad, raw, out) in enumerate(((dq, qr_ref, dq_out), (dk, kr_ref, dk_out))):
            turned = grad[...] * HEAD ** (-0.5)
            turned = turned * cosine + pltpu.roll(turned * sine, HEAD // 2, 1)
            unit = raw[...] * s_ref[:, place : place + 1]
            gain_out[place : place + 1, :] = jnp.sum(turned * unit, axis=0, keepdims=True)
            gained = turned * g_ref[place : place + 1, :]
            out[...] = gained
            inner_out[place] += row_sums(gained * unit)

    head = pl.BlockSpec((length, HEAD), lambda h: (0, h))

    def whole(shape):
        return pl.BlockSpec(shape, lambda h: (0, 0))

    pair = pl.BlockSpec((2, HEAD), lambda h: (0, h))
    wide = jax.ShapeDtypeStruct((length, columns), f32)
    return pl.pallas_call(
        kernel,
        grid=(heads,),
        in_specs=[
            head,
            head,
            head,
            head,
            head,
            head,
            whole((length, 2)),
            pair,
            whole((length, HEAD)),
            whole((length, HEAD)),
            whole((length, 2)),
            whole((2, length)),
            part,
            part,
        ],
        out_specs=[head, head, head, pl.BlockSpec((2, 8, length), lambda h: (0, 0, 0)), pair]
        + split_specs * 2,
        out_shape=[
            wide,
            wide,
            jax.ShapeDtypeStruct((length, columns), bf16),
            jax.ShapeDtypeStruct((2, 8, length), f32),
            jax.ShapeDtypeStruct((2, columns), f32),
        ]
        + [jax.ShapeDtypeStruct((experts // 2,) + fewer, bf16)] * 4,
        scratch_shapes=[
            pltpu.VMEM((widest, length), f32),
            pltpu.VMEM((length, HEAD), f32),
            pltpu.VMEM((length, HEAD), f32),
            pltpu.VMEM((length, HEAD), f32),
        ],
        compiler_params=pltpu.CompilerParams(vmem_limit_bytes=58 << 20),
        cost_estimate=pl.CostEstimate(
            flops=10 * length * widest * columns,
            transcendentals=heads * length * widest,
            bytes_accessed=26 * length * columns,
        ),
        name="attention_backward",
    )(
        query_rot, key_rot, values, grad_mixed, query_raw, key_raw, scales, gains, *tables, marks.T, marks, *addends
    )


def moe_first(xs, fs, weight, arrays, filled, first, total, side):
    count = len(xs)
    chunk, width = xs[0].shape
    rows = count * chunk
    parted = [isinstance(a, list) for a in arrays]
    experts = weight.shape[1]
    pieces = [a if p else [(0, experts, 0, [a])] for a, p in zip(arrays, parted)]
    hidden = pieces[0][0][3][0].shape[-1]
    step = 2 if any(parted) else (4 if count == 1 else 1)
    bf16 = jnp.bfloat16
    before = [] if filled is None else list(filled)
    flat = [(i, *group) for i, groups in enumerate(pieces) for group in groups]
    sizes = [len(entry[-1]) for entry in flat]

    def kernel(side_ref, *refs):
        x_refs, f_refs, w_ref = refs[:count], refs[count : 2 * count], refs[2 * count]
        at = 2 * count + 1
        groups = []
        for size in sizes:
            groups.append(refs[at : at + size])
            at += size
        outs = refs[at + len(before) :]
        dx_ref, gp_ref, wh_ref, dg_ref, du_ref, acc = *outs[:5], outs[-1]
        made = list(outs[5:-1])
        s = pl.program_id(0)
        ready = []
        for i in range(3):
            if not parted[i]:
                ready.append(next(g[0] for g, entry in zip(groups, flat) if entry[0] == i))
                continue
            target = made.pop(0)
            ready.append(target)
            mine = [(g, *entry[1:]) for g, entry in zip(groups, flat) if entry[0] == i]
            for refs_in, begin, held, _, blocks in mine:

                @pl.when((s * step >= begin) & (s * step < begin + held))
                def _(refs_in=refs_in, blocks=blocks, target=target, i=i):
                    high = blocks[0].shape[1]
                    for m in range(len(blocks)):
                        place = 0 if len(blocks) == 1 else (side_ref[i] ^ m) * high
                        place = 0 if len(blocks) == 1 else pl.multiple_of(place, high)
                        target[:, pl.ds(place, high), :] = refs_in[m][...]

        g_ref, u_ref, d_ref = ready

        @pl.when(s == 0)
        def _():
            acc[...] = jnp.zeros_like(acc)
            gp_ref[...] = jnp.zeros_like(gp_ref)

        lane = lax.broadcasted_iota(jnp.int32, (chunk, experts), 1)
        for r in range(count):
            rs = pl.ds(r * chunk, chunk)
            x, f = x_refs[r][...], f_refs[r][...]
            dx = None
            for j in range(step):
                e = s * step + j
                w = jnp.sum(jnp.where(lane == e, w_ref[rs, :], 0.0), axis=1, keepdims=True)
                gate_pre = dot32(x, g_ref[j])
                up_pre = dot32(x, u_ref[j])
                projected = dot32(f, d_ref[j])
                sig = 1.0 / (1.0 + jnp.exp(-gate_pre))
                act = gate_pre * sig
                hidden_f = act * up_pre
                wh_ref[j, rs, :] = (w * hidden_f).astype(bf16)
                inner = jnp.sum(hidden_f * projected, axis=1, keepdims=True)
                gp_ref[rs, :] = jnp.where(lane == e, inner, gp_ref[rs, :])
                grad_hidden = w * projected
                dg = (grad_hidden * up_pre * (sig + act * (1.0 - sig))).astype(bf16)
                du = (grad_hidden * act).astype(bf16)
                dg_ref[j, rs, :] = dg
                du_ref[j, rs, :] = du
                term = dot32(dg, g_ref[j], NT) + dot32(du, u_ref[j], NT)
                dx = term if dx is None else dx + term
            acc[rs, :] += dx

        @pl.when(s == experts // step - 1)
        def _():
            dx_ref[...] = acc[...].astype(bf16)

    def whole(shape):
        return pl.BlockSpec(shape, lambda s, side: (0, 0), pipeline_mode=pl.Buffered(1))

    def block_of(block, begin, held, base):
        return pl.BlockSpec(
            (step,) + block.shape[1:],
            lambda s, side: (base // step + jnp.clip(s - begin // step, 0, held // step - 1), 0, 0),
        )

    w_spec = pl.BlockSpec((step, width, hidden), lambda s, side: (s, 0, 0))
    h_spec = pl.BlockSpec((step, rows, hidden), lambda s, side: (s, first // count, 0))
    kept = jax.ShapeDtypeStruct((experts, total, hidden), bf16)
    blocks_in = [block for entry in flat for block in entry[-1]]
    made_count = sum(parted)
    return pl.pallas_call(
        kernel,
        grid_spec=pltpu.PrefetchScalarGridSpec(
            num_scalar_prefetch=1,
            grid=(experts // step,),
            in_specs=[whole((chunk, width))] * (2 * count)
            + [whole((rows, experts))]
            + [block_of(block, *entry[1:-1]) for entry in flat for block in entry[-1]]
            + [pl.BlockSpec(memory_space=pl.ANY)] * len(before),
            out_specs=[
                pl.BlockSpec((rows, width), lambda s, side: (0, 0)),
                pl.BlockSpec((rows, experts), lambda s, side: (0, 0)),
                h_spec,
                h_spec,
                h_spec,
            ]
            + [w_spec] * made_count,
            scratch_shapes=[pltpu.VMEM((rows, width), jnp.float32)],
        ),
        out_shape=[
            jax.ShapeDtypeStruct((rows, width), bf16),
            jax.ShapeDtypeStruct((rows, experts), jnp.float32),
            kept,
            kept,
            kept,
        ]
        + [jax.ShapeDtypeStruct((experts, width, hidden), bf16)] * made_count,
        input_output_aliases={
            2 + 2 * count + len(blocks_in) + i: 2 + i for i in range(len(before))
        },
        compiler_params=pltpu.CompilerParams(vmem_limit_bytes=58 << 20),
        cost_estimate=pl.CostEstimate(
            flops=10 * rows * width * hidden * experts,
            transcendentals=rows * hidden * experts,
            bytes_accessed=6 * experts * hidden * (width + rows) + 12 * rows * width,
        ),
        name="moe_first",
    )(side, *xs, *fs, weight, *blocks_in, *before)


def add_pair(adds, sums):
    for out in sums:
        total = adds[0][...].astype(jnp.float32) + adds[1][...].astype(jnp.float32)
        out[...] = total.astype(out.dtype)


def moe_grad_split(xs, kept, axis, side, addends=()):
    chunk, width = xs[0].shape
    experts, tokens, hidden = kept.shape
    n = lax.axis_size(axis)
    block = width // n
    count = len(xs)

    def kernel(side_ref, *refs):
        h_ref, *adds = refs[count : count + 1 + len(addends)]
        keep_ref, send_ref, *sums, turned = refs[count + 1 + len(addends) :]
        add_pair(adds, sums)

        @pl.when(pl.program_id(0) == 0)
        def _():
            for r in range(count):
                turned[:, r * chunk : (r + 1) * chunk] = refs[r][...].T

        mine = side_ref[0]
        for q in range(n // 2):
            for out, side in ((keep_ref, mine), (send_ref, 1 - mine)):
                at = pl.multiple_of((2 * q + side) * block, block)
                out[0, q] = dot32(turned[pl.ds(at, block), :], h_ref[0]).astype(jnp.bfloat16)

    half = pl.BlockSpec((1, n // 2, block, hidden), lambda e, side: (e, 0, 0, 0))
    shape = jax.ShapeDtypeStruct((experts, n // 2, block, hidden), jnp.bfloat16)
    return pl.pallas_call(
        kernel,
        grid_spec=pltpu.PrefetchScalarGridSpec(
            num_scalar_prefetch=1,
            grid=(experts,),
            in_specs=[
                pl.BlockSpec((chunk, width), lambda e, side: (0, 0), pipeline_mode=pl.Buffered(1))
            ]
            * count
            + [pl.BlockSpec((1, tokens, hidden), lambda e, side: (e, 0, 0))]
            + [half] * len(addends),
            out_specs=[half, half] + [half] * (len(addends) // 2),
            scratch_shapes=[pltpu.VMEM((width, tokens), jnp.bfloat16)],
        ),
        out_shape=[shape, shape] + [shape] * (len(addends) // 2),
        compiler_params=pltpu.CompilerParams(vmem_limit_bytes=58 << 20),
        cost_estimate=pl.CostEstimate(
            flops=2 * tokens * width * hidden * experts,
            transcendentals=0,
            bytes_accessed=2 * experts * hidden * (width + tokens) + 2 * tokens * width,
        ),
        name="moe_grad_split",
    )(jnp.asarray(side, jnp.int32).reshape(1), *xs, kept, *addends)


def moe_out(wh, down_all):
    experts, tokens, hidden = wh.shape
    width = down_all.shape[1]

    def kernel(h_ref, d_ref, out_ref, acc):
        e = pl.program_id(0)

        @pl.when(e == 0)
        def _():
            acc[...] = jnp.zeros_like(acc)

        acc[...] += dot32(h_ref[0], d_ref[0], NT)

        @pl.when(e == experts - 1)
        def _():
            out_ref[...] = acc[...].astype(jnp.bfloat16)

    return pl.pallas_call(
        kernel,
        grid=(experts,),
        in_specs=[
            pl.BlockSpec((1, tokens, hidden), lambda e: (e, 0, 0)),
            pl.BlockSpec((1, width, hidden), lambda e: (e, 0, 0)),
        ],
        out_specs=pl.BlockSpec((tokens, width), lambda e: (0, 0)),
        out_shape=jax.ShapeDtypeStruct((tokens, width), jnp.bfloat16),
        scratch_shapes=[pltpu.VMEM((tokens, width), jnp.float32)],
        compiler_params=pltpu.CompilerParams(vmem_limit_bytes=58 << 20),
        cost_estimate=pl.CostEstimate(
            flops=2 * tokens * width * hidden * experts,
            transcendentals=0,
            bytes_accessed=2 * experts * hidden * (width + tokens) + 2 * tokens * width,
        ),
        name="moe_out",
    )(wh, down_all)


def on_device(
    tokens,
    segments,
    valid,
    routes,
    cotangent,
    query_weight,
    key_weight,
    value_weight,
    output_weight,
    attn_norm_gain,
    expert_norm_gain,
    query_norm_gain,
    key_norm_gain,
    router_weight,
    gate_weight,
    up_weight,
    down_weight,
):
    f32 = jnp.float32
    bf16 = jnp.bfloat16
    local_x = tokens[0].astype(f32)
    rows_here, model_width = local_x.shape
    route_all = routes[0]
    length = segments.shape[1]
    here = lax.axis_index("tensor")
    around = lax.axis_size("tensor")
    ring_chunks = [(here - step) % around for step in range(around)]

    def rows_of(array, chunk):
        return lax.dynamic_slice_in_dim(array, chunk * rows_here, rows_here, 0)

    def hop(value):
        return ring_hop(value, "tensor")

    own_side = lax.axis_index("dp") % 2
    own_final = cotangent[0].astype(f32) * rows_of(valid[0], here).astype(f32)[:, None]

    attn_all = lax.all_gather(
        jnp.stack([query_weight, key_weight, value_weight, output_weight]), "dp", axis=1, tiled=True
    )
    query_w, key_w, value_w, output_w = (attn_all[i] for i in range(4))
    experts = down_weight.shape[0]
    half = experts // 2
    bits = bits_of(lax.axis_size("dp"))
    exchanged = [
        {0: jnp.concatenate([w[at : at + half] for w in (gate_weight, up_weight, down_weight)])}
        for at in (0, half)
    ]
    far_orders = cube_orders("dp")

    def exchange_far(stage):
        for pieces, order in zip(exchanged, far_orders):
            for mask in list(pieces):
                pieces[mask ^ order[stage]] = swap(pieces[mask], "dp", order[stage])

    def exchange_near():
        for pieces in exchanged:
            for mask in list(pieces):
                if mask ^ 1 not in pieces and not mask & 1:
                    pieces[mask ^ 1] = swap(pieces[mask], "dp", 1)

    def exchange_with(*values):
        leaves, tree = jax.tree.flatten(exchanged)
        out = together(*values, *leaves)
        exchanged[:] = jax.tree.unflatten(tree, out[len(values) :])
        return out[: len(values)]

    head_offset = here * query_w.shape[1]
    gain_attn = attn_norm_gain.astype(f32)
    gain_expert = expert_norm_gain.astype(f32)
    norm_gains = jnp.stack(
        [
            lax.dynamic_slice_in_dim(gain.astype(f32), head_offset, query_w.shape[1])
            for gain in (query_norm_gain, key_norm_gain)
        ]
    )
    normed1, unit1, scale1 = rows_norm(local_x, gain_attn)
    normed1_ring = [normed1.astype(bf16)]
    exchange_far(0)
    for _ in range(1, around):
        normed1_ring.append(hop(normed1_ring[-1]))
    normed1_ring[-2], attn_all = together(normed1_ring[-2], attn_all)
    projected = projections(normed1_ring[:-1], attn_all, ring_chunks[:-1], around, None)
    normed1_ring[-1], *projected = exchange_with(normed1_ring[-1], *projected)
    first_pieces = [dict(pieces) for pieces in exchanged]
    for stage in range(1, len(far_orders[0])):
        exchange_far(stage)
    query_raw, key_raw, value_heads, squares = projections(
        normed1_ring[-1:], attn_all, ring_chunks[-1:], around, projected
    )
    squares = all_sum(squares[:, 0], ("tensor",))
    final_ring = [held_until(xor_blocks(own_final.astype(bf16), "dp"), squares)]
    final_ring.append(hop(final_ring[0]))
    norm_scales = lax.rsqrt(squares / model_width + EPS).T
    tables = rotary_full(length, HEAD)
    marks = jnp.stack([segments[0], valid[0]])
    query_rot, key_rot, mixed_heads = attention_forward(
        query_raw, key_raw, value_heads, norm_scales, norm_gains, tables, marks
    )
    mixed_heads, final_ring[-1] = together(mixed_heads, final_ring[-1])
    for pieces, early in zip(exchanged, first_pieces):
        for mask, piece in early.items():
            pieces[mask ^ 1] = swap(held_until(piece, mixed_heads), "dp", 1)
    attn_local = dot32(rows_of(mixed_heads, (here - 1) % around), output_w, NT)
    for step in range(1, around):
        moved = hop(attn_local.astype(bf16))
        if step + 1 == around:
            (moved,) = exchange_with(moved)
            exchange_near()
        attn_local = moved.astype(f32) + dot32(
            rows_of(mixed_heads, (here - 1 - step) % around), output_w, NT
        )
    resid = local_x + attn_local
    normed2, unit2, scale2 = rows_norm(resid, gain_expert)

    normed2_ring = [normed2.astype(bf16)]
    router_f = router_weight.astype(f32)
    probs_ring, routed_ring, dx_ring, gate_grad_ring = [], [], [], []
    kept = None
    total = total_gate = None
    arrays = [
        [
            (part * half, half, i * half, [pieces[mask] for mask in sorted(pieces)])
            for part, pieces in enumerate(exchanged)
        ]
        for i in range(3)
    ]
    here_dp = lax.axis_index("dp")
    sides = jnp.stack([here_dp, here_dp, jnp.zeros_like(here_dp)]).astype(jnp.int32)
    for call in [[s] for s in range(around)]:
        last = call[-1]
        if last + 1 < around:
            normed2_ring.append(hop(normed2_ring[last]))
        if len(final_ring) < around:
            final_ring.append(hop(held_until(final_ring[-1], normed2_ring[last])))
        for s in call:
            probs_ring.append(jax.nn.softmax(dot32(normed2_ring[s], router_weight), axis=-1))
            route = rows_of(route_all, ring_chunks[s])
            routed_ring.append(
                jnp.any(route[:, :, None] == jnp.arange(EXPERTS, dtype=jnp.int32), axis=1)
            )
        weights = jnp.concatenate(
            [jnp.where(routed_ring[s], probs_ring[s], 0.0) for s in call]
        )
        if last >= 2:
            sent = dx_ring[last - 1] if total is None else (total + dx_ring[last - 1]).astype(bf16)
            sent_gate = gate_grad_ring[last - 1] if total is None else total_gate + gate_grad_ring[last - 1]
            moved, moved_gate = hop(sent), hop(sent_gate)
        outs = moe_first(
            [normed2_ring[s] for s in call],
            [final_ring[s] for s in call],
            weights,
            arrays,
            kept,
            call[0],
            length,
            sides,
        )
        waiting = [normed2_ring[-1], final_ring[-1]] + ([moved, moved_gate] if last >= 2 else [])
        held = together(*outs, *waiting)
        outs, waiting = held[: len(outs)], held[len(outs) :]
        normed2_ring[-1], final_ring[-1] = waiting[:2]
        if last >= 2:
            total, total_gate = waiting[2].astype(f32), waiting[3]
        for i, s in enumerate(call):
            dx_ring.append(outs[0][i * rows_here : (i + 1) * rows_here])
            grads = jnp.where(routed_ring[s], outs[1][i * rows_here : (i + 1) * rows_here], 0.0)
            gate_grad_ring.append(grads.T.reshape(-1))
        kept = outs[2:5]
        if len(outs) > 5:
            arrays = outs[5:]
    weighted_hidden, grad_gpre, grad_upre = kept
    down_all = arrays[2]
    sent = (total + dx_ring[around - 1]).astype(bf16)
    sent_gate = total_gate + gate_grad_ring[around - 1]
    moved, moved_gate = hop(sent), hop(sent_gate)
    gate_keep, gate_send = moe_grad_split(
        normed2_ring, held_until(grad_gpre, sent), "dp", own_side
    )
    moved, moved_gate, gate_keep, gate_send = together(moved, moved_gate, gate_keep, gate_send)
    gate_moved = swap(gate_send, "dp", 1)
    normed2_grad = moved.astype(f32) + dx_ring[0].astype(f32)
    prob_grad = (moved_gate + gate_grad_ring[0]).reshape(EXPERTS, rows_here).T
    probs_here = probs_ring[0]
    grad_logits = probs_here * (prob_grad - jnp.sum(probs_here * prob_grad, axis=1, keepdims=True))
    normed2_grad = normed2_grad + jnp.dot(
        grad_logits, router_f.T, precision=PRECISE, preferred_element_type=f32
    )
    resid_norm_grad, grad_expert_part = norm_back(normed2_grad, gain_expert, unit2, scale2)
    grad_resid = own_final + resid_norm_grad

    def reduce_rows(value):
        return lax.psum_scatter(
            value.reshape(value.shape[0], -1, value.shape[-1]),
            "dp",
            scatter_dimension=1,
            tiled=True,
            axis_index_groups=same_core("dp"),
        )

    resid_ring = [grad_resid.astype(bf16)]
    moved = hop(resid_ring[0])
    up_keep, up_send, gate_sum = moe_grad_split(
        normed2_ring, held_until(grad_upre, resid_ring[0]), "dp", own_side, (gate_keep, gate_moved)
    )
    moved, up_keep, up_send, gate_sum = together(moved, up_keep, up_send, gate_sum)
    resid_ring.append(moved)
    reduced_gate = reduce_rows(gate_sum)
    up_moved = swap(up_send, "dp", 1)
    moved = hop(resid_ring[1])
    moe_part = moe_out(held_until(weighted_hidden, up_keep), down_all)
    moved, moe_part, up_moved = together(moved, moe_part, up_moved)
    resid_ring.append(moved)
    for step in range(3, around):
        resid_ring.append(hop(resid_ring[-1]))
    down_keep, down_send, up_sum = moe_grad_split(
        final_ring, held_until(weighted_hidden, moe_part), "dp", 0, (up_keep, up_moved)
    )
    resid_ring[-1], down_keep, down_send, up_sum = together(
        resid_ring[-1], down_keep, down_send, up_sum
    )
    reduced_up = reduce_rows(up_sum)
    down_moved = swap(down_send, "dp", 1)
    resid_full = in_order(resid_ring, "tensor")
    grad_mixed = dot32(resid_full, output_w).astype(bf16)
    moe_local = moe_part[rows_here : 2 * rows_here].astype(f32)
    moe_moved = hop(held_until(moe_local.astype(bf16), resid_full))
    tn = (((0,), (0,)), ((), ()))
    query_gained, key_gained, value_low, inner_part, gain_grads, *down_split = attention_backward(
        query_rot,
        key_rot,
        value_heads,
        grad_mixed,
        query_raw,
        key_raw,
        norm_scales,
        norm_gains,
        tables,
        marks,
        (down_keep, down_moved),
        "dp",
    )
    query_gained, key_gained, inner_part, reduced_gate, moe_moved, *down_split = together(
        query_gained, key_gained, inner_part, reduced_gate, moe_moved, *down_split
    )
    down_cube = CubeScatter(down_split[:2], "dp")
    down_flying = [
        swap(sent, "dp", order[0]) for sent, order in zip(down_split[2:], cube_orders("dp"))
    ]
    moe_local = moe_moved.astype(f32) + moe_part[2 * rows_here : 3 * rows_here].astype(f32)
    moe_moved = hop(moe_local.astype(bf16))
    inner_sums = all_sum(inner_part[:, 0], ("tensor",)).T / model_width
    back_order = [(here - 1 - step) % around for step in range(around)]
    query_raw_low, key_raw_low, normed1_parts = projection_back(
        (query_raw, key_raw),
        (query_gained, key_gained),
        value_low,
        norm_scales,
        inner_sums,
        attn_all,
        back_order,
    )
    first = normed1_parts[0]
    moved = hop(first)
    attn_keep, attn_send = projection_grads(
        normed1_ring,
        ring_chunks,
        resid_ring,
        [query_raw_low, key_raw_low, value_low, held_until(mixed_heads, first)],
        "dp",
    )
    moved, attn_keep, attn_send, moe_moved, *down_flying = together(
        moved, attn_keep, attn_send, moe_moved, *down_flying
    )
    attn_moved = swap(attn_send, "dp", 1)
    down_cube.finish(down_flying)
    while down_cube.orders[0]:
        down_cube.finish(down_cube.start())
    for step in range(1, around):
        normed1_grad = moved.astype(f32) + normed1_parts[step].astype(f32)
        if step + 1 < around:
            moved = hop(normed1_grad.astype(bf16))
        if step == 1:
            attn_sum = pair_sum(attn_keep, attn_moved)
            moved, attn_sum = together(moved, attn_sum)
            reduced_attn = reduce_rows(attn_sum)
    normed1_grad, reduced_up = together(normed1_grad, reduced_up)
    moe_local = moe_moved.astype(f32) + moe_part[3 * rows_here :].astype(f32)
    moe_moved = hop(held_until(moe_local.astype(bf16), normed1_grad))
    layer_local = resid + xor_blocks(moe_moved.astype(f32) + moe_part[:rows_here].astype(f32), "dp")
    layer_local = layer_local.astype(bf16)
    reduced_down = down_cube.result()
    grad_router_part = lax.dot_general(
        normed2_ring[0].astype(f32), grad_logits, tn, precision=PRECISE, preferred_element_type=f32
    )
    input_norm_grad, grad_attn_part = norm_back(normed1_grad, gain_attn, unit1, scale1)
    grad_input = grad_resid + input_norm_grad
    gains_full = lax.dynamic_update_slice(
        jnp.zeros((2, model_width), f32), gain_grads, (0, head_offset)
    )
    sums = all_sum(
        jnp.concatenate(
            [grad_router_part.T, grad_expert_part[None], gains_full, grad_attn_part[None]]
        ),
        ("tensor", "dp"),
    )
    return (
        layer_local[None],
        grad_input[None],
        reduced_attn[0].astype(f32),
        reduced_attn[1].astype(f32),
        reduced_attn[2].astype(f32),
        reduced_attn[3].astype(f32),
        reduced_gate.astype(f32),
        reduced_up.astype(f32),
        reduced_down,
        sums[:EXPERTS].T,
        sums[EXPERTS + 3],
        sums[EXPERTS],
        sums[EXPERTS + 1],
        sums[EXPERTS + 2],
    )


def solution(mesh):
    in_specs = (
        P("dp", "tensor", None),
        P("dp", None),
        P("dp", None),
        P("dp", None, None),
        P("dp", "tensor", None),
        P("dp", "tensor"),
        P("dp", "tensor"),
        P("dp", "tensor"),
        P("dp", "tensor"),
        P(),
        P(),
        P(),
        P(),
        P(),
        P(None, "dp", "tensor"),
        P(None, "dp", "tensor"),
        P(None, "dp", "tensor"),
    )
    out_specs = (
        P("dp", "tensor", None),
        P("dp", "tensor", None),
        P("dp", "tensor"),
        P("dp", "tensor"),
        P("dp", "tensor"),
        P("dp", "tensor"),
        P(None, "dp", "tensor"),
        P(None, "dp", "tensor"),
        P(None, "dp", "tensor"),
        P(),
        P(),
        P(),
        P(),
        P(),
    )
    return jax.shard_map(
        on_device, mesh=mesh, in_specs=in_specs, out_specs=out_specs, check_vma=False
    )
```

```python
import jax
import jax.numpy as jnp
from jax import lax
from jax.experimental import pallas as pl
from jax.experimental.pallas import tpu as pltpu
from jax.sharding import PartitionSpec as P

HEAD = 128
EXPERTS = 16


EPS = 1e-05
THETA = 10000.0
MASKED = -1e30
PRECISE = lax.Precision.HIGHEST


def rows_norm(values, gain):
    scale = lax.rsqrt(jnp.mean(values * values, axis=-1, keepdims=True) + EPS)
    normed = values * scale
    return (normed * gain, normed, scale)


def norm_back(grad_out, gain, normed, scale):
    grad_normed = grad_out * gain
    inner_mean = jnp.mean(grad_normed * normed, axis=-1, keepdims=True)
    return (scale * (grad_normed - normed * inner_mean), jnp.sum(grad_out * normed, axis=0))


def rotary_tables(length, width):
    half = width // 2
    freq = THETA ** (-(jnp.arange(half, dtype=jnp.float32) * 2.0) / width)
    angle = jnp.arange(length, dtype=jnp.float32)[:, None] * freq[None, :]
    return (jnp.cos(angle)[:, None, :], jnp.sin(angle)[:, None, :])


NN = (((1,), (0,)), ((), ()))
NT = (((1,), (1,)), ((), ()))


def dot32(left, right, dims=NN):
    return lax.dot_general(left, right, dims, preferred_element_type=jnp.float32)


def in_order(chunks, axis):
    n = lax.axis_size(axis)
    here = lax.axis_index(axis)
    rows = chunks[0].shape[0]
    full = jnp.zeros((n * rows,) + chunks[0].shape[1:], chunks[0].dtype)
    for step, chunk in enumerate(chunks):
        full = lax.dynamic_update_slice_in_dim(full, chunk, ((here - step) % n) * rows, 0)
    return full


def held_until(value, *others):
    return lax.optimization_barrier((value,) + others)[0]


def bits_of(n):
    return [1 << k for k in range(n.bit_length() - 1)]


def swap(value, axis, bit):
    n = lax.axis_size(axis)
    return lax.ppermute(value, axis, [(i, i ^ bit) for i in range(n)])


def cube_orders(axis):
    far = bits_of(lax.axis_size(axis))[1:]
    return [far, far[::-1]]


class CubeScatter:
    def __init__(self, stay, axis):
        self.axis = axis
        self.orders = [order[1:] for order in cube_orders(axis)]
        far = bits_of(lax.axis_size(axis))[1:]
        self.left = [[b for b in far[::-1] if b in order] for order in self.orders]
        self.pieces = [
            s.reshape(s.shape[:1] + (2,) * len(order) + s.shape[2:])
            for s, order in zip(stay, self.orders)
        ]

    def start(self):
        flying, stay = [], []
        for part, piece in enumerate(self.pieces):
            bit = self.orders[part].pop(0)
            place = 1 + self.left[part].index(bit)
            self.left[part].remove(bit)
            sent = lax.index_in_dim(piece, 1, place, keepdims=False).astype(jnp.bfloat16)
            flying.append(swap(sent, self.axis, bit))
            stay.append(lax.index_in_dim(piece, 0, place, keepdims=False))
        self.pieces = stay
        return flying

    def finish(self, arrived):
        self.pieces = [
            stay.astype(jnp.float32) + came.reshape(stay.shape).astype(jnp.float32)
            for stay, came in zip(self.pieces, arrived)
        ]

    def result(self):
        return jnp.concatenate(self.pieces)


def ring_hop(total, axis):
    n = lax.axis_size(axis)
    return lax.ppermute(total, axis, [(i, (i + 1) % n) for i in range(n)])


def all_sum(value, axes):
    flat = value.reshape(-1)
    for axis in axes:
        n = lax.axis_size(axis)
        if n & (n - 1):
            flat = lax.psum(flat, axis)
            continue
        for bit in bits_of(n):
            flat = flat + swap(flat, axis, bit)
    return flat.reshape(value.shape)


def together(*values):
    return lax.optimization_barrier(values)


def xor_blocks(value, axis):
    n = lax.axis_size(axis)
    here = lax.axis_index(axis)
    blocks = jnp.split(value, n, axis=1)
    for bit in bits_of(n):
        turned = (here // bit) % 2 == 1
        blocks = [jnp.where(turned, blocks[j ^ bit], blocks[j]) for j in range(n)]
    return jnp.concatenate(blocks, axis=1)


def same_core(axis):
    n = lax.axis_size(axis)
    return [list(range(0, n, 2)), list(range(1, n, 2))]


DOC_MOST = 512
TILE = 256


def key_span(tile):
    first = max(0, tile - (DOC_MOST + TILE - 2) // TILE)
    return first * TILE, (tile + 1 - first) * TILE


def rotary_full(length, width):
    cosine, sine = rotary_tables(length, width)
    cosine, sine = cosine[:, 0], sine[:, 0]
    return jnp.concatenate([cosine, cosine], axis=1), jnp.concatenate([-sine, sine], axis=1)


def row_sums(values):
    sums = jnp.sum(values, axis=1, keepdims=True)
    return jnp.broadcast_to(sums, (values.shape[0], 128)).T[:8]


def projections(chunks, weights, places, n, filled):
    count = len(chunks)
    rows, width = chunks[0].shape
    columns = weights.shape[2]
    f32, bf16 = jnp.float32, jnp.bfloat16
    before = [] if filled is None else list(filled)

    def kernel(place_ref, *refs):
        w_ref = refs[count]
        q_ref, k_ref, v_ref, s_ref = refs[-4:]
        for s in range(count):

            @pl.when(pl.program_id(0) == s)
            def _(s=s):
                x = refs[s][...]
                for i, out in enumerate((q_ref, k_ref)):
                    raw = dot32(x, w_ref[i])
                    out[...] = raw
                    s_ref[i] = row_sums(raw * raw)
                v_ref[...] = dot32(x, w_ref[2]).astype(bf16)

    out = pl.BlockSpec((rows, columns), lambda s, place: (place[s], 0))
    return pl.pallas_call(
        kernel,
        grid_spec=pltpu.PrefetchScalarGridSpec(
            num_scalar_prefetch=1,
            grid=(count,),
            in_specs=[
                pl.BlockSpec((rows, width), lambda s, place: (0, 0), pipeline_mode=pl.Buffered(1))
            ]
            * count
            + [
                pl.BlockSpec(
                    (3, width, columns), lambda s, place: (0, 0, 0), pipeline_mode=pl.Buffered(1)
                )
            ]
            + [pl.BlockSpec(memory_space=pl.ANY)] * len(before),
            out_specs=[out, out, out, pl.BlockSpec((2, 8, rows), lambda s, place: (0, 0, place[s]))],
        ),
        out_shape=[
            jax.ShapeDtypeStruct((n * rows, columns), f32),
            jax.ShapeDtypeStruct((n * rows, columns), f32),
            jax.ShapeDtypeStruct((n * rows, columns), bf16),
            jax.ShapeDtypeStruct((2, 8, n * rows), f32),
        ],
        input_output_aliases={2 + count + i: i for i in range(len(before))},
        compiler_params=pltpu.CompilerParams(vmem_limit_bytes=58 << 20),
        cost_estimate=pl.CostEstimate(
            flops=6 * count * rows * width * columns,
            transcendentals=0,
            bytes_accessed=6 * width * columns + count * rows * (2 * width + 10 * columns),
        ),
        name="projections",
    )(jnp.stack(places).astype(jnp.int32), *chunks, weights, *before)


def projection_back(raws, gaineds, value_low, scales, inner, weights, order):
    count = len(order)
    length, columns = value_low.shape
    rows = length // count
    width = weights.shape[1]
    f32, bf16 = jnp.float32, jnp.bfloat16

    def kernel(place_ref, qr, kr, qg, kg, v_ref, s_ref, i_ref, w_ref, ql, kl, out_ref):
        total = dot32(v_ref[...], w_ref[2], NT)
        for j, (raw, gained, low) in enumerate(((qr, qg, ql), (kr, kg, kl))):
            scale = s_ref[:, j : j + 1]
            value = scale * (gained[...] - raw[...] * scale * i_ref[:, j : j + 1])
            low[...] = value.astype(bf16)
            total += dot32(value.astype(bf16), w_ref[j], NT)
        out_ref[0] = total.astype(bf16)

    part = pl.BlockSpec((rows, columns), lambda s, place: (place[s], 0))
    pair = pl.BlockSpec((rows, 2), lambda s, place: (place[s], 0))
    low_shape = jax.ShapeDtypeStruct((length, columns), bf16)
    return pl.pallas_call(
        kernel,
        grid_spec=pltpu.PrefetchScalarGridSpec(
            num_scalar_prefetch=1,
            grid=(count,),
            in_specs=[part] * 5
            + [
                pair,
                pair,
                pl.BlockSpec(
                    (3, width, columns), lambda s, place: (0, 0, 0), pipeline_mode=pl.Buffered(1)
                ),
            ],
            out_specs=[part, part, pl.BlockSpec((1, rows, width), lambda s, place: (s, 0, 0))],
        ),
        out_shape=[low_shape, low_shape, jax.ShapeDtypeStruct((count, rows, width), bf16)],
        compiler_params=pltpu.CompilerParams(vmem_limit_bytes=58 << 20),
        cost_estimate=pl.CostEstimate(
            flops=6 * length * width * columns,
            transcendentals=0,
            bytes_accessed=6 * width * columns + length * (22 * columns + 2 * width),
        ),
        name="projection_back",
    )(jnp.stack(order).astype(jnp.int32), *raws, *gaineds, value_low, scales, inner, weights)


def pair_split(first, second, axis):
    block = pl.BlockSpec((1,) + first.shape[1:], lambda i: (i, 0, 0, 0))
    steps = first.shape[0]
    specs, shapes = split_outs(first, steps)

    def kernel(a_ref, b_ref, *outs):
        add_split((a_ref, b_ref), outs, pl.program_id(0) >= steps // 2, cube_orders(axis))

    return pl.pallas_call(
        kernel,
        grid=(steps,),
        in_specs=[block, block],
        out_specs=specs,
        out_shape=shapes,
        compiler_params=pltpu.CompilerParams(vmem_limit_bytes=58 << 20),
        cost_estimate=pl.CostEstimate(flops=first.size, transcendentals=0, bytes_accessed=6 * first.size),
        name="pair_split",
    )(first, second)


def projection_grads(firsts, places, seconds, lows, axis):
    n = lax.axis_size(axis)
    count = len(firsts)
    chunk, width = firsts[0].shape
    rows, columns = lows[0].shape
    arrays = len(lows)
    block = width // n
    half = pl.BlockSpec((1, n // 2, block, columns), lambda i, place: (i, 0, 0, 0))
    shape = jax.ShapeDtypeStruct((arrays, n // 2, block, columns), jnp.bfloat16)

    def kernel(place_ref, *refs):
        low_refs = refs[2 * count : 2 * count + arrays]
        keep_ref, send_ref, turned = refs[-3:]
        i = pl.program_id(0)
        for begin, group in ((0, refs[:count]), (arrays - 1, refs[count : 2 * count])):

            @pl.when(i == begin)
            def _(group=group):
                for s in range(count):
                    at = pl.multiple_of(place_ref[s] * chunk, chunk)
                    turned[:, pl.ds(at, chunk)] = group[s][...].T

        for j in range(arrays):

            @pl.when(i == j)
            def _(j=j):
                for q in range(n // 2):
                    for out, side in ((keep_ref, 0), (send_ref, 1)):
                        at = pl.multiple_of(((2 * q + side) ^ place_ref[count]) * block, block)
                        product = dot32(turned[pl.ds(at, block), :], low_refs[j][...])
                        out[0, q] = product.astype(jnp.bfloat16)

    def whole(shape):
        return pl.BlockSpec(shape, lambda i, place: (0, 0), pipeline_mode=pl.Buffered(1))

    return pl.pallas_call(
        kernel,
        grid_spec=pltpu.PrefetchScalarGridSpec(
            num_scalar_prefetch=1,
            grid=(arrays,),
            in_specs=[whole((chunk, width))] * (2 * count) + [whole((rows, columns))] * arrays,
            out_specs=[half, half],
            scratch_shapes=[pltpu.VMEM((width, rows), jnp.bfloat16)],
        ),
        out_shape=[shape, shape],
        compiler_params=pltpu.CompilerParams(vmem_limit_bytes=58 << 20),
        cost_estimate=pl.CostEstimate(
            flops=2 * arrays * rows * width * columns,
            transcendentals=0,
            bytes_accessed=4 * rows * width + 2 * arrays * columns * (width + rows),
        ),
        name="projection_grads",
    )(jnp.stack([*places, lax.axis_index(axis)]).astype(jnp.int32), *firsts, *seconds, *lows)


def attention_forward(query_raw, key_raw, values, scales, gains, tables, marks):
    length, columns = query_raw.shape
    heads = columns // HEAD
    tiles = length // TILE
    f32, bf16 = jnp.float32, jnp.bfloat16
    widest = max(key_span(t)[1] for t in range(tiles))

    def kernel(q_ref, k_ref, v_ref, s_ref, g_ref, cos_ref, sin_ref, col_ref, row_ref, qo, ko, mo, bias):
        @pl.when(pl.program_id(0) == 0)
        def _():
            for t in range(tiles):
                start, width = key_span(t)
                rows = pl.ds(t * TILE, TILE)
                keys = pl.ds(start, width)
                same = col_ref[rows, 0:1] == row_ref[0:1, keys]
                query_at = t * TILE + lax.broadcasted_iota(jnp.int32, (TILE, width), 0)
                key_at = start + lax.broadcasted_iota(jnp.int32, (TILE, width), 1)
                live = (row_ref[1:2, keys] == 1) | (key_at == query_at)
                ok = same & (key_at <= query_at) & live
                bias[rows, 0:width] = jnp.where(ok, 0.0, MASKED)

        cosine, sine = cos_ref[...], sin_ref[...]
        for place, (raw, out) in enumerate(((q_ref, qo), (k_ref, ko))):
            unit = raw[...] * s_ref[:, place : place + 1] * g_ref[place : place + 1, :]
            out[...] = (unit * cosine + pltpu.roll(unit, HEAD // 2, 1) * sine).astype(bf16)
        for t in range(tiles):
            start, width = key_span(t)
            rows = pl.ds(t * TILE, TILE)
            keys = pl.ds(start, width)
            scores = dot32(qo[rows, :], ko[keys, :], NT) * HEAD ** (-0.5) + bias[rows, 0:width]
            raised = jnp.exp(scores - jnp.max(scores, axis=1, keepdims=True))
            probs = (raised * (1.0 / jnp.sum(raised, axis=1, keepdims=True))).astype(bf16)
            mo[rows, :] = dot32(probs, v_ref[keys, :]).astype(bf16)

    head = pl.BlockSpec((length, HEAD), lambda h: (0, h))

    def whole(shape):
        return pl.BlockSpec(shape, lambda h: (0, 0))

    low = jax.ShapeDtypeStruct((length, columns), bf16)
    return pl.pallas_call(
        kernel,
        grid=(heads,),
        in_specs=[
            head,
            head,
            head,
            whole((length, 2)),
            pl.BlockSpec((2, HEAD), lambda h: (0, h)),
            whole((length, HEAD)),
            whole((length, HEAD)),
            whole((length, 2)),
            whole((2, length)),
        ],
        out_specs=[head, head, head],
        out_shape=[low, low, low],
        scratch_shapes=[pltpu.VMEM((length, widest), f32)],
        compiler_params=pltpu.CompilerParams(vmem_limit_bytes=58 << 20),
        cost_estimate=pl.CostEstimate(
            flops=4 * length * widest * columns,
            transcendentals=heads * length * widest,
            bytes_accessed=16 * length * columns,
        ),
        name="attention_forward",
    )(query_raw, key_raw, values, scales, gains, *tables, marks.T, marks)


def attention_backward(
    query_rot, key_rot, values, grad_mixed, query_raw, key_raw, scales, gains, tables, marks, addends, axis
):
    length, columns = query_raw.shape
    heads = columns // HEAD
    tiles = length // TILE
    f32, bf16 = jnp.float32, jnp.bfloat16
    widest = max(key_span(t)[1] for t in range(tiles))
    tn = (((0,), (0,)), ((), ()))
    part = pl.BlockSpec(
        (addends[0].shape[0] // heads,) + addends[0].shape[1:], lambda h: (h, 0, 0, 0)
    )
    sum_specs, sum_shapes = split_outs(addends[0], heads)

    def kernel(
        q_ref, k_ref, v_ref, m_ref, qr_ref, kr_ref, s_ref, g_ref, cos_ref, sin_ref, col_ref, row_ref, a_ref, b_ref,
        dq_out, dk_out, dv_out, inner_out, gain_out, stay_0, stay_1, send_0, send_1, bias, dq, dk, dv,
    ):
        h = pl.program_id(0)
        add_split((a_ref, b_ref), (stay_0, stay_1, send_0, send_1), h >= heads // 2, cube_orders(axis))

        @pl.when(h == 0)
        def _():
            inner_out[...] = jnp.zeros_like(inner_out)
            for t in range(tiles):
                start, width = key_span(t)
                rows = pl.ds(t * TILE, TILE)
                keys = pl.ds(start, width)
                same = col_ref[keys, 0:1] == row_ref[0:1, rows]
                key_at = start + lax.broadcasted_iota(jnp.int32, (width, TILE), 0)
                query_at = t * TILE + lax.broadcasted_iota(jnp.int32, (width, TILE), 1)
                live = (col_ref[keys, 1:2] == 1) | (key_at == query_at)
                ok = same & (key_at <= query_at) & live
                bias[0:width, rows] = jnp.where(ok, 0.0, MASKED)

        dk[...] = jnp.zeros_like(dk)
        dv[...] = jnp.zeros_like(dv)
        for t in range(tiles):
            start, width = key_span(t)
            rows = pl.ds(t * TILE, TILE)
            keys = pl.ds(start, width)
            scores = dot32(k_ref[keys, :], q_ref[rows, :], NT) * HEAD ** (-0.5) + bias[0:width, rows]
            raised = jnp.exp(scores - jnp.max(scores, axis=0, keepdims=True))
            probs = raised * (1.0 / jnp.sum(raised, axis=0, keepdims=True))
            dv[keys, :] += dot32(probs.astype(bf16), m_ref[rows, :])
            grad_probs = dot32(v_ref[keys, :], m_ref[rows, :], NT)
            row_dot = jnp.sum(probs * grad_probs, axis=0, keepdims=True)
            grad_scores = (probs * (grad_probs - row_dot)).astype(bf16)
            dk[keys, :] += dot32(grad_scores, q_ref[rows, :])
            dq[rows, :] = dot32(grad_scores, k_ref[keys, :], tn)
        dv_out[...] = dv[...].astype(bf16)
        cosine, sine = cos_ref[...], sin_ref[...]
        for place, (grad, raw, out) in enumerate(((dq, qr_ref, dq_out), (dk, kr_ref, dk_out))):
            turned = grad[...] * HEAD ** (-0.5)
            turned = turned * cosine + pltpu.roll(turned * sine, HEAD // 2, 1)
            unit = raw[...] * s_ref[:, place : place + 1]
            gain_out[place : place + 1, :] = jnp.sum(turned * unit, axis=0, keepdims=True)
            gained = turned * g_ref[place : place + 1, :]
            out[...] = gained
            inner_out[place] += row_sums(gained * unit)

    head = pl.BlockSpec((length, HEAD), lambda h: (0, h))

    def whole(shape):
        return pl.BlockSpec(shape, lambda h: (0, 0))

    pair = pl.BlockSpec((2, HEAD), lambda h: (0, h))
    wide = jax.ShapeDtypeStruct((length, columns), f32)
    return pl.pallas_call(
        kernel,
        grid=(heads,),
        in_specs=[
            head,
            head,
            head,
            head,
            head,
            head,
            whole((length, 2)),
            pair,
            whole((length, HEAD)),
            whole((length, HEAD)),
            whole((length, 2)),
            whole((2, length)),
            part,
            part,
        ],
        out_specs=[head, head, head, pl.BlockSpec((2, 8, length), lambda h: (0, 0, 0)), pair]
        + sum_specs,
        out_shape=[
            wide,
            wide,
            jax.ShapeDtypeStruct((length, columns), bf16),
            jax.ShapeDtypeStruct((2, 8, length), f32),
            jax.ShapeDtypeStruct((2, columns), f32),
        ]
        + sum_shapes,
        scratch_shapes=[
            pltpu.VMEM((widest, length), f32),
            pltpu.VMEM((length, HEAD), f32),
            pltpu.VMEM((length, HEAD), f32),
            pltpu.VMEM((length, HEAD), f32),
        ],
        compiler_params=pltpu.CompilerParams(vmem_limit_bytes=58 << 20),
        cost_estimate=pl.CostEstimate(
            flops=10 * length * widest * columns,
            transcendentals=heads * length * widest,
            bytes_accessed=26 * length * columns,
        ),
        name="attention_backward",
    )(
        query_rot, key_rot, values, grad_mixed, query_raw, key_raw, scales, gains, *tables, marks.T, marks, *addends
    )


def moe_first(xs, fs, weight, arrays, span, filled, made, before, first, total, side):
    count = len(xs)
    chunk, width = xs[0].shape
    parted = isinstance(arrays[0], list)
    experts = weight.shape[1]
    pieces = arrays if parted else [[(0, experts, [(a, 0)])] for a in arrays]
    hidden = pieces[0][0][2][0][0].shape[-1]
    step = 2
    low, high = span
    bf16 = jnp.bfloat16
    flat = [(i, *group) for i, groups in enumerate(pieces) for group in groups]
    sizes = [len(entry[-1]) for entry in flat]
    aliased = list(filled or []) + list(made or [])
    before = [pair[i] for i in range(2) for pair in before or []]
    makes = 3 if parted else 0

    def kernel(side_ref, *refs):
        x_refs, f_refs, w_ref = refs[:count], refs[count : 2 * count], refs[2 * count]
        at = 2 * count + 1
        groups = []
        for size in sizes:
            groups.append(refs[at : at + size])
            at += size
        earlier = refs[at : at + len(before)]
        outs = refs[at + len(before) + len(aliased) :]
        dx_refs, gp_refs = outs[:count], outs[count : 2 * count]
        wh_ref, dg_ref, du_ref = outs[2 * count : 2 * count + 3]
        target_refs = outs[2 * count + 3 : 2 * count + 3 + makes]
        acc = outs[-1]
        s = pl.program_id(0)
        for i, target in enumerate(target_refs):
            for refs_in, entry in zip(groups, flat):
                if entry[0] != i:
                    continue
                begin, held, blocks = entry[1:]

                @pl.when((low + s * step >= begin) & (low + s * step < begin + held))
                def _(refs_in=refs_in, blocks=blocks, target=target, i=i):
                    tall = blocks[0][0].shape[1]
                    for m in range(len(blocks)):
                        place = pl.multiple_of((side_ref[i] ^ m) * tall, tall)
                        target[:, pl.ds(place, tall), :] = refs_in[m][...]

        g_ref, u_ref, d_ref = target_refs if parted else [group[0] for group in groups]

        @pl.when(s == 0)
        def _():
            for r in range(count):
                rs = pl.ds(r * chunk, chunk)
                if before:
                    acc[rs, :] = earlier[r][...].astype(jnp.float32)
                    gp_refs[r][...] = earlier[count + r][...]
                else:
                    acc[rs, :] = jnp.zeros((chunk, width), jnp.float32)
                    gp_refs[r][...] = jnp.zeros((chunk, experts), jnp.float32)

        lane = lax.broadcasted_iota(jnp.int32, (chunk, experts), 1)
        for r in range(count):
            rs = pl.ds(r * chunk, chunk)
            x, f = x_refs[r][...], f_refs[r][...]
            grads, rows_w = [], []
            for j in range(step):
                e = low + s * step + j
                w = jnp.sum(jnp.where(lane == e, w_ref[rs, :], 0.0), axis=1, keepdims=True)
                gate_pre = dot32(x, g_ref[j])
                up_pre = dot32(x, u_ref[j])
                projected = dot32(f, d_ref[j])
                sig = 1.0 / (1.0 + jnp.exp(-gate_pre))
                act = gate_pre * sig
                hidden_f = act * up_pre
                wh_ref[j, rs, :] = (w * hidden_f).astype(bf16)
                inner = jnp.sum(hidden_f * projected, axis=1, keepdims=True)
                gp_refs[r][...] = jnp.where(lane == e, inner, gp_refs[r][...])
                grad_hidden = w * projected
                dg = (grad_hidden * up_pre * (sig + act * (1.0 - sig))).astype(bf16)
                du = (grad_hidden * act).astype(bf16)
                dg_ref[j, rs, :] = dg
                du_ref[j, rs, :] = du
                grads += [dg, du]
                rows_w += [g_ref[j], u_ref[j]]
            acc[rs, :] += dot32(jnp.concatenate(grads, axis=1), jnp.concatenate(rows_w, axis=1), NT)

        @pl.when(s == (high - low) // step - 1)
        def _():
            for r in range(count):
                dx_refs[r][...] = acc[pl.ds(r * chunk, chunk), :].astype(bf16)

    def whole(shape):
        return pl.BlockSpec(shape, lambda s, side: (0, 0), pipeline_mode=pl.Buffered(1))

    def out_whole(shape):
        return pl.BlockSpec(shape, lambda s, side: (0, 0))

    def block_of(block, begin, held, base):
        return pl.BlockSpec(
            (step,) + block.shape[1:],
            lambda s, side: (
                base // step + jnp.clip(s + low // step - begin // step, 0, held // step - 1),
                0,
                0,
            ),
        )

    w_spec = pl.BlockSpec((step, width, hidden), lambda s, side: (s + low // step, 0, 0))
    h_spec = pl.BlockSpec(
        (step, count * chunk, hidden), lambda s, side: (s + low // step, first // count, 0)
    )
    kept = jax.ShapeDtypeStruct((experts, total, hidden), bf16)
    blocks_in = [block for entry in flat for block, _ in entry[-1]]
    rows = count * chunk
    ahead = 2 + 2 * count + len(blocks_in) + len(before)
    return pl.pallas_call(
        kernel,
        grid_spec=pltpu.PrefetchScalarGridSpec(
            num_scalar_prefetch=1,
            grid=((high - low) // step,),
            in_specs=[whole((chunk, width))] * (2 * count)
            + [whole((rows, experts))]
            + [block_of(block, *entry[1:-1], base) for entry in flat for block, base in entry[-1]]
            + [whole(value.shape) for value in before]
            + [pl.BlockSpec(memory_space=pl.ANY)] * len(aliased),
            out_specs=[out_whole((chunk, width))] * count
            + [out_whole((chunk, experts))] * count
            + [h_spec] * 3
            + [w_spec] * makes,
            scratch_shapes=[pltpu.VMEM((rows, width), jnp.float32)],
        ),
        out_shape=[jax.ShapeDtypeStruct((chunk, width), bf16)] * count
        + [jax.ShapeDtypeStruct((chunk, experts), jnp.float32)] * count
        + [kept] * 3
        + [jax.ShapeDtypeStruct((experts, width, hidden), bf16)] * makes,
        input_output_aliases={ahead + i: 2 * count + i for i in range(len(aliased))},
        compiler_params=pltpu.CompilerParams(vmem_limit_bytes=58 << 20),
        cost_estimate=pl.CostEstimate(
            flops=10 * rows * width * hidden * (high - low),
            transcendentals=rows * hidden * (high - low),
            bytes_accessed=6 * (high - low) * hidden * (width + rows) + 12 * rows * width,
        ),
        name="moe_first",
    )(side, *xs, *fs, weight, *blocks_in, *before, *aliased)


def add_pair(adds, sums):
    for out in sums:
        total = adds[0][...].astype(jnp.float32) + adds[1][...].astype(jnp.float32)
        out[...] = total.astype(out.dtype)


def add_split(adds, outs, late, orders):
    for p in range(2):
        targets = (outs[p], outs[2 + p])

        @pl.when(late == bool(p))
        def _(p=p, targets=targets):
            at = [0, 0]
            for m in range(adds[0].shape[1]):
                sent = 1 if m & (orders[p][0] // 2) else 0
                total = adds[0][:, m].astype(jnp.float32) + adds[1][:, m].astype(jnp.float32)
                targets[sent][:, at[sent]] = total.astype(jnp.bfloat16)
                at[sent] += 1


def split_outs(addend, steps):
    experts, blocks = addend.shape[:2]
    fewer = (blocks // 2,) + addend.shape[2:]
    each = (experts // steps,) + fewer
    specs = [
        pl.BlockSpec(each, lambda h, *_: (jnp.minimum(h, steps // 2 - 1), 0, 0, 0)),
        pl.BlockSpec(each, lambda h, *_: (jnp.maximum(h - steps // 2, 0), 0, 0, 0)),
    ]
    return specs * 2, [jax.ShapeDtypeStruct((experts // 2,) + fewer, jnp.bfloat16)] * 4


def moe_grad_split(xs, kept, axis, side, flip, addends=(), split=False):
    chunk, width = xs[0].shape
    experts, tokens, hidden = kept.shape
    n = lax.axis_size(axis)
    block = width // n
    count = len(xs)

    def kernel(side_ref, *refs):
        h_ref, *adds = refs[count : count + 1 + len(addends)]
        keep_ref, send_ref, *sums, turned = refs[count + 1 + len(addends) :]
        if split:
            add_split(adds, sums, pl.program_id(0) >= experts // 2, cube_orders(axis))
        else:
            add_pair(adds, sums)

        @pl.when(pl.program_id(0) == 0)
        def _():
            for r in range(count):
                columns = refs[r][...].T
                for j in range(n):
                    place = j ^ side_ref[1]
                    at = ((place ^ side_ref[0]) % 2) * (n // 2) + place // 2
                    at = pl.multiple_of(at * block, block)
                    turned[pl.ds(at, block), r * chunk : (r + 1) * chunk] = columns[
                        j * block : (j + 1) * block
                    ]

        product = dot32(turned[...], h_ref[0]).astype(jnp.bfloat16)
        product = product.reshape(n, block, hidden)
        keep_ref[0] = product[: n // 2]
        send_ref[0] = product[n // 2 :]

    half = pl.BlockSpec((1, n // 2, block, hidden), lambda e, side: (e, 0, 0, 0))
    shape = jax.ShapeDtypeStruct((experts, n // 2, block, hidden), jnp.bfloat16)
    sum_specs, sum_shapes = [half] * (len(addends) // 2), [shape] * (len(addends) // 2)
    if split:
        sum_specs, sum_shapes = split_outs(addends[0], experts)
    return pl.pallas_call(
        kernel,
        grid_spec=pltpu.PrefetchScalarGridSpec(
            num_scalar_prefetch=1,
            grid=(experts,),
            in_specs=[
                pl.BlockSpec((chunk, width), lambda e, side: (0, 0), pipeline_mode=pl.Buffered(1))
            ]
            * count
            + [pl.BlockSpec((1, tokens, hidden), lambda e, side: (e, 0, 0))]
            + [half] * len(addends),
            out_specs=[half, half] + sum_specs,
            scratch_shapes=[pltpu.VMEM((width, tokens), jnp.bfloat16)],
        ),
        out_shape=[shape, shape] + sum_shapes,
        compiler_params=pltpu.CompilerParams(vmem_limit_bytes=58 << 20),
        cost_estimate=pl.CostEstimate(
            flops=2 * tokens * width * hidden * experts,
            transcendentals=0,
            bytes_accessed=2 * experts * hidden * (width + tokens) + 2 * tokens * width,
        ),
        name="moe_grad_split",
    )(jnp.stack([jnp.asarray(side, jnp.int32), jnp.asarray(flip, jnp.int32)]), *xs, kept, *addends)


def moe_out(wh, down_all):
    experts, tokens, hidden = wh.shape
    width = down_all.shape[1]

    def kernel(h_ref, d_ref, out_ref, acc):
        e = pl.program_id(0)

        @pl.when(e == 0)
        def _():
            acc[...] = jnp.zeros_like(acc)

        acc[...] += dot32(h_ref[0], d_ref[0], NT)

        @pl.when(e == experts - 1)
        def _():
            out_ref[...] = acc[...].astype(jnp.bfloat16)

    return pl.pallas_call(
        kernel,
        grid=(experts,),
        in_specs=[
            pl.BlockSpec((1, tokens, hidden), lambda e: (e, 0, 0)),
            pl.BlockSpec((1, width, hidden), lambda e: (e, 0, 0)),
        ],
        out_specs=pl.BlockSpec((tokens, width), lambda e: (0, 0)),
        out_shape=jax.ShapeDtypeStruct((tokens, width), jnp.bfloat16),
        scratch_shapes=[pltpu.VMEM((tokens, width), jnp.float32)],
        compiler_params=pltpu.CompilerParams(vmem_limit_bytes=58 << 20),
        cost_estimate=pl.CostEstimate(
            flops=2 * tokens * width * hidden * experts,
            transcendentals=0,
            bytes_accessed=2 * experts * hidden * (width + tokens) + 2 * tokens * width,
        ),
        name="moe_out",
    )(wh, down_all)


def on_device(
    tokens,
    segments,
    valid,
    routes,
    cotangent,
    query_weight,
    key_weight,
    value_weight,
    output_weight,
    attn_norm_gain,
    expert_norm_gain,
    query_norm_gain,
    key_norm_gain,
    router_weight,
    gate_weight,
    up_weight,
    down_weight,
):
    f32 = jnp.float32
    bf16 = jnp.bfloat16
    local_x = tokens[0].astype(f32)
    rows_here, model_width = local_x.shape
    route_all = routes[0]
    length = segments.shape[1]
    here = lax.axis_index("tensor")
    around = lax.axis_size("tensor")
    ring_chunks = [(here - step) % around for step in range(around)]

    def rows_of(array, chunk):
        return lax.dynamic_slice_in_dim(array, chunk * rows_here, rows_here, 0)

    def hop(value):
        return ring_hop(value, "tensor")

    own_side = lax.axis_index("dp") % 2
    own_final = cotangent[0].astype(f32) * rows_of(valid[0], here).astype(f32)[:, None]

    attn_all = lax.all_gather(
        jnp.stack([query_weight, key_weight, value_weight, output_weight]), "dp", axis=1, tiled=True
    )
    query_w, key_w, value_w, output_w = (attn_all[i] for i in range(4))
    experts = down_weight.shape[0]
    half = experts // 2
    bits = bits_of(lax.axis_size("dp"))
    quarter = experts // 4
    exchanged = [
        jnp.concatenate([w[at : at + quarter] for w in (gate_weight, up_weight, down_weight)])
        for at in range(0, experts, quarter)
    ]
    masks = [[0] for _ in exchanged]
    arriving = [None] * len(exchanged)
    far_orders = cube_orders("dp")
    early, late = (0, 1), (2, 3)

    def exchange_far(stage, sets):
        for i in sets:
            arriving[i] = swap(exchanged[i], "dp", far_orders[i % 2][stage])

    def exchange_near(sets):
        for i in sets:
            arriving[i] = swap(exchanged[i], "dp", 1)

    def arrived(sets, stage, *values):
        out = together(*values, *(arriving[i] for i in sets))
        for i, value in zip(sets, out[len(values) :]):
            arriving[i] = value
        for i in sets:
            if stage is not None:
                bit = far_orders[i % 2][stage]
                exchanged[i] = jnp.concatenate([exchanged[i], arriving[i]])
                masks[i] = masks[i] + [mask ^ bit for mask in masks[i]]
        return out[: len(values)]

    def far_rest(sets):
        for stage in range(1, len(far_orders[0])):
            if stage > 1:
                arrived(sets, stage - 1)
            exchange_far(stage, sets)

    last_far = len(far_orders[0]) - 1

    head_offset = here * query_w.shape[1]
    gain_attn = attn_norm_gain.astype(f32)
    gain_expert = expert_norm_gain.astype(f32)
    norm_gains = jnp.stack(
        [
            lax.dynamic_slice_in_dim(gain.astype(f32), head_offset, query_w.shape[1])
            for gain in (query_norm_gain, key_norm_gain)
        ]
    )
    normed1, unit1, scale1 = rows_norm(local_x, gain_attn)
    normed1_ring = [normed1.astype(bf16)]
    exchange_far(0, early + late)
    for _ in range(1, around):
        normed1_ring.append(hop(normed1_ring[-1]))
    normed1_ring[-2], attn_all = together(normed1_ring[-2], attn_all)
    projected = projections(normed1_ring[:-1], attn_all, ring_chunks[:-1], around, None)
    normed1_ring[-1], *projected = arrived(early + late, 0, normed1_ring[-1], *projected)
    far_rest(early)
    query_raw, key_raw, value_heads, squares = projections(
        normed1_ring[-1:], attn_all, ring_chunks[-1:], around, projected
    )
    squares = all_sum(squares[:, 0], ("tensor",))
    final_ring = [held_until(xor_blocks(own_final.astype(bf16), "dp"), squares)]
    final_ring.append(hop(final_ring[0]))
    norm_scales = lax.rsqrt(squares / model_width + EPS).T
    tables = rotary_full(length, HEAD)
    marks = jnp.stack([segments[0], valid[0]])
    query_rot, key_rot, mixed_heads = attention_forward(
        query_raw, key_raw, value_heads, norm_scales, norm_gains, tables, marks
    )
    mixed_heads, final_ring[-1] = together(mixed_heads, final_ring[-1])
    for i in late:
        exchanged[i] = held_until(exchanged[i], mixed_heads)
    far_rest(late)
    attn_local = dot32(rows_of(mixed_heads, (here - 1) % around), output_w, NT)
    for step in range(1, around):
        moved = hop(attn_local.astype(bf16))
        if step + 2 == around:
            (moved,) = arrived(early, last_far, moved)
            exchange_near(early)
        attn_local = moved.astype(f32) + dot32(
            rows_of(mixed_heads, (here - 1 - step) % around), output_w, NT
        )
    resid = local_x + attn_local
    normed2, unit2, scale2 = rows_norm(resid, gain_expert)

    normed2_ring = [normed2.astype(bf16)]
    router_f = router_weight.astype(f32)
    probs_ring, routed_ring = [], []
    kept = None
    total = total_gate = None

    def gate_grad_of(s):
        return jnp.where(routed_ring[s], gate_part[s], 0.0).T.reshape(-1)

    late_far, late_far_near = {}, {}

    def parts_of(sets):
        groups = [[], [], []]
        for j in sets:
            places = {}
            for at, mask in enumerate(masks[j]):
                places[mask], places[mask ^ 1] = (exchanged[j], at), (arriving[j], at)
                if j in late_far:
                    turned = mask ^ far_orders[j % 2][last_far]
                    places[turned], places[turned ^ 1] = (late_far[j], at), (late_far_near[j], at)
            for i in range(3):
                blocks = [
                    (places[m][0], (3 * places[m][1] + i) * quarter) for m in sorted(places)
                ]
                groups[i].append((j * quarter, quarter, blocks))
        return groups

    here_dp = lax.axis_index("dp")
    sides = jnp.stack([here_dp, here_dp, jnp.zeros_like(here_dp)]).astype(jnp.int32)
    dx_ring, gate_part = {}, {}
    arrays = made = None
    calls = [((0,), early), ((1,), early), ((0, 1), late)] + [((s,), None) for s in range(2, around)]
    for number, (call, sets) in enumerate(calls):
        if number + 1 < around:
            normed2_ring.append(hop(normed2_ring[number]))
        if len(final_ring) < around and number >= 2:
            final_ring.append(hop(final_ring[-1]))
        for s in call:
            if s < len(probs_ring):
                continue
            probs_ring.append(jax.nn.softmax(dot32(normed2_ring[s], router_weight), axis=-1))
            route = rows_of(route_all, ring_chunks[s])
            routed_ring.append(
                jnp.any(route[:, :, None] == jnp.arange(EXPERTS, dtype=jnp.int32), axis=1)
            )
        weights = jnp.concatenate([jnp.where(routed_ring[s], probs_ring[s], 0.0) for s in call])
        flying = []
        if sets is None:
            s = call[0] - 1
            sent = dx_ring[s] if total is None else (total + dx_ring[s]).astype(bf16)
            sent_gate = gate_grad_of(s) if total is None else total_gate + gate_grad_of(s)
            flying = [hop(sent), hop(sent_gate)]
        outs = moe_first(
            [normed2_ring[s] for s in call],
            [final_ring[s] for s in call],
            weights,
            arrays if sets != late and arrays is not None and number > 0 else parts_of(sets),
            (0, experts) if sets is None else (half * (sets == late), half * (1 + (sets == late))),
            kept,
            made if sets == late else None,
            [(dx_ring[s], gate_part[s]) for s in call] if sets == late else None,
            call[0],
            length,
            sides,
        )
        waiting = [normed2_ring[-1], final_ring[-1], *flying]
        held = together(*outs, *waiting)
        outs, waiting = held[: len(outs)], held[len(outs) :]
        normed2_ring[-1], final_ring[-1] = waiting[:2]
        if number == 0:
            (normed2_ring[-1],) = arrived(late, None, normed2_ring[-1])
            late_far = {i: arriving[i] for i in late}
            late_far_near = {i: swap(late_far[i], "dp", 1) for i in late}
            exchange_near(late)
        if flying:
            total, total_gate = waiting[2].astype(f32), waiting[3]
        count = len(call)
        for i, s in enumerate(call):
            dx_ring[s], gate_part[s] = outs[i], outs[count + i]
        kept = outs[2 * count : 2 * count + 3]
        if len(outs) > 2 * count + 3:
            arrays = made = outs[2 * count + 3 :]
    weighted_hidden, grad_gpre, grad_upre = kept
    down_all = arrays[2]
    sent = (total + dx_ring[around - 1]).astype(bf16)
    sent_gate = total_gate + gate_grad_of(around - 1)
    moved, moved_gate = hop(sent), hop(sent_gate)
    gate_keep, gate_send = moe_grad_split(
        normed2_ring, held_until(grad_gpre, sent), "dp", own_side, 0
    )
    moved, moved_gate, gate_keep, gate_send = together(moved, moved_gate, gate_keep, gate_send)
    gate_moved = swap(gate_send, "dp", 1)
    normed2_grad = moved.astype(f32) + dx_ring[0].astype(f32)
    prob_grad = (moved_gate + gate_grad_of(0)).reshape(EXPERTS, rows_here).T
    probs_here = probs_ring[0]
    grad_logits = probs_here * (prob_grad - jnp.sum(probs_here * prob_grad, axis=1, keepdims=True))
    normed2_grad = normed2_grad + jnp.dot(
        grad_logits, router_f.T, precision=PRECISE, preferred_element_type=f32
    )
    resid_norm_grad, grad_expert_part = norm_back(normed2_grad, gain_expert, unit2, scale2)
    grad_resid = own_final + resid_norm_grad

    def reduce_rows(value):
        return lax.psum_scatter(
            value.reshape(value.shape[0], -1, value.shape[-1]),
            "dp",
            scatter_dimension=1,
            tiled=True,
            axis_index_groups=same_core("dp"),
        )

    resid_ring = [grad_resid.astype(bf16)]
    moved = hop(resid_ring[0])
    up_keep, up_send, gate_sum = moe_grad_split(
        normed2_ring, held_until(grad_upre, resid_ring[0]), "dp", 0, here_dp, (gate_keep, gate_moved)
    )
    moved, up_keep, up_send, gate_sum = together(moved, up_keep, up_send, gate_sum)
    resid_ring.append(moved)
    reduced_gate = reduce_rows(gate_sum)
    up_moved = swap(up_send, "dp", 1)
    moved = hop(resid_ring[1])
    moe_part = moe_out(held_until(weighted_hidden, up_keep), down_all)
    moved, moe_part, up_moved = together(moved, moe_part, up_moved)
    resid_ring.append(moved)
    for step in range(3, around):
        resid_ring.append(hop(resid_ring[-1]))
    down_keep, down_send, *up_split = moe_grad_split(
        final_ring, held_until(weighted_hidden, moe_part), "dp", 0, 0, (up_keep, up_moved), True
    )
    resid_ring[-1], down_keep, down_send, *up_split = together(
        resid_ring[-1], down_keep, down_send, *up_split
    )

    def cube_begin(split):
        flying = [swap(sent, "dp", order[0]) for sent, order in zip(split[2:], cube_orders("dp"))]
        return CubeScatter(split[:2], "dp"), flying

    up_cube, up_flying = cube_begin(up_split)
    down_moved = swap(down_send, "dp", 1)
    resid_full = in_order(resid_ring, "tensor")
    grad_mixed = dot32(resid_full, output_w).astype(bf16)
    moe_local = moe_part[rows_here : 2 * rows_here].astype(f32)
    moe_moved = hop(held_until(moe_local.astype(bf16), resid_full))
    tn = (((0,), (0,)), ((), ()))
    query_gained, key_gained, value_low, inner_part, gain_grads, *down_split = attention_backward(
        query_rot,
        key_rot,
        value_heads,
        grad_mixed,
        query_raw,
        key_raw,
        norm_scales,
        norm_gains,
        tables,
        marks,
        (down_keep, down_moved),
        "dp",
    )
    query_gained, key_gained, inner_part, reduced_gate, moe_moved, *down_split = together(
        query_gained, key_gained, inner_part, reduced_gate, moe_moved, *down_split
    )
    down_cube, down_flying = cube_begin(down_split)
    moe_local = moe_moved.astype(f32) + moe_part[2 * rows_here : 3 * rows_here].astype(f32)
    moe_moved = hop(moe_local.astype(bf16))
    inner_sums = all_sum(inner_part[:, 0], ("tensor",)).T / model_width
    inner_sums, *up_flying = together(inner_sums, *up_flying)
    up_cube.finish(up_flying)
    up_flying = up_cube.start()
    back_order = [(here - 1 - step) % around for step in range(around)]
    query_raw_low, key_raw_low, normed1_parts = projection_back(
        (query_raw, key_raw),
        (query_gained, key_gained),
        value_low,
        norm_scales,
        inner_sums,
        attn_all,
        back_order,
    )
    first = normed1_parts[0]
    moved = hop(first)
    attn_keep, attn_send = projection_grads(
        normed1_ring,
        ring_chunks,
        resid_ring,
        [query_raw_low, key_raw_low, value_low, held_until(mixed_heads, first)],
        "dp",
    )
    moved, attn_keep, attn_send, moe_moved, up_flying, down_flying = jax.tree.unflatten(
        jax.tree.structure((0, 0, 0, 0, [0, 0], [0, 0])),
        together(moved, attn_keep, attn_send, moe_moved, *up_flying, *down_flying),
    )
    up_cube.finish(up_flying)
    while up_cube.orders[0]:
        up_cube.finish(up_cube.start())
    attn_moved = swap(attn_send, "dp", 1)
    down_cube.finish(down_flying)
    while down_cube.orders[0]:
        down_cube.finish(down_cube.start())
    for step in range(1, around):
        normed1_grad = moved.astype(f32) + normed1_parts[step].astype(f32)
        if step + 1 < around:
            moved = hop(normed1_grad.astype(bf16))
        if step == 1:
            attn_split = pair_split(attn_keep, attn_moved, "dp")
            attn_cube, attn_flying = cube_begin(attn_split)
    normed1_grad, moe_moved, *attn_flying = together(normed1_grad, moe_moved, *attn_flying)
    attn_cube.finish(attn_flying)
    while attn_cube.orders[0]:
        attn_cube.finish(attn_cube.start())
    reduced_up = up_cube.result()
    reduced_attn = attn_cube.result()
    moe_local = moe_moved.astype(f32) + moe_part[3 * rows_here :].astype(f32)
    moe_moved = hop(moe_local.astype(bf16))
    layer_local = resid + xor_blocks(moe_moved.astype(f32) + moe_part[:rows_here].astype(f32), "dp")
    layer_local = layer_local.astype(bf16)
    reduced_down = down_cube.result()
    grad_router_part = lax.dot_general(
        normed2_ring[0].astype(f32), grad_logits, tn, precision=PRECISE, preferred_element_type=f32
    )
    input_norm_grad, grad_attn_part = norm_back(normed1_grad, gain_attn, unit1, scale1)
    grad_input = grad_resid + input_norm_grad
    gains_full = lax.dynamic_update_slice(
        jnp.zeros((2, model_width), f32), gain_grads, (0, head_offset)
    )
    sums = all_sum(
        jnp.concatenate(
            [grad_router_part.T, grad_expert_part[None], gains_full, grad_attn_part[None]]
        ),
        ("dp", "tensor"),
    )
    return (
        layer_local[None],
        grad_input[None],
        reduced_attn[0],
        reduced_attn[1],
        reduced_attn[2],
        reduced_attn[3],
        reduced_gate.astype(f32),
        reduced_up,
        reduced_down,
        sums[:EXPERTS].T,
        sums[EXPERTS + 3],
        sums[EXPERTS],
        sums[EXPERTS + 1],
        sums[EXPERTS + 2],
    )


def solution(mesh):
    in_specs = (
        P("dp", "tensor", None),
        P("dp", None),
        P("dp", None),
        P("dp", None, None),
        P("dp", "tensor", None),
        P("dp", "tensor"),
        P("dp", "tensor"),
        P("dp", "tensor"),
        P("dp", "tensor"),
        P(),
        P(),
        P(),
        P(),
        P(),
        P(None, "dp", "tensor"),
        P(None, "dp", "tensor"),
        P(None, "dp", "tensor"),
    )
    out_specs = (
        P("dp", "tensor", None),
        P("dp", "tensor", None),
        P("dp", "tensor"),
        P("dp", "tensor"),
        P("dp", "tensor"),
        P("dp", "tensor"),
        P(None, "dp", "tensor"),
        P(None, "dp", "tensor"),
        P(None, "dp", "tensor"),
        P(),
        P(),
        P(),
        P(),
        P(),
    )
    return jax.shard_map(
        on_device, mesh=mesh, in_specs=in_specs, out_specs=out_specs, check_vma=False
    )
```

```python
import jax
import jax.numpy as jnp
from jax import lax
from jax.experimental import pallas as pl
from jax.experimental.pallas import tpu as pltpu
from jax.sharding import PartitionSpec as P

HEAD = 128
EXPERTS = 16


EPS = 1e-05
THETA = 10000.0
MASKED = -1e30
PRECISE = lax.Precision.HIGHEST


def rows_norm(values, gain):
    scale = lax.rsqrt(jnp.mean(values * values, axis=-1, keepdims=True) + EPS)
    normed = values * scale
    return (normed * gain, normed, scale)


def norm_back(grad_out, gain, normed, scale):
    grad_normed = grad_out * gain
    inner_mean = jnp.mean(grad_normed * normed, axis=-1, keepdims=True)
    return (scale * (grad_normed - normed * inner_mean), jnp.sum(grad_out * normed, axis=0))


def rotary_tables(length, width):
    half = width // 2
    freq = THETA ** (-(jnp.arange(half, dtype=jnp.float32) * 2.0) / width)
    angle = jnp.arange(length, dtype=jnp.float32)[:, None] * freq[None, :]
    return (jnp.cos(angle)[:, None, :], jnp.sin(angle)[:, None, :])


NN = (((1,), (0,)), ((), ()))
NT = (((1,), (1,)), ((), ()))


def dot32(left, right, dims=NN):
    return lax.dot_general(left, right, dims, preferred_element_type=jnp.float32)


def in_order(chunks, axis):
    n = lax.axis_size(axis)
    here = lax.axis_index(axis)
    rows = chunks[0].shape[0]
    full = jnp.zeros((n * rows,) + chunks[0].shape[1:], chunks[0].dtype)
    for step, chunk in enumerate(chunks):
        full = lax.dynamic_update_slice_in_dim(full, chunk, ((here - step) % n) * rows, 0)
    return full


def held_until(value, *others):
    return lax.optimization_barrier((value,) + others)[0]


def bits_of(n):
    return [1 << k for k in range(n.bit_length() - 1)]


def swap(value, axis, bit):
    n = lax.axis_size(axis)
    return lax.ppermute(value, axis, [(i, i ^ bit) for i in range(n)])


def cube_orders(axis):
    far = bits_of(lax.axis_size(axis))[1:]
    return [far, far[::-1]]


class CubeScatter:
    def __init__(self, stay, axis):
        self.axis = axis
        self.orders = [order[1:] for order in cube_orders(axis)]
        far = bits_of(lax.axis_size(axis))[1:]
        self.left = [[b for b in far[::-1] if b in order] for order in self.orders]
        self.pieces = [
            s.reshape(s.shape[:1] + (2,) * len(order) + s.shape[2:])
            for s, order in zip(stay, self.orders)
        ]

    def start(self):
        flying, stay = [], []
        for part, piece in enumerate(self.pieces):
            bit = self.orders[part].pop(0)
            place = 1 + self.left[part].index(bit)
            self.left[part].remove(bit)
            sent = lax.index_in_dim(piece, 1, place, keepdims=False).astype(jnp.bfloat16)
            flying.append(swap(sent, self.axis, bit))
            stay.append(lax.index_in_dim(piece, 0, place, keepdims=False))
        self.pieces = stay
        return flying

    def finish(self, arrived):
        self.pieces = [
            stay.astype(jnp.float32) + came.reshape(stay.shape).astype(jnp.float32)
            for stay, came in zip(self.pieces, arrived)
        ]

    def result(self):
        return jnp.concatenate(self.pieces)


def ring_hop(total, axis):
    n = lax.axis_size(axis)
    return lax.ppermute(total, axis, [(i, (i + 1) % n) for i in range(n)])


def all_sum(value, axes):
    flat = value.reshape(-1)
    for axis in axes:
        n = lax.axis_size(axis)
        if n & (n - 1):
            flat = lax.psum(flat, axis)
            continue
        for bit in bits_of(n):
            flat = flat + swap(flat, axis, bit)
    return flat.reshape(value.shape)


def together(*values):
    return lax.optimization_barrier(values)


def xor_blocks(value, axis):
    n = lax.axis_size(axis)
    here = lax.axis_index(axis)
    blocks = jnp.split(value, n, axis=1)
    for bit in bits_of(n):
        turned = (here // bit) % 2 == 1
        blocks = [jnp.where(turned, blocks[j ^ bit], blocks[j]) for j in range(n)]
    return jnp.concatenate(blocks, axis=1)


def same_core(axis):
    n = lax.axis_size(axis)
    return [list(range(0, n, 2)), list(range(1, n, 2))]


DOC_MOST = 512
TILE = 256


def key_span(tile):
    first = max(0, tile - (DOC_MOST + TILE - 2) // TILE)
    return first * TILE, (tile + 1 - first) * TILE


def rotary_full(length, width):
    cosine, sine = rotary_tables(length, width)
    cosine, sine = cosine[:, 0], sine[:, 0]
    return jnp.concatenate([cosine, cosine], axis=1), jnp.concatenate([-sine, sine], axis=1)


def row_sums(values):
    sums = jnp.sum(values, axis=1, keepdims=True)
    return jnp.broadcast_to(sums, (values.shape[0], 128)).T[:8]


def projections(chunks, weights, places, n, filled):
    count = len(chunks)
    rows, width = chunks[0].shape
    columns = weights.shape[2]
    f32, bf16 = jnp.float32, jnp.bfloat16
    before = [] if filled is None else list(filled)

    def kernel(place_ref, *refs):
        w_ref = refs[count]
        q_ref, k_ref, v_ref, s_ref = refs[-4:]
        for s in range(count):

            @pl.when(pl.program_id(0) == s)
            def _(s=s):
                x = refs[s][...]
                for i, out in enumerate((q_ref, k_ref)):
                    raw = dot32(x, w_ref[i])
                    out[...] = raw
                    s_ref[i] = row_sums(raw * raw)
                v_ref[...] = dot32(x, w_ref[2]).astype(bf16)

    out = pl.BlockSpec((rows, columns), lambda s, place: (place[s], 0))
    return pl.pallas_call(
        kernel,
        grid_spec=pltpu.PrefetchScalarGridSpec(
            num_scalar_prefetch=1,
            grid=(count,),
            in_specs=[
                pl.BlockSpec((rows, width), lambda s, place: (0, 0), pipeline_mode=pl.Buffered(1))
            ]
            * count
            + [
                pl.BlockSpec(
                    (3, width, columns), lambda s, place: (0, 0, 0), pipeline_mode=pl.Buffered(1)
                )
            ]
            + [pl.BlockSpec(memory_space=pl.ANY)] * len(before),
            out_specs=[out, out, out, pl.BlockSpec((2, 8, rows), lambda s, place: (0, 0, place[s]))],
        ),
        out_shape=[
            jax.ShapeDtypeStruct((n * rows, columns), f32),
            jax.ShapeDtypeStruct((n * rows, columns), f32),
            jax.ShapeDtypeStruct((n * rows, columns), bf16),
            jax.ShapeDtypeStruct((2, 8, n * rows), f32),
        ],
        input_output_aliases={2 + count + i: i for i in range(len(before))},
        compiler_params=pltpu.CompilerParams(vmem_limit_bytes=58 << 20),
        cost_estimate=pl.CostEstimate(
            flops=6 * count * rows * width * columns,
            transcendentals=0,
            bytes_accessed=6 * width * columns + count * rows * (2 * width + 10 * columns),
        ),
        name="projections",
    )(jnp.stack(places).astype(jnp.int32), *chunks, weights, *before)


def projection_back(raws, gaineds, value_low, scales, inner, weights, order):
    count = len(order)
    length, columns = value_low.shape
    rows = length // count
    width = weights.shape[1]
    f32, bf16 = jnp.float32, jnp.bfloat16

    def kernel(place_ref, qr, kr, qg, kg, v_ref, s_ref, i_ref, w_ref, ql, kl, out_ref):
        total = dot32(v_ref[...], w_ref[2], NT)
        for j, (raw, gained, low) in enumerate(((qr, qg, ql), (kr, kg, kl))):
            scale = s_ref[:, j : j + 1]
            value = scale * (gained[...] - raw[...] * scale * i_ref[:, j : j + 1])
            low[...] = value.astype(bf16)
            total += dot32(value.astype(bf16), w_ref[j], NT)
        out_ref[0] = total.astype(bf16)

    part = pl.BlockSpec((rows, columns), lambda s, place: (place[s], 0))
    pair = pl.BlockSpec((rows, 2), lambda s, place: (place[s], 0))
    low_shape = jax.ShapeDtypeStruct((length, columns), bf16)
    return pl.pallas_call(
        kernel,
        grid_spec=pltpu.PrefetchScalarGridSpec(
            num_scalar_prefetch=1,
            grid=(count,),
            in_specs=[part] * 5
            + [
                pair,
                pair,
                pl.BlockSpec(
                    (3, width, columns), lambda s, place: (0, 0, 0), pipeline_mode=pl.Buffered(1)
                ),
            ],
            out_specs=[part, part, pl.BlockSpec((1, rows, width), lambda s, place: (s, 0, 0))],
        ),
        out_shape=[low_shape, low_shape, jax.ShapeDtypeStruct((count, rows, width), bf16)],
        compiler_params=pltpu.CompilerParams(vmem_limit_bytes=58 << 20),
        cost_estimate=pl.CostEstimate(
            flops=6 * length * width * columns,
            transcendentals=0,
            bytes_accessed=6 * width * columns + length * (22 * columns + 2 * width),
        ),
        name="projection_back",
    )(jnp.stack(order).astype(jnp.int32), *raws, *gaineds, value_low, scales, inner, weights)


def pair_split(first, second, axis):
    block = pl.BlockSpec((1,) + first.shape[1:], lambda i: (i, 0, 0, 0))
    steps = first.shape[0]
    specs, shapes = split_outs(first, steps)

    def kernel(a_ref, b_ref, *outs):
        add_split((a_ref, b_ref), outs, pl.program_id(0) >= steps // 2, cube_orders(axis))

    return pl.pallas_call(
        kernel,
        grid=(steps,),
        in_specs=[block, block],
        out_specs=specs,
        out_shape=shapes,
        compiler_params=pltpu.CompilerParams(vmem_limit_bytes=58 << 20),
        cost_estimate=pl.CostEstimate(flops=first.size, transcendentals=0, bytes_accessed=6 * first.size),
        name="pair_split",
    )(first, second)


def projection_grads(firsts, places, seconds, lows, axis):
    n = lax.axis_size(axis)
    count = len(firsts)
    chunk, width = firsts[0].shape
    rows, columns = lows[0].shape
    arrays = len(lows)
    block = width // n
    half = pl.BlockSpec((1, n // 2, block, columns), lambda i, place: (i, 0, 0, 0))
    shape = jax.ShapeDtypeStruct((arrays, n // 2, block, columns), jnp.bfloat16)

    def kernel(place_ref, *refs):
        low_refs = refs[2 * count : 2 * count + arrays]
        keep_ref, send_ref, turned = refs[-3:]
        i = pl.program_id(0)
        for begin, group in ((0, refs[:count]), (arrays - 1, refs[count : 2 * count])):

            @pl.when(i == begin)
            def _(group=group):
                for s in range(count):
                    at = pl.multiple_of(place_ref[s] * chunk, chunk)
                    turned[:, pl.ds(at, chunk)] = group[s][...].T

        for j in range(arrays):

            @pl.when(i == j)
            def _(j=j):
                for q in range(n // 2):
                    for out, side in ((keep_ref, 0), (send_ref, 1)):
                        at = pl.multiple_of(((2 * q + side) ^ place_ref[count]) * block, block)
                        product = dot32(turned[pl.ds(at, block), :], low_refs[j][...])
                        out[0, q] = product.astype(jnp.bfloat16)

    def whole(shape):
        return pl.BlockSpec(shape, lambda i, place: (0, 0), pipeline_mode=pl.Buffered(1))

    return pl.pallas_call(
        kernel,
        grid_spec=pltpu.PrefetchScalarGridSpec(
            num_scalar_prefetch=1,
            grid=(arrays,),
            in_specs=[whole((chunk, width))] * (2 * count) + [whole((rows, columns))] * arrays,
            out_specs=[half, half],
            scratch_shapes=[pltpu.VMEM((width, rows), jnp.bfloat16)],
        ),
        out_shape=[shape, shape],
        compiler_params=pltpu.CompilerParams(vmem_limit_bytes=58 << 20),
        cost_estimate=pl.CostEstimate(
            flops=2 * arrays * rows * width * columns,
            transcendentals=0,
            bytes_accessed=4 * rows * width + 2 * arrays * columns * (width + rows),
        ),
        name="projection_grads",
    )(jnp.stack([*places, lax.axis_index(axis)]).astype(jnp.int32), *firsts, *seconds, *lows)


def attention_forward(query_raw, key_raw, values, scales, gains, tables, marks):
    length, columns = query_raw.shape
    heads = columns // HEAD
    tiles = length // TILE
    f32, bf16 = jnp.float32, jnp.bfloat16
    widest = max(key_span(t)[1] for t in range(tiles))

    def kernel(q_ref, k_ref, v_ref, s_ref, g_ref, cos_ref, sin_ref, col_ref, row_ref, qo, ko, mo, bias):
        @pl.when(pl.program_id(0) == 0)
        def _():
            for t in range(tiles):
                start, width = key_span(t)
                rows = pl.ds(t * TILE, TILE)
                keys = pl.ds(start, width)
                same = col_ref[rows, 0:1] == row_ref[0:1, keys]
                query_at = t * TILE + lax.broadcasted_iota(jnp.int32, (TILE, width), 0)
                key_at = start + lax.broadcasted_iota(jnp.int32, (TILE, width), 1)
                live = (row_ref[1:2, keys] == 1) | (key_at == query_at)
                ok = same & (key_at <= query_at) & live
                bias[rows, 0:width] = jnp.where(ok, 0.0, MASKED)

        cosine, sine = cos_ref[...], sin_ref[...]
        for place, (raw, out) in enumerate(((q_ref, qo), (k_ref, ko))):
            unit = raw[...] * s_ref[:, place : place + 1] * g_ref[place : place + 1, :]
            out[...] = (unit * cosine + pltpu.roll(unit, HEAD // 2, 1) * sine).astype(bf16)
        for t in range(tiles):
            start, width = key_span(t)
            rows = pl.ds(t * TILE, TILE)
            keys = pl.ds(start, width)
            scores = dot32(qo[rows, :], ko[keys, :], NT) * HEAD ** (-0.5) + bias[rows, 0:width]
            raised = jnp.exp(scores - jnp.max(scores, axis=1, keepdims=True))
            probs = (raised * (1.0 / jnp.sum(raised, axis=1, keepdims=True))).astype(bf16)
            mo[rows, :] = dot32(probs, v_ref[keys, :]).astype(bf16)

    head = pl.BlockSpec((length, HEAD), lambda h: (0, h))

    def whole(shape):
        return pl.BlockSpec(shape, lambda h: (0, 0))

    low = jax.ShapeDtypeStruct((length, columns), bf16)
    return pl.pallas_call(
        kernel,
        grid=(heads,),
        in_specs=[
            head,
            head,
            head,
            whole((length, 2)),
            pl.BlockSpec((2, HEAD), lambda h: (0, h)),
            whole((length, HEAD)),
            whole((length, HEAD)),
            whole((length, 2)),
            whole((2, length)),
        ],
        out_specs=[head, head, head],
        out_shape=[low, low, low],
        scratch_shapes=[pltpu.VMEM((length, widest), f32)],
        compiler_params=pltpu.CompilerParams(vmem_limit_bytes=58 << 20),
        cost_estimate=pl.CostEstimate(
            flops=4 * length * widest * columns,
            transcendentals=heads * length * widest,
            bytes_accessed=16 * length * columns,
        ),
        name="attention_forward",
    )(query_raw, key_raw, values, scales, gains, *tables, marks.T, marks)


def attention_backward(
    query_rot, key_rot, values, grad_mixed, query_raw, key_raw, scales, gains, tables, marks, addends, axis
):
    length, columns = query_raw.shape
    heads = columns // HEAD
    tiles = length // TILE
    f32, bf16 = jnp.float32, jnp.bfloat16
    widest = max(key_span(t)[1] for t in range(tiles))
    tn = (((0,), (0,)), ((), ()))
    part = pl.BlockSpec(
        (addends[0].shape[0] // heads,) + addends[0].shape[1:], lambda h: (h, 0, 0, 0)
    )
    sum_specs, sum_shapes = split_outs(addends[0], heads)

    def kernel(
        q_ref, k_ref, v_ref, m_ref, qr_ref, kr_ref, s_ref, g_ref, cos_ref, sin_ref, col_ref, row_ref, a_ref, b_ref,
        dq_out, dk_out, dv_out, inner_out, gain_out, stay_0, stay_1, send_0, send_1, bias, dq, dk, dv,
    ):
        h = pl.program_id(0)
        add_split((a_ref, b_ref), (stay_0, stay_1, send_0, send_1), h >= heads // 2, cube_orders(axis))

        @pl.when(h == 0)
        def _():
            inner_out[...] = jnp.zeros_like(inner_out)
            for t in range(tiles):
                start, width = key_span(t)
                rows = pl.ds(t * TILE, TILE)
                keys = pl.ds(start, width)
                same = col_ref[keys, 0:1] == row_ref[0:1, rows]
                key_at = start + lax.broadcasted_iota(jnp.int32, (width, TILE), 0)
                query_at = t * TILE + lax.broadcasted_iota(jnp.int32, (width, TILE), 1)
                live = (col_ref[keys, 1:2] == 1) | (key_at == query_at)
                ok = same & (key_at <= query_at) & live
                bias[0:width, rows] = jnp.where(ok, 0.0, MASKED)

        dk[...] = jnp.zeros_like(dk)
        dv[...] = jnp.zeros_like(dv)
        for t in range(tiles):
            start, width = key_span(t)
            rows = pl.ds(t * TILE, TILE)
            keys = pl.ds(start, width)
            scores = dot32(k_ref[keys, :], q_ref[rows, :], NT) * HEAD ** (-0.5) + bias[0:width, rows]
            raised = jnp.exp(scores - jnp.max(scores, axis=0, keepdims=True))
            probs = raised * (1.0 / jnp.sum(raised, axis=0, keepdims=True))
            dv[keys, :] += dot32(probs.astype(bf16), m_ref[rows, :])
            grad_probs = dot32(v_ref[keys, :], m_ref[rows, :], NT)
            row_dot = jnp.sum(probs * grad_probs, axis=0, keepdims=True)
            grad_scores = (probs * (grad_probs - row_dot)).astype(bf16)
            dk[keys, :] += dot32(grad_scores, q_ref[rows, :])
            dq[rows, :] = dot32(grad_scores, k_ref[keys, :], tn)
        dv_out[...] = dv[...].astype(bf16)
        cosine, sine = cos_ref[...], sin_ref[...]
        for place, (grad, raw, out) in enumerate(((dq, qr_ref, dq_out), (dk, kr_ref, dk_out))):
            turned = grad[...] * HEAD ** (-0.5)
            turned = turned * cosine + pltpu.roll(turned * sine, HEAD // 2, 1)
            unit = raw[...] * s_ref[:, place : place + 1]
            gain_out[place : place + 1, :] = jnp.sum(turned * unit, axis=0, keepdims=True)
            gained = turned * g_ref[place : place + 1, :]
            out[...] = gained
            inner_out[place] += row_sums(gained * unit)

    head = pl.BlockSpec((length, HEAD), lambda h: (0, h))

    def whole(shape):
        return pl.BlockSpec(shape, lambda h: (0, 0))

    pair = pl.BlockSpec((2, HEAD), lambda h: (0, h))
    wide = jax.ShapeDtypeStruct((length, columns), f32)
    return pl.pallas_call(
        kernel,
        grid=(heads,),
        in_specs=[
            head,
            head,
            head,
            head,
            head,
            head,
            whole((length, 2)),
            pair,
            whole((length, HEAD)),
            whole((length, HEAD)),
            whole((length, 2)),
            whole((2, length)),
            part,
            part,
        ],
        out_specs=[head, head, head, pl.BlockSpec((2, 8, length), lambda h: (0, 0, 0)), pair]
        + sum_specs,
        out_shape=[
            wide,
            wide,
            jax.ShapeDtypeStruct((length, columns), bf16),
            jax.ShapeDtypeStruct((2, 8, length), f32),
            jax.ShapeDtypeStruct((2, columns), f32),
        ]
        + sum_shapes,
        scratch_shapes=[
            pltpu.VMEM((widest, length), f32),
            pltpu.VMEM((length, HEAD), f32),
            pltpu.VMEM((length, HEAD), f32),
            pltpu.VMEM((length, HEAD), f32),
        ],
        compiler_params=pltpu.CompilerParams(vmem_limit_bytes=58 << 20),
        cost_estimate=pl.CostEstimate(
            flops=10 * length * widest * columns,
            transcendentals=heads * length * widest,
            bytes_accessed=26 * length * columns,
        ),
        name="attention_backward",
    )(
        query_rot, key_rot, values, grad_mixed, query_raw, key_raw, scales, gains, *tables, marks.T, marks, *addends
    )


def moe_first(xs, fs, weight, arrays, span, filled, made, before, first, total, side):
    count = len(xs)
    chunk, width = xs[0].shape
    parted = isinstance(arrays[0], list)
    experts = weight.shape[1]
    pieces = arrays if parted else [[(0, experts, [(a, 0)])] for a in arrays]
    hidden = pieces[0][0][2][0][0].shape[-1]
    step = 2
    low, high = span
    bf16 = jnp.bfloat16
    flat = [(i, *group) for i, groups in enumerate(pieces) for group in groups]
    sizes = [len(entry[-1]) for entry in flat]
    aliased = list(filled or []) + list(made or [])
    before = [pair[i] for i in range(2) for pair in before or []]
    makes = 3 if parted else 0

    def kernel(side_ref, *refs):
        x_refs, f_refs, w_ref = refs[:count], refs[count : 2 * count], refs[2 * count]
        at = 2 * count + 1
        groups = []
        for size in sizes:
            groups.append(refs[at : at + size])
            at += size
        earlier = refs[at : at + len(before)]
        outs = refs[at + len(before) + len(aliased) :]
        dx_refs, gp_refs = outs[:count], outs[count : 2 * count]
        wh_ref, dg_ref, du_ref = outs[2 * count : 2 * count + 3]
        target_refs = outs[2 * count + 3 : 2 * count + 3 + makes]
        acc = outs[-1]
        s = pl.program_id(0)
        for i, target in enumerate(target_refs):
            for refs_in, entry in zip(groups, flat):
                if entry[0] != i:
                    continue
                begin, held, blocks = entry[1:]

                @pl.when((low + s * step >= begin) & (low + s * step < begin + held))
                def _(refs_in=refs_in, blocks=blocks, target=target, i=i):
                    tall = blocks[0][0].shape[1]
                    for m in range(len(blocks)):
                        place = pl.multiple_of((side_ref[i] ^ m) * tall, tall)
                        target[:, pl.ds(place, tall), :] = refs_in[m][...]

        g_ref, u_ref, d_ref = target_refs if parted else [group[0] for group in groups]

        @pl.when(s == 0)
        def _():
            for r in range(count):
                rs = pl.ds(r * chunk, chunk)
                if before:
                    acc[rs, :] = earlier[r][...].astype(jnp.float32)
                    gp_refs[r][...] = earlier[count + r][...]
                else:
                    acc[rs, :] = jnp.zeros((chunk, width), jnp.float32)
                    gp_refs[r][...] = jnp.zeros((chunk, experts), jnp.float32)

        lane = lax.broadcasted_iota(jnp.int32, (chunk, experts), 1)
        for r in range(count):
            rs = pl.ds(r * chunk, chunk)
            x, f = x_refs[r][...], f_refs[r][...]
            grads, rows_w = [], []
            for j in range(step):
                e = low + s * step + j
                w = jnp.sum(jnp.where(lane == e, w_ref[rs, :], 0.0), axis=1, keepdims=True)
                gate_pre = dot32(x, g_ref[j])
                up_pre = dot32(x, u_ref[j])
                projected = dot32(f, d_ref[j])
                sig = 1.0 / (1.0 + jnp.exp(-gate_pre))
                act = gate_pre * sig
                hidden_f = act * up_pre
                wh_ref[j, rs, :] = (w * hidden_f).astype(bf16)
                inner = jnp.sum(hidden_f * projected, axis=1, keepdims=True)
                gp_refs[r][...] = jnp.where(lane == e, inner, gp_refs[r][...])
                grad_hidden = w * projected
                dg = (grad_hidden * up_pre * (sig + act * (1.0 - sig))).astype(bf16)
                du = (grad_hidden * act).astype(bf16)
                dg_ref[j, rs, :] = dg
                du_ref[j, rs, :] = du
                grads += [dg, du]
                rows_w += [g_ref[j], u_ref[j]]
            acc[rs, :] += dot32(jnp.concatenate(grads, axis=1), jnp.concatenate(rows_w, axis=1), NT)

        @pl.when(s == (high - low) // step - 1)
        def _():
            for r in range(count):
                dx_refs[r][...] = acc[pl.ds(r * chunk, chunk), :].astype(bf16)

    def whole(shape):
        return pl.BlockSpec(shape, lambda s, side: (0, 0), pipeline_mode=pl.Buffered(1))

    def out_whole(shape):
        return pl.BlockSpec(shape, lambda s, side: (0, 0))

    def block_of(block, begin, held, base):
        return pl.BlockSpec(
            (step,) + block.shape[1:],
            lambda s, side: (
                base // step + jnp.clip(s + low // step - begin // step, 0, held // step - 1),
                0,
                0,
            ),
        )

    w_spec = pl.BlockSpec((step, width, hidden), lambda s, side: (s + low // step, 0, 0))
    h_spec = pl.BlockSpec(
        (step, count * chunk, hidden), lambda s, side: (s + low // step, first // count, 0)
    )
    kept = jax.ShapeDtypeStruct((experts, total, hidden), bf16)
    blocks_in = [block for entry in flat for block, _ in entry[-1]]
    rows = count * chunk
    ahead = 2 + 2 * count + len(blocks_in) + len(before)
    return pl.pallas_call(
        kernel,
        grid_spec=pltpu.PrefetchScalarGridSpec(
            num_scalar_prefetch=1,
            grid=((high - low) // step,),
            in_specs=[whole((chunk, width))] * (2 * count)
            + [whole((rows, experts))]
            + [block_of(block, *entry[1:-1], base) for entry in flat for block, base in entry[-1]]
            + [whole(value.shape) for value in before]
            + [pl.BlockSpec(memory_space=pl.ANY)] * len(aliased),
            out_specs=[out_whole((chunk, width))] * count
            + [out_whole((chunk, experts))] * count
            + [h_spec] * 3
            + [w_spec] * makes,
            scratch_shapes=[pltpu.VMEM((rows, width), jnp.float32)],
        ),
        out_shape=[jax.ShapeDtypeStruct((chunk, width), bf16)] * count
        + [jax.ShapeDtypeStruct((chunk, experts), jnp.float32)] * count
        + [kept] * 3
        + [jax.ShapeDtypeStruct((experts, width, hidden), bf16)] * makes,
        input_output_aliases={ahead + i: 2 * count + i for i in range(len(aliased))},
        compiler_params=pltpu.CompilerParams(vmem_limit_bytes=58 << 20),
        cost_estimate=pl.CostEstimate(
            flops=10 * rows * width * hidden * (high - low),
            transcendentals=rows * hidden * (high - low),
            bytes_accessed=6 * (high - low) * hidden * (width + rows) + 12 * rows * width,
        ),
        name="moe_first",
    )(side, *xs, *fs, weight, *blocks_in, *before, *aliased)


def add_pair(adds, sums):
    for out in sums:
        total = adds[0][...].astype(jnp.float32) + adds[1][...].astype(jnp.float32)
        out[...] = total.astype(out.dtype)


def add_split(adds, outs, late, orders):
    for p in range(2):
        targets = (outs[p], outs[2 + p])

        @pl.when(late == bool(p))
        def _(p=p, targets=targets):
            at = [0, 0]
            for m in range(adds[0].shape[1]):
                sent = 1 if m & (orders[p][0] // 2) else 0
                total = adds[0][:, m].astype(jnp.float32) + adds[1][:, m].astype(jnp.float32)
                targets[sent][:, at[sent]] = total.astype(jnp.bfloat16)
                at[sent] += 1


def split_outs(addend, steps):
    experts, blocks = addend.shape[:2]
    fewer = (blocks // 2,) + addend.shape[2:]
    each = (experts // steps,) + fewer
    specs = [
        pl.BlockSpec(each, lambda h, *_: (jnp.minimum(h, steps // 2 - 1), 0, 0, 0)),
        pl.BlockSpec(each, lambda h, *_: (jnp.maximum(h - steps // 2, 0), 0, 0, 0)),
    ]
    return specs * 2, [jax.ShapeDtypeStruct((experts // 2,) + fewer, jnp.bfloat16)] * 4


def moe_grad_split(xs, kept, axis, side, flip, addends=(), split=False):
    chunk, width = xs[0].shape
    experts, tokens, hidden = kept.shape
    n = lax.axis_size(axis)
    block = width // n
    count = len(xs)

    def kernel(side_ref, *refs):
        h_ref, *adds = refs[count : count + 1 + len(addends)]
        keep_ref, send_ref, *sums, turned = refs[count + 1 + len(addends) :]
        if split:
            add_split(adds, sums, pl.program_id(0) >= experts // 2, cube_orders(axis))
        else:
            add_pair(adds, sums)

        @pl.when(pl.program_id(0) == 0)
        def _():
            for r in range(count):
                columns = refs[r][...].T
                for j in range(n):
                    place = j ^ side_ref[1]
                    at = ((place ^ side_ref[0]) % 2) * (n // 2) + place // 2
                    at = pl.multiple_of(at * block, block)
                    turned[pl.ds(at, block), r * chunk : (r + 1) * chunk] = columns[
                        j * block : (j + 1) * block
                    ]

        product = dot32(turned[...], h_ref[0]).astype(jnp.bfloat16)
        product = product.reshape(n, block, hidden)
        keep_ref[0] = product[: n // 2]
        send_ref[0] = product[n // 2 :]

    half = pl.BlockSpec((1, n // 2, block, hidden), lambda e, side: (e, 0, 0, 0))
    shape = jax.ShapeDtypeStruct((experts, n // 2, block, hidden), jnp.bfloat16)
    sum_specs, sum_shapes = [half] * (len(addends) // 2), [shape] * (len(addends) // 2)
    if split:
        sum_specs, sum_shapes = split_outs(addends[0], experts)
    return pl.pallas_call(
        kernel,
        grid_spec=pltpu.PrefetchScalarGridSpec(
            num_scalar_prefetch=1,
            grid=(experts,),
            in_specs=[
                pl.BlockSpec((chunk, width), lambda e, side: (0, 0), pipeline_mode=pl.Buffered(1))
            ]
            * count
            + [pl.BlockSpec((1, tokens, hidden), lambda e, side: (e, 0, 0))]
            + [half] * len(addends),
            out_specs=[half, half] + sum_specs,
            scratch_shapes=[pltpu.VMEM((width, tokens), jnp.bfloat16)],
        ),
        out_shape=[shape, shape] + sum_shapes,
        compiler_params=pltpu.CompilerParams(vmem_limit_bytes=58 << 20),
        cost_estimate=pl.CostEstimate(
            flops=2 * tokens * width * hidden * experts,
            transcendentals=0,
            bytes_accessed=2 * experts * hidden * (width + tokens) + 2 * tokens * width,
        ),
        name="moe_grad_split",
    )(jnp.stack([jnp.asarray(side, jnp.int32), jnp.asarray(flip, jnp.int32)]), *xs, kept, *addends)


def moe_out(wh, down_all):
    experts, tokens, hidden = wh.shape
    width = down_all.shape[1]

    def kernel(h_ref, d_ref, out_ref, acc):
        e = pl.program_id(0)

        @pl.when(e == 0)
        def _():
            acc[...] = jnp.zeros_like(acc)

        acc[...] += dot32(h_ref[0], d_ref[0], NT)

        @pl.when(e == experts - 1)
        def _():
            out_ref[...] = acc[...].astype(jnp.bfloat16)

    return pl.pallas_call(
        kernel,
        grid=(experts,),
        in_specs=[
            pl.BlockSpec((1, tokens, hidden), lambda e: (e, 0, 0)),
            pl.BlockSpec((1, width, hidden), lambda e: (e, 0, 0)),
        ],
        out_specs=pl.BlockSpec((tokens, width), lambda e: (0, 0)),
        out_shape=jax.ShapeDtypeStruct((tokens, width), jnp.bfloat16),
        scratch_shapes=[pltpu.VMEM((tokens, width), jnp.float32)],
        compiler_params=pltpu.CompilerParams(vmem_limit_bytes=58 << 20),
        cost_estimate=pl.CostEstimate(
            flops=2 * tokens * width * hidden * experts,
            transcendentals=0,
            bytes_accessed=2 * experts * hidden * (width + tokens) + 2 * tokens * width,
        ),
        name="moe_out",
    )(wh, down_all)


def on_device(
    tokens,
    segments,
    valid,
    routes,
    cotangent,
    query_weight,
    key_weight,
    value_weight,
    output_weight,
    attn_norm_gain,
    expert_norm_gain,
    query_norm_gain,
    key_norm_gain,
    router_weight,
    gate_weight,
    up_weight,
    down_weight,
):
    f32 = jnp.float32
    bf16 = jnp.bfloat16
    local_x = tokens[0].astype(f32)
    rows_here, model_width = local_x.shape
    route_all = routes[0]
    length = segments.shape[1]
    here = lax.axis_index("tensor")
    around = lax.axis_size("tensor")
    ring_chunks = [(here - step) % around for step in range(around)]

    def rows_of(array, chunk):
        return lax.dynamic_slice_in_dim(array, chunk * rows_here, rows_here, 0)

    def hop(value):
        return ring_hop(value, "tensor")

    own_side = lax.axis_index("dp") % 2
    own_final = cotangent[0].astype(f32) * rows_of(valid[0], here).astype(f32)[:, None]

    attn_all = lax.all_gather(
        jnp.stack([query_weight, key_weight, value_weight, output_weight]), "dp", axis=1, tiled=True
    )
    query_w, key_w, value_w, output_w = (attn_all[i] for i in range(4))
    experts = down_weight.shape[0]
    half = experts // 2
    bits = bits_of(lax.axis_size("dp"))
    quarter = experts // 4
    exchanged = [
        jnp.concatenate([w[at : at + quarter] for w in (gate_weight, up_weight, down_weight)])
        for at in range(0, experts, quarter)
    ]
    masks = [[0] for _ in exchanged]
    arriving = [None] * len(exchanged)
    far_orders = cube_orders("dp")
    early, late = (0, 1), (2, 3)

    def exchange_far(stage, sets):
        for i in sets:
            arriving[i] = swap(exchanged[i], "dp", far_orders[i % 2][stage])

    def exchange_near(sets):
        for i in sets:
            arriving[i] = swap(exchanged[i], "dp", 1)

    def arrived(sets, stage, *values):
        out = together(*values, *(arriving[i] for i in sets))
        for i, value in zip(sets, out[len(values) :]):
            arriving[i] = value
        for i in sets:
            if stage is not None:
                bit = far_orders[i % 2][stage]
                exchanged[i] = jnp.concatenate([exchanged[i], arriving[i]])
                masks[i] = masks[i] + [mask ^ bit for mask in masks[i]]
        return out[: len(values)]

    def far_rest(sets):
        for stage in range(1, len(far_orders[0])):
            if stage > 1:
                arrived(sets, stage - 1)
            exchange_far(stage, sets)

    last_far = len(far_orders[0]) - 1

    head_offset = here * query_w.shape[1]
    gain_attn = attn_norm_gain.astype(f32)
    gain_expert = expert_norm_gain.astype(f32)
    norm_gains = jnp.stack(
        [
            lax.dynamic_slice_in_dim(gain.astype(f32), head_offset, query_w.shape[1])
            for gain in (query_norm_gain, key_norm_gain)
        ]
    )
    normed1, unit1, scale1 = rows_norm(local_x, gain_attn)
    normed1_ring = [normed1.astype(bf16)]
    exchange_far(0, early)
    for _ in range(1, around):
        normed1_ring.append(hop(normed1_ring[-1]))
    normed1_ring[-2], attn_all, exchanged[2], exchanged[3] = together(
        normed1_ring[-2], attn_all, exchanged[2], exchanged[3]
    )
    exchange_far(0, late)
    projected = projections(normed1_ring[:-1], attn_all, ring_chunks[:-1], around, None)
    normed1_ring[-1], *projected = arrived(early, 0, normed1_ring[-1], *projected)
    far_rest(early)
    query_raw, key_raw, value_heads, squares = projections(
        normed1_ring[-1:], attn_all, ring_chunks[-1:], around, projected
    )
    squares = all_sum(squares[:, 0], ("tensor",))
    final_ring = [held_until(xor_blocks(own_final.astype(bf16), "dp"), squares)]
    final_ring.append(hop(final_ring[0]))
    norm_scales = lax.rsqrt(squares / model_width + EPS).T
    tables = rotary_full(length, HEAD)
    marks = jnp.stack([segments[0], valid[0]])
    query_rot, key_rot, mixed_heads = attention_forward(
        query_raw, key_raw, value_heads, norm_scales, norm_gains, tables, marks
    )
    mixed_heads, final_ring[-1] = arrived(late, 0, mixed_heads, final_ring[-1])
    far_rest(late)
    attn_local = dot32(rows_of(mixed_heads, (here - 1) % around), output_w, NT)
    for step in range(1, around):
        moved = hop(attn_local.astype(bf16))
        if step + 2 == around:
            (moved,) = arrived(early, last_far, moved)
            exchange_near(early)
        attn_local = moved.astype(f32) + dot32(
            rows_of(mixed_heads, (here - 1 - step) % around), output_w, NT
        )
    resid = local_x + attn_local
    normed2, unit2, scale2 = rows_norm(resid, gain_expert)

    normed2_ring = [normed2.astype(bf16)]
    router_f = router_weight.astype(f32)
    probs_ring, routed_ring = [], []
    kept = None
    total = total_gate = None

    def gate_grad_of(s):
        return jnp.where(routed_ring[s], gate_part[s], 0.0).T.reshape(-1)

    late_far, late_far_near = {}, {}

    def parts_of(sets):
        groups = [[], [], []]
        for j in sets:
            places = {}
            for at, mask in enumerate(masks[j]):
                places[mask], places[mask ^ 1] = (exchanged[j], at), (arriving[j], at)
                if j in late_far:
                    turned = mask ^ far_orders[j % 2][last_far]
                    places[turned], places[turned ^ 1] = (late_far[j], at), (late_far_near[j], at)
            for i in range(3):
                blocks = [
                    (places[m][0], (3 * places[m][1] + i) * quarter) for m in sorted(places)
                ]
                groups[i].append((j * quarter, quarter, blocks))
        return groups

    here_dp = lax.axis_index("dp")
    sides = jnp.stack([here_dp, here_dp, jnp.zeros_like(here_dp)]).astype(jnp.int32)
    dx_ring, gate_part = {}, {}
    arrays = made = None
    calls = [((0,), early), ((1,), early), ((0, 1), late)] + [((s,), None) for s in range(2, around)]
    for number, (call, sets) in enumerate(calls):
        if number + 1 < around:
            normed2_ring.append(hop(normed2_ring[number]))
        if len(final_ring) < around and number != 1:
            final_ring.append(hop(final_ring[-1]))
        for s in call:
            if s < len(probs_ring):
                continue
            probs_ring.append(jax.nn.softmax(dot32(normed2_ring[s], router_weight), axis=-1))
            route = rows_of(route_all, ring_chunks[s])
            routed_ring.append(
                jnp.any(route[:, :, None] == jnp.arange(EXPERTS, dtype=jnp.int32), axis=1)
            )
        weights = jnp.concatenate([jnp.where(routed_ring[s], probs_ring[s], 0.0) for s in call])
        flying = []
        if sets is None:
            s = call[0] - 1
            sent = dx_ring[s] if total is None else (total + dx_ring[s]).astype(bf16)
            sent_gate = gate_grad_of(s) if total is None else total_gate + gate_grad_of(s)
            flying = [hop(sent), hop(sent_gate)]
        outs = moe_first(
            [normed2_ring[s] for s in call],
            [final_ring[s] for s in call],
            weights,
            arrays if sets != late and arrays is not None and number > 0 else parts_of(sets),
            (0, experts) if sets is None else (half * (sets == late), half * (1 + (sets == late))),
            kept,
            made if sets == late else None,
            [(dx_ring[s], gate_part[s]) for s in call] if sets == late else None,
            call[0],
            length,
            sides,
        )
        waiting = [normed2_ring[-1], final_ring[-1], *flying]
        held = together(*outs, *waiting)
        outs, waiting = held[: len(outs)], held[len(outs) :]
        normed2_ring[-1], final_ring[-1] = waiting[:2]
        if number == 0:
            (normed2_ring[-1],) = arrived(late, None, normed2_ring[-1])
            late_far = {i: arriving[i] for i in late}
            late_far_near = {i: swap(late_far[i], "dp", 1) for i in late}
            exchange_near(late)
        if flying:
            total, total_gate = waiting[2].astype(f32), waiting[3]
        count = len(call)
        for i, s in enumerate(call):
            dx_ring[s], gate_part[s] = outs[i], outs[count + i]
        kept = outs[2 * count : 2 * count + 3]
        if len(outs) > 2 * count + 3:
            arrays = made = outs[2 * count + 3 :]
    weighted_hidden, grad_gpre, grad_upre = kept
    down_all = arrays[2]
    sent = (total + dx_ring[around - 1]).astype(bf16)
    sent_gate = total_gate + gate_grad_of(around - 1)
    moved, moved_gate = hop(sent), hop(sent_gate)
    gate_keep, gate_send = moe_grad_split(
        normed2_ring, held_until(grad_gpre, sent), "dp", own_side, 0
    )
    moved, moved_gate, gate_keep, gate_send = together(moved, moved_gate, gate_keep, gate_send)
    gate_moved = swap(gate_send, "dp", 1)
    normed2_grad = moved.astype(f32) + dx_ring[0].astype(f32)
    prob_grad = (moved_gate + gate_grad_of(0)).reshape(EXPERTS, rows_here).T
    probs_here = probs_ring[0]
    grad_logits = probs_here * (prob_grad - jnp.sum(probs_here * prob_grad, axis=1, keepdims=True))
    normed2_grad = normed2_grad + jnp.dot(
        grad_logits, router_f.T, precision=PRECISE, preferred_element_type=f32
    )
    resid_norm_grad, grad_expert_part = norm_back(normed2_grad, gain_expert, unit2, scale2)
    tn = (((0,), (0,)), ((), ()))
    grad_router_part = lax.dot_general(
        normed2_ring[0].astype(f32), grad_logits, tn, precision=PRECISE, preferred_element_type=f32
    )
    first_sums = jnp.concatenate([grad_router_part.T, grad_expert_part[None]]).reshape(-1)
    sum_steps = [(axis, bit) for axis in ("dp", "tensor") for bit in bits_of(lax.axis_size(axis))]

    def sum_hop():
        axis, bit = sum_steps.pop(0)
        return swap(first_sums, axis, bit)

    grad_resid = own_final + resid_norm_grad

    def reduce_rows(value):
        return lax.psum_scatter(
            value.reshape(value.shape[0], -1, value.shape[-1]),
            "dp",
            scatter_dimension=1,
            tiled=True,
            axis_index_groups=same_core("dp"),
        )

    resid_ring = [grad_resid.astype(bf16)]
    moved = hop(resid_ring[0])
    up_keep, up_send, gate_sum = moe_grad_split(
        normed2_ring, held_until(grad_upre, resid_ring[0]), "dp", 0, here_dp, (gate_keep, gate_moved)
    )
    moved, up_keep, up_send, gate_sum, hopped = together(
        moved, up_keep, up_send, gate_sum, sum_hop()
    )
    first_sums = first_sums + hopped
    resid_ring.append(moved)
    reduced_gate = reduce_rows(gate_sum)
    up_moved = swap(up_send, "dp", 1)
    moved = hop(resid_ring[1])
    moe_part = moe_out(held_until(weighted_hidden, up_keep), down_all)
    moved, moe_part, up_moved, hopped = together(moved, moe_part, up_moved, sum_hop())
    first_sums = first_sums + hopped
    resid_ring.append(moved)
    for step in range(3, around):
        resid_ring.append(hop(resid_ring[-1]))
    down_keep, down_send, *up_split = moe_grad_split(
        final_ring, held_until(weighted_hidden, moe_part), "dp", 0, 0, (up_keep, up_moved), True
    )
    resid_ring[-1], down_keep, down_send, hopped, *up_split = together(
        resid_ring[-1], down_keep, down_send, sum_hop(), *up_split
    )
    first_sums = first_sums + hopped

    def cube_begin(split):
        flying = [swap(sent, "dp", order[0]) for sent, order in zip(split[2:], cube_orders("dp"))]
        return CubeScatter(split[:2], "dp"), flying

    up_cube, up_flying = cube_begin(up_split)
    down_moved = swap(down_send, "dp", 1)
    resid_full = in_order(resid_ring, "tensor")
    grad_mixed = dot32(resid_full, output_w).astype(bf16)
    moe_local = moe_part[rows_here : 2 * rows_here].astype(f32)
    moe_moved = hop(held_until(moe_local.astype(bf16), resid_full))
    query_gained, key_gained, value_low, inner_part, gain_grads, *down_split = attention_backward(
        query_rot,
        key_rot,
        value_heads,
        grad_mixed,
        query_raw,
        key_raw,
        norm_scales,
        norm_gains,
        tables,
        marks,
        (down_keep, down_moved),
        "dp",
    )
    query_gained, key_gained, inner_part, reduced_gate, moe_moved, hopped, *down_split = together(
        query_gained, key_gained, inner_part, reduced_gate, moe_moved, sum_hop(), *down_split
    )
    first_sums = first_sums + hopped
    down_cube, down_flying = cube_begin(down_split)
    moe_local = moe_moved.astype(f32) + moe_part[2 * rows_here : 3 * rows_here].astype(f32)
    inner_sums = all_sum(inner_part[:, 0], ("tensor",))
    inner_sums, moe_low = together(inner_sums, moe_local.astype(bf16))
    moe_moved = hop(moe_low)
    inner_sums = inner_sums.T / model_width
    inner_sums, moe_moved, *up_flying = together(inner_sums, moe_moved, *up_flying)
    up_cube.finish(up_flying)
    back_order = [(here - 1 - step) % around for step in range(around)]
    query_raw_low, key_raw_low, normed1_parts = projection_back(
        (query_raw, key_raw),
        (query_gained, key_gained),
        value_low,
        norm_scales,
        inner_sums,
        attn_all,
        back_order,
    )
    first = normed1_parts[0]
    moved = hop(first)
    attn_keep, attn_send = projection_grads(
        normed1_ring,
        ring_chunks,
        resid_ring,
        [query_raw_low, key_raw_low, value_low, held_until(mixed_heads, first)],
        "dp",
    )
    moved, attn_keep, attn_send, *down_flying = together(moved, attn_keep, attn_send, *down_flying)
    attn_moved = swap(attn_send, "dp", 1)
    down_cube.finish(down_flying)
    up_cube.pieces = [
        jnp.concatenate(pair) for pair in zip(up_cube.pieces, down_cube.pieces)
    ]
    while len(up_cube.orders[0]) > 1:
        up_cube.finish(up_cube.start())
    up_flying = up_cube.start()
    for step in range(1, around):
        normed1_grad = moved.astype(f32) + normed1_parts[step].astype(f32)
        if step + 1 < around:
            moved = hop(normed1_grad.astype(bf16))
        if step == 1:
            attn_split = pair_split(attn_keep, attn_moved, "dp")
            moved, *attn_split = together(moved, *attn_split)
            attn_cube, attn_flying = cube_begin(attn_split)
    normed1_grad, *up_flying = together(normed1_grad, *up_flying)
    up_cube.finish(up_flying)
    reduced_up = jnp.concatenate([piece[:half] for piece in up_cube.pieces])
    reduced_down = jnp.concatenate([piece[half:] for piece in up_cube.pieces])
    moe_local = moe_moved.astype(f32) + moe_part[3 * rows_here :].astype(f32)
    moe_moved = hop(moe_local.astype(bf16))
    input_norm_grad, grad_attn_part = norm_back(normed1_grad, gain_attn, unit1, scale1)
    grad_input = grad_resid + input_norm_grad
    gains_full = lax.dynamic_update_slice(
        jnp.zeros((2, model_width), f32), gain_grads, (0, head_offset)
    )
    while len(sum_steps) > 1:
        first_sums = first_sums + sum_hop()
    last_sums = jnp.concatenate([gains_full.reshape(-1), grad_attn_part])
    last_sums = last_sums + swap(last_sums, "dp", 1)
    last_sums, *attn_flying = together(last_sums, *attn_flying)
    attn_cube.finish(attn_flying)
    while attn_cube.orders[0]:
        attn_cube.finish(attn_cube.start())
    reduced_attn = attn_cube.result()
    for bit in bits_of(lax.axis_size("dp"))[1:]:
        last_sums = last_sums + swap(last_sums, "dp", bit)
    last_sums, moe_moved = together(last_sums, moe_moved)
    layer_local = resid + xor_blocks(moe_moved.astype(f32) + moe_part[:rows_here].astype(f32), "dp")
    layer_local = layer_local.astype(bf16)
    axis, bit = sum_steps.pop()
    for early_bit in bits_of(lax.axis_size(axis)):
        if early_bit != bit:
            last_sums = last_sums + swap(last_sums, axis, early_bit)
    sums = jnp.concatenate([first_sums, last_sums])
    sums = (sums + swap(sums, axis, bit)).reshape(EXPERTS + 4, model_width)
    return (
        layer_local[None],
        grad_input[None],
        reduced_attn[0],
        reduced_attn[1],
        reduced_attn[2],
        reduced_attn[3],
        reduced_gate.astype(f32),
        reduced_up,
        reduced_down,
        sums[:EXPERTS].T,
        sums[EXPERTS + 3],
        sums[EXPERTS],
        sums[EXPERTS + 1],
        sums[EXPERTS + 2],
    )


def solution(mesh):
    in_specs = (
        P("dp", "tensor", None),
        P("dp", None),
        P("dp", None),
        P("dp", None, None),
        P("dp", "tensor", None),
        P("dp", "tensor"),
        P("dp", "tensor"),
        P("dp", "tensor"),
        P("dp", "tensor"),
        P(),
        P(),
        P(),
        P(),
        P(),
        P(None, "dp", "tensor"),
        P(None, "dp", "tensor"),
        P(None, "dp", "tensor"),
    )
    out_specs = (
        P("dp", "tensor", None),
        P("dp", "tensor", None),
        P("dp", "tensor"),
        P("dp", "tensor"),
        P("dp", "tensor"),
        P("dp", "tensor"),
        P(None, "dp", "tensor"),
        P(None, "dp", "tensor"),
        P(None, "dp", "tensor"),
        P(),
        P(),
        P(),
        P(),
        P(),
    )
    return jax.shard_map(
        on_device, mesh=mesh, in_specs=in_specs, out_specs=out_specs, check_vma=False
    )
```

```python
import jax
import jax.numpy as jnp
from jax import lax
from jax.experimental import pallas as pl
from jax.experimental.pallas import tpu as pltpu
from jax.sharding import PartitionSpec as P

HEAD = 128
EXPERTS = 16


EPS = 1e-05
THETA = 10000.0
MASKED = -1e30
PRECISE = lax.Precision.HIGHEST


def rows_norm(values, gain):
    scale = lax.rsqrt(jnp.mean(values * values, axis=-1, keepdims=True) + EPS)
    normed = values * scale
    return (normed * gain, normed, scale)


def norm_back(grad_out, gain, normed, scale):
    grad_normed = grad_out * gain
    inner_mean = jnp.mean(grad_normed * normed, axis=-1, keepdims=True)
    return (scale * (grad_normed - normed * inner_mean), jnp.sum(grad_out * normed, axis=0))


def rotary_tables(length, width):
    half = width // 2
    freq = THETA ** (-(jnp.arange(half, dtype=jnp.float32) * 2.0) / width)
    angle = jnp.arange(length, dtype=jnp.float32)[:, None] * freq[None, :]
    return (jnp.cos(angle)[:, None, :], jnp.sin(angle)[:, None, :])


NN = (((1,), (0,)), ((), ()))
NT = (((1,), (1,)), ((), ()))


def dot32(left, right, dims=NN):
    return lax.dot_general(left, right, dims, preferred_element_type=jnp.float32)


def in_order(chunks, axis):
    n = lax.axis_size(axis)
    here = lax.axis_index(axis)
    rows = chunks[0].shape[0]
    full = jnp.zeros((n * rows,) + chunks[0].shape[1:], chunks[0].dtype)
    for step, chunk in enumerate(chunks):
        full = lax.dynamic_update_slice_in_dim(full, chunk, ((here - step) % n) * rows, 0)
    return full


def held_until(value, *others):
    return lax.optimization_barrier((value,) + others)[0]


def bits_of(n):
    return [1 << k for k in range(n.bit_length() - 1)]


def swap(value, axis, bit):
    n = lax.axis_size(axis)
    return lax.ppermute(value, axis, [(i, i ^ bit) for i in range(n)])


def cube_orders(axis):
    far = bits_of(lax.axis_size(axis))[1:]
    return [far, far[::-1]]


class CubeScatter:
    def __init__(self, stay, axis):
        self.axis = axis
        self.orders = [order[1:] for order in cube_orders(axis)]
        far = bits_of(lax.axis_size(axis))[1:]
        self.left = [[b for b in far[::-1] if b in order] for order in self.orders]
        self.pieces = [
            s.reshape(s.shape[:1] + (2,) * len(order) + s.shape[2:])
            for s, order in zip(stay, self.orders)
        ]

    def start(self):
        flying, stay = [], []
        for part, piece in enumerate(self.pieces):
            bit = self.orders[part].pop(0)
            place = 1 + self.left[part].index(bit)
            self.left[part].remove(bit)
            sent = lax.index_in_dim(piece, 1, place, keepdims=False).astype(jnp.bfloat16)
            flying.append(swap(sent, self.axis, bit))
            stay.append(lax.index_in_dim(piece, 0, place, keepdims=False))
        self.pieces = stay
        return flying

    def finish(self, arrived):
        self.pieces = [
            stay.astype(jnp.float32) + came.reshape(stay.shape).astype(jnp.float32)
            for stay, came in zip(self.pieces, arrived)
        ]

    def result(self):
        return jnp.concatenate(self.pieces)


def ring_hop(total, axis):
    n = lax.axis_size(axis)
    return lax.ppermute(total, axis, [(i, (i + 1) % n) for i in range(n)])


def all_sum(value, axes):
    flat = value.reshape(-1)
    for axis in axes:
        n = lax.axis_size(axis)
        if n & (n - 1):
            flat = lax.psum(flat, axis)
            continue
        for bit in bits_of(n):
            flat = flat + swap(flat, axis, bit)
    return flat.reshape(value.shape)


def together(*values):
    return lax.optimization_barrier(values)


def xor_blocks(value, axis):
    n = lax.axis_size(axis)
    here = lax.axis_index(axis)
    blocks = jnp.split(value, n, axis=1)
    for bit in bits_of(n):
        turned = (here // bit) % 2 == 1
        blocks = [jnp.where(turned, blocks[j ^ bit], blocks[j]) for j in range(n)]
    return jnp.concatenate(blocks, axis=1)


def same_core(axis):
    n = lax.axis_size(axis)
    return [list(range(0, n, 2)), list(range(1, n, 2))]


DOC_MOST = 512
TILE = 256


def key_span(tile):
    first = max(0, tile - (DOC_MOST + TILE - 2) // TILE)
    return first * TILE, (tile + 1 - first) * TILE


def rotary_full(length, width):
    cosine, sine = rotary_tables(length, width)
    cosine, sine = cosine[:, 0], sine[:, 0]
    return jnp.concatenate([cosine, cosine], axis=1), jnp.concatenate([-sine, sine], axis=1)


def row_sums(values):
    sums = jnp.sum(values, axis=1, keepdims=True)
    return jnp.broadcast_to(sums, (values.shape[0], 128)).T[:8]


def projections(chunks, weights, places, n, filled):
    count = len(chunks)
    rows, width = chunks[0].shape
    columns = weights.shape[2]
    f32, bf16 = jnp.float32, jnp.bfloat16
    before = [] if filled is None else list(filled)

    def kernel(place_ref, *refs):
        w_ref = refs[count]
        q_ref, k_ref, v_ref, s_ref = refs[-4:]
        for s in range(count):

            @pl.when(pl.program_id(0) == s)
            def _(s=s):
                x = refs[s][...]
                for i, out in enumerate((q_ref, k_ref)):
                    raw = dot32(x, w_ref[i])
                    out[...] = raw
                    s_ref[i] = row_sums(raw * raw)
                v_ref[...] = dot32(x, w_ref[2]).astype(bf16)

    out = pl.BlockSpec((rows, columns), lambda s, place: (place[s], 0))
    return pl.pallas_call(
        kernel,
        grid_spec=pltpu.PrefetchScalarGridSpec(
            num_scalar_prefetch=1,
            grid=(count,),
            in_specs=[
                pl.BlockSpec((rows, width), lambda s, place: (0, 0), pipeline_mode=pl.Buffered(1))
            ]
            * count
            + [
                pl.BlockSpec(
                    (3, width, columns), lambda s, place: (0, 0, 0), pipeline_mode=pl.Buffered(1)
                )
            ]
            + [pl.BlockSpec(memory_space=pl.ANY)] * len(before),
            out_specs=[out, out, out, pl.BlockSpec((2, 8, rows), lambda s, place: (0, 0, place[s]))],
        ),
        out_shape=[
            jax.ShapeDtypeStruct((n * rows, columns), f32),
            jax.ShapeDtypeStruct((n * rows, columns), f32),
            jax.ShapeDtypeStruct((n * rows, columns), bf16),
            jax.ShapeDtypeStruct((2, 8, n * rows), f32),
        ],
        input_output_aliases={2 + count + i: i for i in range(len(before))},
        compiler_params=pltpu.CompilerParams(vmem_limit_bytes=58 << 20),
        cost_estimate=pl.CostEstimate(
            flops=6 * count * rows * width * columns,
            transcendentals=0,
            bytes_accessed=6 * width * columns + count * rows * (2 * width + 10 * columns),
        ),
        name="projections",
    )(jnp.stack(places).astype(jnp.int32), *chunks, weights, *before)


def projection_back(raws, gaineds, value_low, scales, inner, weights, order):
    count = len(order)
    length, columns = value_low.shape
    rows = length // count
    width = weights.shape[1]
    f32, bf16 = jnp.float32, jnp.bfloat16

    def kernel(place_ref, qr, kr, qg, kg, v_ref, s_ref, i_ref, w_ref, ql, kl, out_ref):
        total = dot32(v_ref[...], w_ref[2], NT)
        for j, (raw, gained, low) in enumerate(((qr, qg, ql), (kr, kg, kl))):
            scale = s_ref[:, j : j + 1]
            value = scale * (gained[...] - raw[...] * scale * i_ref[:, j : j + 1])
            low[...] = value.astype(bf16)
            total += dot32(value.astype(bf16), w_ref[j], NT)
        out_ref[0] = total.astype(bf16)

    part = pl.BlockSpec((rows, columns), lambda s, place: (place[s], 0))
    pair = pl.BlockSpec((rows, 2), lambda s, place: (place[s], 0))
    low_shape = jax.ShapeDtypeStruct((length, columns), bf16)
    return pl.pallas_call(
        kernel,
        grid_spec=pltpu.PrefetchScalarGridSpec(
            num_scalar_prefetch=1,
            grid=(count,),
            in_specs=[part] * 5
            + [
                pair,
                pair,
                pl.BlockSpec(
                    (3, width, columns), lambda s, place: (0, 0, 0), pipeline_mode=pl.Buffered(1)
                ),
            ],
            out_specs=[part, part, pl.BlockSpec((1, rows, width), lambda s, place: (s, 0, 0))],
        ),
        out_shape=[low_shape, low_shape, jax.ShapeDtypeStruct((count, rows, width), bf16)],
        compiler_params=pltpu.CompilerParams(vmem_limit_bytes=58 << 20),
        cost_estimate=pl.CostEstimate(
            flops=6 * length * width * columns,
            transcendentals=0,
            bytes_accessed=6 * width * columns + length * (22 * columns + 2 * width),
        ),
        name="projection_back",
    )(jnp.stack(order).astype(jnp.int32), *raws, *gaineds, value_low, scales, inner, weights)


def pair_sum(first, second):
    each = 4
    block = pl.BlockSpec((each,) + first.shape[1:], lambda i: (i, 0, 0, 0))

    def kernel(a_ref, b_ref, out_ref):
        add_pair((a_ref, b_ref), (out_ref,))

    return pl.pallas_call(
        kernel,
        grid=(first.shape[0] // each,),
        in_specs=[block, block],
        out_specs=block,
        out_shape=jax.ShapeDtypeStruct(first.shape, first.dtype),
        compiler_params=pltpu.CompilerParams(vmem_limit_bytes=58 << 20),
        cost_estimate=pl.CostEstimate(flops=first.size, transcendentals=0, bytes_accessed=6 * first.size),
        name="pair_sum",
    )(first, second)


def pair_split(first, second, axis):
    block = pl.BlockSpec((1,) + first.shape[1:], lambda i: (i, 0, 0, 0))
    steps = first.shape[0]
    specs, shapes = split_outs(first, steps)

    def kernel(a_ref, b_ref, *outs):
        add_split((a_ref, b_ref), outs, pl.program_id(0) >= steps // 2, cube_orders(axis))

    return pl.pallas_call(
        kernel,
        grid=(steps,),
        in_specs=[block, block],
        out_specs=specs,
        out_shape=shapes,
        compiler_params=pltpu.CompilerParams(vmem_limit_bytes=58 << 20),
        cost_estimate=pl.CostEstimate(flops=first.size, transcendentals=0, bytes_accessed=6 * first.size),
        name="pair_split",
    )(first, second)


def projection_grads(firsts, places, seconds, lows, axis):
    n = lax.axis_size(axis)
    count = len(firsts)
    chunk, width = firsts[0].shape
    rows, columns = lows[0].shape
    arrays = len(lows)
    block = width // n
    half = pl.BlockSpec((1, n // 2, block, columns), lambda i, place: (i, 0, 0, 0))
    shape = jax.ShapeDtypeStruct((arrays, n // 2, block, columns), jnp.bfloat16)

    def kernel(place_ref, *refs):
        low_refs = refs[2 * count : 2 * count + arrays]
        keep_ref, send_ref, turned = refs[-3:]
        i = pl.program_id(0)
        for begin, group in ((0, refs[:count]), (arrays - 1, refs[count : 2 * count])):

            @pl.when(i == begin)
            def _(group=group):
                for s in range(count):
                    at = pl.multiple_of(place_ref[s] * chunk, chunk)
                    turned[:, pl.ds(at, chunk)] = group[s][...].T

        for j in range(arrays):

            @pl.when(i == j)
            def _(j=j):
                for q in range(n // 2):
                    for out, side in ((keep_ref, 0), (send_ref, 1)):
                        at = pl.multiple_of(((2 * q + side) ^ place_ref[count]) * block, block)
                        product = dot32(turned[pl.ds(at, block), :], low_refs[j][...])
                        out[0, q] = product.astype(jnp.bfloat16)

    def whole(shape):
        return pl.BlockSpec(shape, lambda i, place: (0, 0), pipeline_mode=pl.Buffered(1))

    return pl.pallas_call(
        kernel,
        grid_spec=pltpu.PrefetchScalarGridSpec(
            num_scalar_prefetch=1,
            grid=(arrays,),
            in_specs=[whole((chunk, width))] * (2 * count) + [whole((rows, columns))] * arrays,
            out_specs=[half, half],
            scratch_shapes=[pltpu.VMEM((width, rows), jnp.bfloat16)],
        ),
        out_shape=[shape, shape],
        compiler_params=pltpu.CompilerParams(vmem_limit_bytes=58 << 20),
        cost_estimate=pl.CostEstimate(
            flops=2 * arrays * rows * width * columns,
            transcendentals=0,
            bytes_accessed=4 * rows * width + 2 * arrays * columns * (width + rows),
        ),
        name="projection_grads",
    )(jnp.stack([*places, lax.axis_index(axis)]).astype(jnp.int32), *firsts, *seconds, *lows)


def attention_forward(query_raw, key_raw, values, scales, gains, tables, marks):
    length, columns = query_raw.shape
    heads = columns // HEAD
    tiles = length // TILE
    f32, bf16 = jnp.float32, jnp.bfloat16
    widest = max(key_span(t)[1] for t in range(tiles))

    def kernel(q_ref, k_ref, v_ref, s_ref, g_ref, cos_ref, sin_ref, col_ref, row_ref, qo, ko, mo, bias):
        @pl.when(pl.program_id(0) == 0)
        def _():
            for t in range(tiles):
                start, width = key_span(t)
                rows = pl.ds(t * TILE, TILE)
                keys = pl.ds(start, width)
                same = col_ref[rows, 0:1] == row_ref[0:1, keys]
                query_at = t * TILE + lax.broadcasted_iota(jnp.int32, (TILE, width), 0)
                key_at = start + lax.broadcasted_iota(jnp.int32, (TILE, width), 1)
                live = (row_ref[1:2, keys] == 1) | (key_at == query_at)
                ok = same & (key_at <= query_at) & live
                bias[rows, 0:width] = jnp.where(ok, 0.0, MASKED)

        cosine, sine = cos_ref[...], sin_ref[...]
        for place, (raw, out) in enumerate(((q_ref, qo), (k_ref, ko))):
            unit = raw[...] * s_ref[:, place : place + 1] * g_ref[place : place + 1, :]
            out[...] = (unit * cosine + pltpu.roll(unit, HEAD // 2, 1) * sine).astype(bf16)
        for t in range(tiles):
            start, width = key_span(t)
            rows = pl.ds(t * TILE, TILE)
            keys = pl.ds(start, width)
            scores = dot32(qo[rows, :], ko[keys, :], NT) * HEAD ** (-0.5) + bias[rows, 0:width]
            raised = jnp.exp(scores - jnp.max(scores, axis=1, keepdims=True))
            probs = (raised * (1.0 / jnp.sum(raised, axis=1, keepdims=True))).astype(bf16)
            mo[rows, :] = dot32(probs, v_ref[keys, :]).astype(bf16)

    head = pl.BlockSpec((length, HEAD), lambda h: (0, h))

    def whole(shape):
        return pl.BlockSpec(shape, lambda h: (0, 0))

    low = jax.ShapeDtypeStruct((length, columns), bf16)
    return pl.pallas_call(
        kernel,
        grid=(heads,),
        in_specs=[
            head,
            head,
            head,
            whole((length, 2)),
            pl.BlockSpec((2, HEAD), lambda h: (0, h)),
            whole((length, HEAD)),
            whole((length, HEAD)),
            whole((length, 2)),
            whole((2, length)),
        ],
        out_specs=[head, head, head],
        out_shape=[low, low, low],
        scratch_shapes=[pltpu.VMEM((length, widest), f32)],
        compiler_params=pltpu.CompilerParams(vmem_limit_bytes=58 << 20),
        cost_estimate=pl.CostEstimate(
            flops=4 * length * widest * columns,
            transcendentals=heads * length * widest,
            bytes_accessed=16 * length * columns,
        ),
        name="attention_forward",
    )(query_raw, key_raw, values, scales, gains, *tables, marks.T, marks)


def attention_backward(
    query_rot, key_rot, values, grad_mixed, query_raw, key_raw, scales, gains, tables, marks, addends, axis
):
    length, columns = query_raw.shape
    heads = columns // HEAD
    tiles = length // TILE
    f32, bf16 = jnp.float32, jnp.bfloat16
    widest = max(key_span(t)[1] for t in range(tiles))
    tn = (((0,), (0,)), ((), ()))
    part = pl.BlockSpec(
        (addends[0].shape[0] // heads,) + addends[0].shape[1:], lambda h: (h, 0, 0, 0)
    )
    sum_specs, sum_shapes = split_outs(addends[0], heads)

    def kernel(
        q_ref, k_ref, v_ref, m_ref, qr_ref, kr_ref, s_ref, g_ref, cos_ref, sin_ref, col_ref, row_ref, a_ref, b_ref,
        dq_out, dk_out, dv_out, inner_out, gain_out, stay_0, stay_1, send_0, send_1, bias, dq, dk, dv,
    ):
        h = pl.program_id(0)
        add_split((a_ref, b_ref), (stay_0, stay_1, send_0, send_1), h >= heads // 2, cube_orders(axis))

        @pl.when(h == 0)
        def _():
            inner_out[...] = jnp.zeros_like(inner_out)
            for t in range(tiles):
                start, width = key_span(t)
                rows = pl.ds(t * TILE, TILE)
                keys = pl.ds(start, width)
                same = col_ref[keys, 0:1] == row_ref[0:1, rows]
                key_at = start + lax.broadcasted_iota(jnp.int32, (width, TILE), 0)
                query_at = t * TILE + lax.broadcasted_iota(jnp.int32, (width, TILE), 1)
                live = (col_ref[keys, 1:2] == 1) | (key_at == query_at)
                ok = same & (key_at <= query_at) & live
                bias[0:width, rows] = jnp.where(ok, 0.0, MASKED)

        dk[...] = jnp.zeros_like(dk)
        dv[...] = jnp.zeros_like(dv)
        for t in range(tiles):
            start, width = key_span(t)
            rows = pl.ds(t * TILE, TILE)
            keys = pl.ds(start, width)
            scores = dot32(k_ref[keys, :], q_ref[rows, :], NT) * HEAD ** (-0.5) + bias[0:width, rows]
            raised = jnp.exp(scores - jnp.max(scores, axis=0, keepdims=True))
            probs = raised * (1.0 / jnp.sum(raised, axis=0, keepdims=True))
            dv[keys, :] += dot32(probs.astype(bf16), m_ref[rows, :])
            grad_probs = dot32(v_ref[keys, :], m_ref[rows, :], NT)
            row_dot = jnp.sum(probs * grad_probs, axis=0, keepdims=True)
            grad_scores = (probs * (grad_probs - row_dot)).astype(bf16)
            dk[keys, :] += dot32(grad_scores, q_ref[rows, :])
            dq[rows, :] = dot32(grad_scores, k_ref[keys, :], tn)
        dv_out[...] = dv[...].astype(bf16)
        cosine, sine = cos_ref[...], sin_ref[...]
        for place, (grad, raw, out) in enumerate(((dq, qr_ref, dq_out), (dk, kr_ref, dk_out))):
            turned = grad[...] * HEAD ** (-0.5)
            turned = turned * cosine + pltpu.roll(turned * sine, HEAD // 2, 1)
            unit = raw[...] * s_ref[:, place : place + 1]
            gain_out[place : place + 1, :] = jnp.sum(turned * unit, axis=0, keepdims=True)
            gained = turned * g_ref[place : place + 1, :]
            out[...] = gained
            inner_out[place] += row_sums(gained * unit)

    head = pl.BlockSpec((length, HEAD), lambda h: (0, h))

    def whole(shape):
        return pl.BlockSpec(shape, lambda h: (0, 0))

    pair = pl.BlockSpec((2, HEAD), lambda h: (0, h))
    wide = jax.ShapeDtypeStruct((length, columns), f32)
    return pl.pallas_call(
        kernel,
        grid=(heads,),
        in_specs=[
            head,
            head,
            head,
            head,
            head,
            head,
            whole((length, 2)),
            pair,
            whole((length, HEAD)),
            whole((length, HEAD)),
            whole((length, 2)),
            whole((2, length)),
            part,
            part,
        ],
        out_specs=[head, head, head, pl.BlockSpec((2, 8, length), lambda h: (0, 0, 0)), pair]
        + sum_specs,
        out_shape=[
            wide,
            wide,
            jax.ShapeDtypeStruct((length, columns), bf16),
            jax.ShapeDtypeStruct((2, 8, length), f32),
            jax.ShapeDtypeStruct((2, columns), f32),
        ]
        + sum_shapes,
        scratch_shapes=[
            pltpu.VMEM((widest, length), f32),
            pltpu.VMEM((length, HEAD), f32),
            pltpu.VMEM((length, HEAD), f32),
            pltpu.VMEM((length, HEAD), f32),
        ],
        compiler_params=pltpu.CompilerParams(vmem_limit_bytes=58 << 20),
        cost_estimate=pl.CostEstimate(
            flops=10 * length * widest * columns,
            transcendentals=heads * length * widest,
            bytes_accessed=26 * length * columns,
        ),
        name="attention_backward",
    )(
        query_rot, key_rot, values, grad_mixed, query_raw, key_raw, scales, gains, *tables, marks.T, marks, *addends
    )


def moe_first(xs, fs, weight, arrays, span, filled, made, before, first, total, side):
    count = len(xs)
    chunk, width = xs[0].shape
    parted = isinstance(arrays[0], list)
    experts = weight.shape[1]
    pieces = arrays if parted else [[(0, experts, [(a, 0)])] for a in arrays]
    hidden = pieces[0][0][2][0][0].shape[-1]
    step = 2
    low, high = span
    bf16 = jnp.bfloat16
    flat = [(i, *group) for i, groups in enumerate(pieces) for group in groups]
    sizes = [len(entry[-1]) for entry in flat]
    aliased = list(filled or []) + list(made or [])
    before = [pair[i] for i in range(2) for pair in before or []]
    makes = 3 if parted else 0

    def kernel(side_ref, *refs):
        x_refs, f_refs, w_ref = refs[:count], refs[count : 2 * count], refs[2 * count]
        at = 2 * count + 1
        groups = []
        for size in sizes:
            groups.append(refs[at : at + size])
            at += size
        earlier = refs[at : at + len(before)]
        outs = refs[at + len(before) + len(aliased) :]
        dx_refs, gp_refs = outs[:count], outs[count : 2 * count]
        wh_ref, dg_ref, du_ref = outs[2 * count : 2 * count + 3]
        target_refs = outs[2 * count + 3 : 2 * count + 3 + makes]
        acc = outs[-1]
        s = pl.program_id(0)
        for i, target in enumerate(target_refs):
            for refs_in, entry in zip(groups, flat):
                if entry[0] != i:
                    continue
                begin, held, blocks = entry[1:]

                @pl.when((low + s * step >= begin) & (low + s * step < begin + held))
                def _(refs_in=refs_in, blocks=blocks, target=target, i=i):
                    tall = blocks[0][0].shape[1]
                    for m in range(len(blocks)):
                        place = pl.multiple_of((side_ref[i] ^ m) * tall, tall)
                        target[:, pl.ds(place, tall), :] = refs_in[m][...]

        g_ref, u_ref, d_ref = target_refs if parted else [group[0] for group in groups]

        @pl.when(s == 0)
        def _():
            for r in range(count):
                rs = pl.ds(r * chunk, chunk)
                if before:
                    acc[rs, :] = earlier[r][...].astype(jnp.float32)
                    gp_refs[r][...] = earlier[count + r][...]
                else:
                    acc[rs, :] = jnp.zeros((chunk, width), jnp.float32)
                    gp_refs[r][...] = jnp.zeros((chunk, experts), jnp.float32)

        lane = lax.broadcasted_iota(jnp.int32, (chunk, experts), 1)
        for r in range(count):
            rs = pl.ds(r * chunk, chunk)
            x, f = x_refs[r][...], f_refs[r][...]
            grads, rows_w = [], []
            for j in range(step):
                e = low + s * step + j
                w = jnp.sum(jnp.where(lane == e, w_ref[rs, :], 0.0), axis=1, keepdims=True)
                gate_pre = dot32(x, g_ref[j])
                up_pre = dot32(x, u_ref[j])
                projected = dot32(f, d_ref[j])
                sig = 1.0 / (1.0 + jnp.exp(-gate_pre))
                act = gate_pre * sig
                hidden_f = act * up_pre
                wh_ref[j, rs, :] = (w * hidden_f).astype(bf16)
                inner = jnp.sum(hidden_f * projected, axis=1, keepdims=True)
                gp_refs[r][...] = jnp.where(lane == e, inner, gp_refs[r][...])
                grad_hidden = w * projected
                dg = (grad_hidden * up_pre * (sig + act * (1.0 - sig))).astype(bf16)
                du = (grad_hidden * act).astype(bf16)
                dg_ref[j, rs, :] = dg
                du_ref[j, rs, :] = du
                grads += [dg, du]
                rows_w += [g_ref[j], u_ref[j]]
            acc[rs, :] += dot32(jnp.concatenate(grads, axis=1), jnp.concatenate(rows_w, axis=1), NT)

        @pl.when(s == (high - low) // step - 1)
        def _():
            for r in range(count):
                dx_refs[r][...] = acc[pl.ds(r * chunk, chunk), :].astype(bf16)

    def whole(shape):
        return pl.BlockSpec(shape, lambda s, side: (0, 0), pipeline_mode=pl.Buffered(1))

    def out_whole(shape):
        return pl.BlockSpec(shape, lambda s, side: (0, 0))

    def block_of(block, begin, held, base):
        return pl.BlockSpec(
            (step,) + block.shape[1:],
            lambda s, side: (
                base // step + jnp.clip(s + low // step - begin // step, 0, held // step - 1),
                0,
                0,
            ),
        )

    w_spec = pl.BlockSpec((step, width, hidden), lambda s, side: (s + low // step, 0, 0))
    h_spec = pl.BlockSpec(
        (step, count * chunk, hidden), lambda s, side: (s + low // step, first // count, 0)
    )
    kept = jax.ShapeDtypeStruct((experts, total, hidden), bf16)
    blocks_in = [block for entry in flat for block, _ in entry[-1]]
    rows = count * chunk
    ahead = 2 + 2 * count + len(blocks_in) + len(before)
    return pl.pallas_call(
        kernel,
        grid_spec=pltpu.PrefetchScalarGridSpec(
            num_scalar_prefetch=1,
            grid=((high - low) // step,),
            in_specs=[whole((chunk, width))] * (2 * count)
            + [whole((rows, experts))]
            + [block_of(block, *entry[1:-1], base) for entry in flat for block, base in entry[-1]]
            + [whole(value.shape) for value in before]
            + [pl.BlockSpec(memory_space=pl.ANY)] * len(aliased),
            out_specs=[out_whole((chunk, width))] * count
            + [out_whole((chunk, experts))] * count
            + [h_spec] * 3
            + [w_spec] * makes,
            scratch_shapes=[pltpu.VMEM((rows, width), jnp.float32)],
        ),
        out_shape=[jax.ShapeDtypeStruct((chunk, width), bf16)] * count
        + [jax.ShapeDtypeStruct((chunk, experts), jnp.float32)] * count
        + [kept] * 3
        + [jax.ShapeDtypeStruct((experts, width, hidden), bf16)] * makes,
        input_output_aliases={ahead + i: 2 * count + i for i in range(len(aliased))},
        compiler_params=pltpu.CompilerParams(vmem_limit_bytes=58 << 20),
        cost_estimate=pl.CostEstimate(
            flops=10 * rows * width * hidden * (high - low),
            transcendentals=rows * hidden * (high - low),
            bytes_accessed=6 * (high - low) * hidden * (width + rows) + 12 * rows * width,
        ),
        name="moe_first",
    )(side, *xs, *fs, weight, *blocks_in, *before, *aliased)


def add_pair(adds, sums):
    for out in sums:
        total = adds[0][...].astype(jnp.float32) + adds[1][...].astype(jnp.float32)
        out[...] = total.astype(out.dtype)


def add_split(adds, outs, late, orders):
    for p in range(2):
        targets = (outs[p], outs[2 + p])

        @pl.when(late == bool(p))
        def _(p=p, targets=targets):
            at = [0, 0]
            for m in range(adds[0].shape[1]):
                sent = 1 if m & (orders[p][0] // 2) else 0
                total = adds[0][:, m].astype(jnp.float32) + adds[1][:, m].astype(jnp.float32)
                targets[sent][:, at[sent]] = total.astype(jnp.bfloat16)
                at[sent] += 1


def split_outs(addend, steps):
    experts, blocks = addend.shape[:2]
    fewer = (blocks // 2,) + addend.shape[2:]
    each = (experts // steps,) + fewer
    specs = [
        pl.BlockSpec(each, lambda h, *_: (jnp.minimum(h, steps // 2 - 1), 0, 0, 0)),
        pl.BlockSpec(each, lambda h, *_: (jnp.maximum(h - steps // 2, 0), 0, 0, 0)),
    ]
    return specs * 2, [jax.ShapeDtypeStruct((experts // 2,) + fewer, jnp.bfloat16)] * 4


def moe_grad_split(xs, kept, axis, side, flip, addends=(), split=False):
    chunk, width = xs[0].shape
    experts, tokens, hidden = kept.shape
    n = lax.axis_size(axis)
    block = width // n
    count = len(xs)

    def kernel(side_ref, *refs):
        h_ref, *adds = refs[count : count + 1 + len(addends)]
        keep_ref, send_ref, *sums, turned = refs[count + 1 + len(addends) :]
        if split:
            add_split(adds, sums, pl.program_id(0) >= experts // 2, cube_orders(axis))
        else:
            add_pair(adds, sums)

        @pl.when(pl.program_id(0) == 0)
        def _():
            for r in range(count):
                columns = refs[r][...].T
                for j in range(n):
                    place = j ^ side_ref[1]
                    at = ((place ^ side_ref[0]) % 2) * (n // 2) + place // 2
                    at = pl.multiple_of(at * block, block)
                    turned[pl.ds(at, block), r * chunk : (r + 1) * chunk] = columns[
                        j * block : (j + 1) * block
                    ]

        product = dot32(turned[...], h_ref[0]).astype(jnp.bfloat16)
        product = product.reshape(n, block, hidden)
        keep_ref[0] = product[: n // 2]
        send_ref[0] = product[n // 2 :]

    half = pl.BlockSpec((1, n // 2, block, hidden), lambda e, side: (e, 0, 0, 0))
    shape = jax.ShapeDtypeStruct((experts, n // 2, block, hidden), jnp.bfloat16)
    sum_specs, sum_shapes = [half] * (len(addends) // 2), [shape] * (len(addends) // 2)
    if split:
        sum_specs, sum_shapes = split_outs(addends[0], experts)
    return pl.pallas_call(
        kernel,
        grid_spec=pltpu.PrefetchScalarGridSpec(
            num_scalar_prefetch=1,
            grid=(experts,),
            in_specs=[
                pl.BlockSpec((chunk, width), lambda e, side: (0, 0), pipeline_mode=pl.Buffered(1))
            ]
            * count
            + [pl.BlockSpec((1, tokens, hidden), lambda e, side: (e, 0, 0))]
            + [half] * len(addends),
            out_specs=[half, half] + sum_specs,
            scratch_shapes=[pltpu.VMEM((width, tokens), jnp.bfloat16)],
        ),
        out_shape=[shape, shape] + sum_shapes,
        compiler_params=pltpu.CompilerParams(vmem_limit_bytes=58 << 20),
        cost_estimate=pl.CostEstimate(
            flops=2 * tokens * width * hidden * experts,
            transcendentals=0,
            bytes_accessed=2 * experts * hidden * (width + tokens) + 2 * tokens * width,
        ),
        name="moe_grad_split",
    )(jnp.stack([jnp.asarray(side, jnp.int32), jnp.asarray(flip, jnp.int32)]), *xs, kept, *addends)


def moe_out(wh, down_all):
    experts, tokens, hidden = wh.shape
    width = down_all.shape[1]
    step, block = 2, min(256, tokens)

    def kernel(h_ref, d_ref, out_ref, acc):
        e = pl.program_id(0)

        @pl.when(e == 0)
        def _():
            acc[...] = jnp.zeros_like(acc)

        down = jnp.concatenate([d_ref[j] for j in range(step)], axis=1)
        for r in range(tokens // block):
            rs = pl.ds(r * block, block)
            rows = jnp.concatenate([h_ref[j, rs, :] for j in range(step)], axis=1)
            acc[rs, :] += dot32(rows, down, NT)

        @pl.when(e == experts // step - 1)
        def _():
            out_ref[...] = acc[...].astype(jnp.bfloat16)

    return pl.pallas_call(
        kernel,
        grid=(experts // step,),
        in_specs=[
            pl.BlockSpec((step, tokens, hidden), lambda e: (e, 0, 0)),
            pl.BlockSpec((step, width, hidden), lambda e: (e, 0, 0)),
        ],
        out_specs=pl.BlockSpec((tokens, width), lambda e: (0, 0)),
        out_shape=jax.ShapeDtypeStruct((tokens, width), jnp.bfloat16),
        scratch_shapes=[pltpu.VMEM((tokens, width), jnp.float32)],
        compiler_params=pltpu.CompilerParams(vmem_limit_bytes=58 << 20),
        cost_estimate=pl.CostEstimate(
            flops=2 * tokens * width * hidden * experts,
            transcendentals=0,
            bytes_accessed=2 * experts * hidden * (width + tokens) + 2 * tokens * width,
        ),
        name="moe_out",
    )(wh, down_all)


def on_device(
    tokens,
    segments,
    valid,
    routes,
    cotangent,
    query_weight,
    key_weight,
    value_weight,
    output_weight,
    attn_norm_gain,
    expert_norm_gain,
    query_norm_gain,
    key_norm_gain,
    router_weight,
    gate_weight,
    up_weight,
    down_weight,
):
    f32 = jnp.float32
    bf16 = jnp.bfloat16
    local_x = tokens[0].astype(f32)
    rows_here, model_width = local_x.shape
    route_all = routes[0]
    length = segments.shape[1]
    here = lax.axis_index("tensor")
    around = lax.axis_size("tensor")
    ring_chunks = [(here - step) % around for step in range(around)]

    def rows_of(array, chunk):
        return lax.dynamic_slice_in_dim(array, chunk * rows_here, rows_here, 0)

    def hop(value):
        return ring_hop(value, "tensor")

    own_side = lax.axis_index("dp") % 2
    own_final = cotangent[0].astype(f32) * rows_of(valid[0], here).astype(f32)[:, None]

    attn_all = lax.all_gather(
        jnp.stack([query_weight, key_weight, value_weight, output_weight]), "dp", axis=1, tiled=True
    )
    query_w, key_w, value_w, output_w = (attn_all[i] for i in range(4))
    experts = down_weight.shape[0]
    half = experts // 2
    bits = bits_of(lax.axis_size("dp"))
    quarter = experts // 4
    exchanged = [
        jnp.concatenate([w[at : at + quarter] for w in (gate_weight, up_weight, down_weight)])
        for at in range(0, experts, quarter)
    ]
    masks = [[0] for _ in exchanged]
    arriving = [None] * len(exchanged)
    far_orders = cube_orders("dp")
    early, late = (0, 1), (2, 3)

    def exchange_far(stage, sets):
        for i in sets:
            arriving[i] = swap(exchanged[i], "dp", far_orders[i % 2][stage])

    def exchange_near(sets):
        for i in sets:
            arriving[i] = swap(exchanged[i], "dp", 1)

    def arrived(sets, stage, *values):
        out = together(*values, *(arriving[i] for i in sets))
        for i, value in zip(sets, out[len(values) :]):
            arriving[i] = value
        for i in sets:
            if stage is not None:
                bit = far_orders[i % 2][stage]
                exchanged[i] = jnp.concatenate([exchanged[i], arriving[i]])
                masks[i] = masks[i] + [mask ^ bit for mask in masks[i]]
        return out[: len(values)]

    def far_rest(sets):
        for stage in range(1, len(far_orders[0])):
            if stage > 1:
                arrived(sets, stage - 1)
            exchange_far(stage, sets)

    last_far = len(far_orders[0]) - 1

    head_offset = here * query_w.shape[1]
    gain_attn = attn_norm_gain.astype(f32)
    gain_expert = expert_norm_gain.astype(f32)
    norm_gains = jnp.stack(
        [
            lax.dynamic_slice_in_dim(gain.astype(f32), head_offset, query_w.shape[1])
            for gain in (query_norm_gain, key_norm_gain)
        ]
    )
    normed1, unit1, scale1 = rows_norm(local_x, gain_attn)
    normed1_ring = [normed1.astype(bf16)]
    exchange_far(0, early)
    for _ in range(1, around):
        normed1_ring.append(hop(normed1_ring[-1]))
    normed1_ring[-2], attn_all, exchanged[2], exchanged[3] = together(
        normed1_ring[-2], attn_all, exchanged[2], exchanged[3]
    )
    exchange_far(0, late)
    projected = projections(normed1_ring[:-1], attn_all, ring_chunks[:-1], around, None)
    normed1_ring[-1], *projected = arrived(early, 0, normed1_ring[-1], *projected)
    far_rest(early)
    query_raw, key_raw, value_heads, squares = projections(
        normed1_ring[-1:], attn_all, ring_chunks[-1:], around, projected
    )
    squares = all_sum(squares[:, 0], ("tensor",))
    final_ring = [held_until(xor_blocks(own_final.astype(bf16), "dp"), squares)]
    final_ring.append(hop(final_ring[0]))
    norm_scales = lax.rsqrt(squares / model_width + EPS).T
    tables = rotary_full(length, HEAD)
    marks = jnp.stack([segments[0], valid[0]])
    query_rot, key_rot, mixed_heads = attention_forward(
        query_raw, key_raw, value_heads, norm_scales, norm_gains, tables, marks
    )
    mixed_heads, final_ring[-1] = arrived(late, 0, mixed_heads, final_ring[-1])
    far_rest(late)
    attn_local = dot32(rows_of(mixed_heads, (here - 1) % around), output_w, NT)
    for step in range(1, around):
        moved = hop(attn_local.astype(bf16))
        if step + 2 == around:
            (moved,) = arrived(early, last_far, moved)
            exchange_near(early)
        attn_local = moved.astype(f32) + dot32(
            rows_of(mixed_heads, (here - 1 - step) % around), output_w, NT
        )
    resid = local_x + attn_local
    normed2, unit2, scale2 = rows_norm(resid, gain_expert)

    normed2_ring = [normed2.astype(bf16)]
    router_f = router_weight.astype(f32)
    probs_ring, routed_ring = [], []
    kept = None
    total = total_gate = None

    def gate_grad_of(s):
        return jnp.where(routed_ring[s], gate_part[s], 0.0).T.reshape(-1)

    late_far, late_far_near = {}, {}

    def parts_of(sets):
        groups = [[], [], []]
        for j in sets:
            places = {}
            for at, mask in enumerate(masks[j]):
                places[mask], places[mask ^ 1] = (exchanged[j], at), (arriving[j], at)
                if j in late_far:
                    turned = mask ^ far_orders[j % 2][last_far]
                    places[turned], places[turned ^ 1] = (late_far[j], at), (late_far_near[j], at)
            for i in range(3):
                blocks = [
                    (places[m][0], (3 * places[m][1] + i) * quarter) for m in sorted(places)
                ]
                groups[i].append((j * quarter, quarter, blocks))
        return groups

    here_dp = lax.axis_index("dp")
    sides = jnp.stack([here_dp, here_dp, jnp.zeros_like(here_dp)]).astype(jnp.int32)
    dx_ring, gate_part = {}, {}
    arrays = made = None
    calls = [((0,), early), ((1,), early), ((0, 1), late)] + [((s,), None) for s in range(2, around)]
    for number, (call, sets) in enumerate(calls):
        if number + 1 < around:
            normed2_ring.append(hop(normed2_ring[number]))
        if len(final_ring) < around and number != 1:
            final_ring.append(hop(final_ring[-1]))
        for s in call:
            if s < len(probs_ring):
                continue
            probs_ring.append(jax.nn.softmax(dot32(normed2_ring[s], router_weight), axis=-1))
            route = rows_of(route_all, ring_chunks[s])
            routed_ring.append(
                jnp.any(route[:, :, None] == jnp.arange(EXPERTS, dtype=jnp.int32), axis=1)
            )
        weights = jnp.concatenate([jnp.where(routed_ring[s], probs_ring[s], 0.0) for s in call])
        flying = []
        if sets is None:
            s = call[0] - 1
            sent = dx_ring[s] if total is None else (total + dx_ring[s]).astype(bf16)
            sent_gate = gate_grad_of(s) if total is None else total_gate + gate_grad_of(s)
            flying = [hop(sent), hop(sent_gate)]
        outs = moe_first(
            [normed2_ring[s] for s in call],
            [final_ring[s] for s in call],
            weights,
            arrays if sets != late and arrays is not None and number > 0 else parts_of(sets),
            (0, experts) if sets is None else (half * (sets == late), half * (1 + (sets == late))),
            kept,
            made if sets == late else None,
            [(dx_ring[s], gate_part[s]) for s in call] if sets == late else None,
            call[0],
            length,
            sides,
        )
        waiting = [normed2_ring[-1], final_ring[-1], *flying]
        held = together(*outs, *waiting)
        outs, waiting = held[: len(outs)], held[len(outs) :]
        normed2_ring[-1], final_ring[-1] = waiting[:2]
        if number == 0:
            (normed2_ring[-1],) = arrived(late, None, normed2_ring[-1])
            late_far = {i: arriving[i] for i in late}
            late_far_near = {i: swap(late_far[i], "dp", 1) for i in late}
            exchange_near(late)
        if flying:
            total, total_gate = waiting[2].astype(f32), waiting[3]
        count = len(call)
        for i, s in enumerate(call):
            dx_ring[s], gate_part[s] = outs[i], outs[count + i]
        kept = outs[2 * count : 2 * count + 3]
        if len(outs) > 2 * count + 3:
            arrays = made = outs[2 * count + 3 :]
    weighted_hidden, grad_gpre, grad_upre = kept
    down_all = arrays[2]
    sent = (total + dx_ring[around - 1]).astype(bf16)
    sent_gate = total_gate + gate_grad_of(around - 1)
    moved, moved_gate = hop(sent), hop(sent_gate)
    gate_keep, gate_send = moe_grad_split(
        normed2_ring, held_until(grad_gpre, sent), "dp", own_side, 0
    )
    moved, moved_gate, gate_keep, gate_send = together(moved, moved_gate, gate_keep, gate_send)
    gate_moved = swap(gate_send, "dp", 1)
    normed2_grad = moved.astype(f32) + dx_ring[0].astype(f32)
    prob_grad = (moved_gate + gate_grad_of(0)).reshape(EXPERTS, rows_here).T
    probs_here = probs_ring[0]
    grad_logits = probs_here * (prob_grad - jnp.sum(probs_here * prob_grad, axis=1, keepdims=True))
    normed2_grad = normed2_grad + jnp.dot(
        grad_logits, router_f.T, precision=PRECISE, preferred_element_type=f32
    )
    resid_norm_grad, grad_expert_part = norm_back(normed2_grad, gain_expert, unit2, scale2)
    tn = (((0,), (0,)), ((), ()))
    grad_router_part = lax.dot_general(
        normed2_ring[0].astype(f32), grad_logits, tn, precision=PRECISE, preferred_element_type=f32
    )
    first_sums = jnp.concatenate([grad_router_part.T, grad_expert_part[None]]).reshape(-1)
    sum_steps = [(axis, bit) for axis in ("dp", "tensor") for bit in bits_of(lax.axis_size(axis))]

    def sum_hop():
        axis, bit = sum_steps.pop(0)
        return swap(first_sums, axis, bit)

    grad_resid = own_final + resid_norm_grad

    def reduce_rows(value):
        return lax.psum_scatter(
            value.reshape(value.shape[0], -1, value.shape[-1]),
            "dp",
            scatter_dimension=1,
            tiled=True,
            axis_index_groups=same_core("dp"),
        )

    resid_low, gate_moved = together(grad_resid.astype(bf16), gate_moved)
    resid_ring = [resid_low]
    moved = hop(resid_ring[0])
    gate_moved, first_sums = together(gate_moved, first_sums)
    gate_sum = pair_sum(gate_keep, gate_moved)
    gate_sum, grad_upre = together(gate_sum, grad_upre)
    reduced_gate = reduce_rows(gate_sum)
    up_keep, up_send = moe_grad_split(normed2_ring, grad_upre, "dp", 0, here_dp)
    moved, up_keep, up_send, hopped = together(moved, up_keep, up_send, sum_hop())
    first_sums = first_sums + hopped
    resid_ring.append(moved)
    up_moved = swap(up_send, "dp", 1)
    moved = hop(resid_ring[1])
    moe_part = moe_out(held_until(weighted_hidden, up_keep), down_all)
    moved, moe_part, up_moved, hopped = together(moved, moe_part, up_moved, sum_hop())
    first_sums = first_sums + hopped
    resid_ring.append(moved)
    for step in range(3, around):
        resid_ring.append(hop(resid_ring[-1]))
    moe_moved = hop(moe_part[rows_here : 2 * rows_here])
    down_keep, down_send, *up_split = moe_grad_split(
        final_ring, held_until(weighted_hidden, moe_part), "dp", 0, 0, (up_keep, up_moved), True
    )
    resid_ring[-1], down_keep, down_send, reduced_gate, hopped, *up_split = together(
        resid_ring[-1], down_keep, down_send, reduced_gate, sum_hop(), *up_split
    )
    first_sums = first_sums + hopped

    def cube_begin(split):
        flying = [swap(sent, "dp", order[0]) for sent, order in zip(split[2:], cube_orders("dp"))]
        return CubeScatter(split[:2], "dp"), flying

    up_cube, up_flying = cube_begin(up_split)
    down_moved = swap(down_send, "dp", 1)
    resid_full = in_order(resid_ring, "tensor")
    grad_mixed = dot32(resid_full, output_w).astype(bf16)
    grad_mixed, moe_moved = together(grad_mixed, moe_moved)
    moe_local = moe_moved.astype(f32) + moe_part[2 * rows_here : 3 * rows_here].astype(f32)
    moe_moved = hop(moe_local.astype(bf16))
    query_gained, key_gained, value_low, inner_part, gain_grads, *down_split = attention_backward(
        query_rot,
        key_rot,
        value_heads,
        grad_mixed,
        query_raw,
        key_raw,
        norm_scales,
        norm_gains,
        tables,
        marks,
        (down_keep, down_moved),
        "dp",
    )
    query_gained, key_gained, inner_part, reduced_gate, moe_moved, hopped, *down_split = together(
        query_gained, key_gained, inner_part, reduced_gate, moe_moved, sum_hop(), *down_split
    )
    first_sums = first_sums + hopped
    down_cube, down_flying = cube_begin(down_split)
    moe_local = moe_moved.astype(f32) + moe_part[3 * rows_here :].astype(f32)
    inner_sums = all_sum(inner_part[:, 0], ("tensor",))
    inner_sums, moe_low = together(inner_sums, moe_local.astype(bf16))
    moe_moved = hop(moe_low)
    inner_sums = inner_sums.T / model_width
    inner_sums, moe_moved, *up_flying = together(inner_sums, moe_moved, *up_flying)
    up_cube.finish(up_flying)
    back_order = [(here - 1 - step) % around for step in range(around)]
    query_raw_low, key_raw_low, normed1_parts = projection_back(
        (query_raw, key_raw),
        (query_gained, key_gained),
        value_low,
        norm_scales,
        inner_sums,
        attn_all,
        back_order,
    )
    first = normed1_parts[0]
    moved = hop(first)
    attn_keep, attn_send = projection_grads(
        normed1_ring,
        ring_chunks,
        resid_ring,
        [query_raw_low, key_raw_low, value_low, held_until(mixed_heads, first)],
        "dp",
    )
    moved, attn_keep, attn_send, *down_flying = together(moved, attn_keep, attn_send, *down_flying)
    attn_moved = swap(attn_send, "dp", 1)
    down_cube.finish(down_flying)
    up_cube.pieces = [
        jnp.concatenate(pair) for pair in zip(up_cube.pieces, down_cube.pieces)
    ]
    while len(up_cube.orders[0]) > 1:
        up_cube.finish(up_cube.start())
    up_flying = up_cube.start()
    for step in range(1, around):
        normed1_grad = moved.astype(f32) + normed1_parts[step].astype(f32)
        if step + 1 < around:
            moved = hop(normed1_grad.astype(bf16))
        if step == 1:
            attn_split = pair_split(attn_keep, attn_moved, "dp")
            moved, *attn_split = together(moved, *attn_split)
            attn_cube, attn_flying = cube_begin(attn_split)
    normed1_grad, *up_flying = together(normed1_grad, *up_flying)
    up_cube.finish(up_flying)
    reduced_up = jnp.concatenate([piece[:half] for piece in up_cube.pieces])
    reduced_down = jnp.concatenate([piece[half:] for piece in up_cube.pieces])
    input_norm_grad, grad_attn_part = norm_back(normed1_grad, gain_attn, unit1, scale1)
    grad_input = grad_resid + input_norm_grad
    gains_full = lax.dynamic_update_slice(
        jnp.zeros((2, model_width), f32), gain_grads, (0, head_offset)
    )
    while len(sum_steps) > 1:
        first_sums = first_sums + sum_hop()
    last_sums = jnp.concatenate([gains_full.reshape(-1), grad_attn_part])
    last_sums = last_sums + swap(last_sums, "dp", 1)
    last_sums, *attn_flying = together(last_sums, *attn_flying)
    attn_cube.finish(attn_flying)
    while attn_cube.orders[0]:
        attn_cube.finish(attn_cube.start())
    reduced_attn = attn_cube.result()
    for bit in bits_of(lax.axis_size("dp"))[1:]:
        last_sums = last_sums + swap(last_sums, "dp", bit)
    last_sums, moe_moved = together(last_sums, moe_moved)
    layer_local = resid + xor_blocks(moe_moved.astype(f32) + moe_part[:rows_here].astype(f32), "dp")
    layer_local = layer_local.astype(bf16)
    axis, bit = sum_steps.pop()
    for early_bit in bits_of(lax.axis_size(axis)):
        if early_bit != bit:
            last_sums = last_sums + swap(last_sums, axis, early_bit)
    sums = jnp.concatenate([first_sums, last_sums])
    sums = (sums + swap(sums, axis, bit)).reshape(EXPERTS + 4, model_width)
    return (
        layer_local[None],
        grad_input[None],
        reduced_attn[0],
        reduced_attn[1],
        reduced_attn[2],
        reduced_attn[3],
        reduced_gate.astype(f32),
        reduced_up,
        reduced_down,
        sums[:EXPERTS].T,
        sums[EXPERTS + 3],
        sums[EXPERTS],
        sums[EXPERTS + 1],
        sums[EXPERTS + 2],
    )


def solution(mesh):
    in_specs = (
        P("dp", "tensor", None),
        P("dp", None),
        P("dp", None),
        P("dp", None, None),
        P("dp", "tensor", None),
        P("dp", "tensor"),
        P("dp", "tensor"),
        P("dp", "tensor"),
        P("dp", "tensor"),
        P(),
        P(),
        P(),
        P(),
        P(),
        P(None, "dp", "tensor"),
        P(None, "dp", "tensor"),
        P(None, "dp", "tensor"),
    )
    out_specs = (
        P("dp", "tensor", None),
        P("dp", "tensor", None),
        P("dp", "tensor"),
        P("dp", "tensor"),
        P("dp", "tensor"),
        P("dp", "tensor"),
        P(None, "dp", "tensor"),
        P(None, "dp", "tensor"),
        P(None, "dp", "tensor"),
        P(),
        P(),
        P(),
        P(),
        P(),
    )
    return jax.shard_map(
        on_device, mesh=mesh, in_specs=in_specs, out_specs=out_specs, check_vma=False
    )
```
